32 devices in a mesh: dp: 4 (over z), row: 4 (over x, core), col: 2 (over y).
Axes of the slice: x: 2, y: 2, z: 4, core: 2. Of those that a mesh axis runs over, the one named last changes fastest.
Arguments:
- block_input: bfloat16 [2, 16384, 768], P(None, ('dp', 'row', 'col')), may hold values from -6 to 6
- segment_ids: int32 [2, 16384], P(None, ('dp', 'row', 'col')), may hold values from 0 to 127, never falling along the last dimension, each value on 1 to 512 neighbouring positions
- bucket: int32 [1023], replicated, may hold values from 0 to 31
- gain_attn: bfloat16 [768], P(('row', 'col')), may hold values from 0.5 to 1.5
- w_query: bfloat16 [768, 768], P('row', 'col'), may hold values from -0.0546875 to 0.0546875
- w_key: bfloat16 [768, 768], P('row', 'col'), may hold values from -0.21875 to 0.21875
- w_value: bfloat16 [768, 768], P('row', 'col'), may hold values from -0.21875 to 0.21875
- w_out: bfloat16 [768, 768], P('row', 'col'), may hold values from -0.875 to 0.875
- bias_table: float32 [32, 12], replicated, may hold values from -4 to 4
- gain_ffn: bfloat16 [768], P(('row', 'col')), may hold values from 0.5 to 1.5
- w_gate: bfloat16 [768, 2048], P('row', 'col'), may hold values from -0.21875 to 0.21875
- w_up: bfloat16 [768, 2048], P('row', 'col'), may hold values from -0.21875 to 0.21875
- w_down: bfloat16 [2048, 768], P('row', 'col'), may hold values from -0.125 to 0.125
- cotangent: bfloat16 [2, 16384, 768], P(None, ('dp', 'row', 'col')), may hold values from -6 to 6
Outputs:
- block_output: bfloat16 [2, 16384, 768], P(None, ('dp', 'row', 'col'))
- grad_input: bfloat16 [2, 16384, 768], P(None, ('dp', 'row', 'col'))
- grad_gain_attn: float32 [768], P(('row', 'col'))
- grad_query: float32 [768, 768], P('row', 'col')
- grad_key: float32 [768, 768], P('row', 'col')
- grad_value: float32 [768, 768], P('row', 'col')
- grad_out: float32 [768, 768], P('row', 'col')
- grad_table: float32 [32, 12], replicated
- grad_gain_ffn: float32 [768], P(('row', 'col'))
- grad_gate: float32 [768, 2048], P('row', 'col')
- grad_up: float32 [768, 2048], P('row', 'col')
- grad_down: float32 [2048, 768], P('row', 'col')
The draws below stay inside these ranges and needn't reach their ends.
Inputs may be any that keep to these rules, and one draw needn't show every extreme that they name: `segment_ids`: segment ids never fall along the tokens of a micro-batch; a document has 1 to 512 tokens, one has exactly 512. Entry n is the bucket of a key standing n - 511 tokens after its query.
All inputs are finite; a program needn't handle non-finite values.
Results may differ from the reference program's by a relative error of at most 0.017.
Values may be sent and summed in bfloat16 or wider, within the bound.
A program may use at most 320 MiB of HBM per device.

```python
import math
import jax
import jax.numpy as jnp
import numpy as np
from jax import lax

D = 768
H = 12
DH = 64
FF = 2048
NB = 32
LEN = 512
MICRO = 2
TOKENS = 16384
SEGMENTS = 128


def place_ends(drawn, key, least, largest):
    longest = drawn.shape.index(max(drawn.shape))
    spots = []
    for shift in (0, 1):
        where = [jax.random.randint(jax.random.fold_in(key, axis), (), 0, length) for axis, length in enumerate(drawn.shape)]
        where[longest] = (where[longest] + shift) % drawn.shape[longest]
        spots.append(tuple(where))
    return drawn.at[spots[0]].set(least).at[spots[1]].set(largest)


def level_of(key, dims, shards, least, largest):
    def one(position, parts):
        steps = jax.random.uniform(jax.random.fold_in(jax.random.fold_in(key, 6), position), (parts,), jnp.float32, least / len(shards), largest / len(shards))
        return jnp.repeat(jnp.exp(steps), dims[position] // parts).reshape((-1,) + (1,) * (len(dims) - position - 1))

    factor_of = one(*shards[0])
    for cut in shards[1:]:
        factor_of = factor_of * one(*cut)
    return factor_of


def length_profile(number_of, total, bound, lean):
    loads = [(1 << 20) // math.isqrt(grade ** lean) + 1 for grade in range(2, number_of + 1)]
    rest, given = total - bound - (number_of - 1), [1] * (number_of - 1)
    while rest > 0:
        candidates = [i for i in range(number_of - 1) if given[i] < bound]
        mass, remaining = sum([loads[i] for i in candidates]), rest
        for i in candidates:
            more = min(bound - given[i], max(1, remaining * loads[i] // mass), rest)
            given[i] = given[i] + more
            rest = rest - more
    return np.array([bound] + given)


def uneven_parts(key, amount, total, most, lean):
    if amount == 2:
        one = jax.random.randint(key, (), max(1, total - most), min(most, total - 1) + 1)
        return jnp.stack([one, total - one])
    tallies = jnp.asarray(length_profile(amount, total, most, lean), jnp.int32)
    twos = (amount - 1) // 2
    source_of, taker = tallies[1:1 + 2 * twos:2], tallies[2:2 + 2 * twos:2]
    margin = jnp.minimum(source_of - 1, most - taker)
    shifted = jax.random.randint(jax.random.fold_in(key, 1), (twos,), 0, 1 << 20) % (margin + 1)
    tallies = tallies.at[1:1 + 2 * twos:2].set(source_of - shifted).at[2:2 + 2 * twos:2].set(taker + shifted)
    return tallies[jax.random.permutation(jax.random.fold_in(key, 2), amount)]


def gaussian(key, shape, width, reach, cuts=(), kind=jnp.bfloat16):
    entries = jax.random.normal(key, shape, jnp.float32) * width
    if len(cuts) > 0:
        entries = level_of(key, shape, cuts, -0.22, 0.18) * entries
    return jnp.clip(entries, min=-reach, max=reach).astype(kind)


def setup_inputs(seed: int = 0) -> dict:
    streams_of = jax.random.split(jax.random.key(seed), 15)
    return {
        "block_input": gaussian(streams_of[0], (MICRO, TOKENS, D), 1.0, 6.0, ((1, 32),)),
        "segment_ids": jax.vmap(lambda own: jnp.searchsorted(jnp.cumsum(uneven_parts(own, SEGMENTS, TOKENS, LEN, 2)), jnp.arange(TOKENS), side="right"))(jax.random.split(streams_of[1], MICRO)).reshape((MICRO, TOKENS)).astype(jnp.int32),
        "bucket": place_ends(jax.random.randint(streams_of[2], (2 * LEN - 1,), 0, NB), jax.random.fold_in(streams_of[2], 1), 0, NB - 1).astype(jnp.int32),
        "gain_attn": jnp.clip(1.0 + 0.1 * jax.random.normal(streams_of[3], (D,), jnp.float32), 0.5, 1.5).astype(jnp.bfloat16),
        "w_query": gaussian(streams_of[4], (D, D), (16 * D) ** -0.5, 0.0546875, ((0, 4), (1, 2))),
        "w_key": gaussian(streams_of[5], (D, D), D ** -0.5, 0.21875, ((0, 4), (1, 2))),
        "w_value": gaussian(streams_of[6], (D, D), D ** -0.5, 0.21875, ((0, 4), (1, 2))),
        "w_out": gaussian(streams_of[7], (D, D), (D // 16) ** -0.5, 0.875, ((0, 4), (1, 2))),
        "bias_table": gaussian(streams_of[8], (NB, H), 1.0, 4.0, (), jnp.float32),
        "gain_ffn": jnp.clip(1.0 + 0.1 * jax.random.normal(streams_of[9], (D,), jnp.float32), 0.5, 1.5).astype(jnp.bfloat16),
        "w_gate": gaussian(streams_of[10], (D, FF), D ** -0.5, 0.21875, ((0, 4), (1, 2))),
        "w_up": gaussian(streams_of[11], (D, FF), D ** -0.5, 0.21875, ((0, 4), (1, 2))),
        "w_down": gaussian(streams_of[12], (FF, D), FF ** -0.5, 0.125, ((0, 4), (1, 2))),
        "cotangent": gaussian(streams_of[13], (MICRO, TOKENS, D), 1.0, 6.0, ((1, 32),)),
    }


EPSILON = 1e-06
NEGATIVE = -1e+30
PRECISE = lax.Precision.HIGHEST

@jax.custom_vjp
def low(v):
    return lax.optimization_barrier(v.astype(jnp.bfloat16)).astype(jnp.float32)

@jax.custom_vjp
def low_back(v):
    return v

def low_keep(v):
    return (low(v), None)

def low_pass(kept, grad):
    return (grad,)

def back_keep(v):
    return (v, None)

def back_low(kept, grad):
    return (low(grad),)
low.defvjp(low_keep, low_pass)
low_back.defvjp(back_keep, back_low)

def norm_scale(values, gain):
    mean_square = lax.optimization_barrier(jnp.mean(values * values, axis=-1, keepdims=True))
    return values * lax.rsqrt(mean_square + EPSILON) * gain

def matmul_exact(left, right):
    return jnp.dot(left, right, precision=PRECISE, preferred_element_type=jnp.float32)

def make_offsets(bias_table, bucket):
    classes = jnp.arange(bias_table.shape[0], dtype=jnp.int32)
    onehot = (bucket[:, None] == classes[None, :]).astype(bias_table.dtype)
    looked = jnp.dot(onehot, bias_table, precision=PRECISE)
    return jnp.pad(looked.T, ((0, 0), (0, 1)))

def bias_block(offsets, start_row, block_rows):
    head_count, twice_len = offsets.shape
    length = twice_len // 2
    tiled = jnp.tile(offsets, (1, block_rows))[:, :block_rows * (twice_len - 1)]
    skewed = tiled.reshape(head_count, block_rows, twice_len - 1)
    return lax.dynamic_slice_in_dim(skewed, length - 1 - start_row, length, 2)

def attention(queries, keys_in, values_in, segment_ids, offsets):
    length = queries.shape[0]
    block_rows = min(512, length)
    query_heads = queries.reshape(length, H, DH)
    key_heads = keys_in.reshape(length, H, DH)
    value_heads = values_in.reshape(length, H, DH)

    def one_block(start_row):
        query_block = lax.dynamic_slice_in_dim(query_heads, start_row, block_rows, 0)
        segment_block = lax.dynamic_slice_in_dim(segment_ids, start_row, block_rows, 0)
        scores = jnp.einsum('qhd,khd->hqk', query_block, key_heads, precision=PRECISE)
        scores = low_back(scores + bias_block(offsets, start_row, block_rows))
        allowed = segment_block[:, None] == segment_ids[None, :]
        scores = jnp.where(allowed[None], scores, NEGATIVE)
        softmax_low = low(jax.nn.softmax(scores, axis=-1))
        attended = jnp.einsum('hqk,khd->qhd', softmax_low, value_heads, precision=PRECISE)
        return attended.reshape(block_rows, H * DH)
    starts = jnp.arange(length // block_rows, dtype=jnp.int32) * block_rows
    return lax.map(jax.checkpoint(one_block), starts).reshape(length, H * DH)

def block_layer(inputs, segment_ids, bucket, params):
    gain_one, w_query, w_key, w_value, w_out, bias_table, gain_two, w_gate, w_up, w_down = params
    offsets = make_offsets(bias_table, bucket)
    normed = low(norm_scale(inputs, gain_one))
    queries = low(low_back(matmul_exact(normed, w_query)))
    keys_in = low(low_back(matmul_exact(normed, w_key)))
    values_in = low(low_back(matmul_exact(normed, w_value)))
    attended = low(low_back(attention(queries, keys_in, values_in, segment_ids, offsets)))
    middle = inputs + low_back(matmul_exact(attended, w_out))
    normed_two = low(norm_scale(middle, gain_two))
    gate_act = low_back(matmul_exact(normed_two, w_gate))
    up_act = low_back(matmul_exact(normed_two, w_up))
    hidden = low(jax.nn.gelu(gate_act, approximate=True) * up_act)
    return middle + low_back(matmul_exact(hidden, w_down))

def reference(block_input, segment_ids, bucket, gain_attn, w_query, w_key, w_value, w_out, bias_table, gain_ffn, w_gate, w_up, w_down, cotangent):
    params = tuple((item.astype(jnp.float32) for item in (gain_attn, w_query, w_key, w_value, w_out, bias_table, gain_ffn, w_gate, w_up, w_down)))
    seq_count = MICRO * TOKENS // LEN
    inputs_all = block_input.astype(jnp.float32).reshape(seq_count, LEN, D)
    segments_all = segment_ids.reshape(seq_count, LEN)
    cotangents_all = cotangent.astype(jnp.float32).reshape(seq_count, LEN, D)

    def scan_step(running, packed):
        inputs_now, segment_now, cotangent_now = packed

        def forward(inputs_var, params_var):
            return block_layer(inputs_var, segment_now, bucket, params_var)
        result, pull = jax.vjp(forward, inputs_now, params)
        grad_in, grad_params = pull(cotangent_now)
        running = jax.tree.map(lambda older, newer: older + newer, running, grad_params)
        return (running, (result.astype(jnp.bfloat16), grad_in.astype(jnp.bfloat16)))
    zeros = tuple((jnp.zeros_like(item) for item in params))
    running, (results, grads_in) = lax.scan(scan_step, zeros, (inputs_all, segments_all, cotangents_all))
    return (results.reshape(MICRO, TOKENS, D), grads_in.reshape(MICRO, TOKENS, D), running[0], running[1], running[2], running[3], running[4], running[5], running[6], running[7], running[8], running[9])
```

```python
import functools
import types

import jax
import jax.numpy as jnp
from jax import lax
from jax.experimental import pallas as pl
from jax.experimental.pallas import tpu as pltpu
from jax.sharding import PartitionSpec as P

F32 = jnp.float32
BF = jnp.bfloat16
EPSILON = 1e-06
NEGATIVE = -1e30
PRECISE = lax.Precision.HIGHEST


def nn(left, right):
    return lax.dot_general(left, right, (((1,), (0,)), ((), ())), preferred_element_type=F32)


def nt(left, right):
    return lax.dot_general(left, right, (((1,), (1,)), ((), ())), preferred_element_type=F32)


def rows_of(index, size):
    return pl.ds(pl.multiple_of(index * size, size), size)


def loop(count, body):
    lax.fori_loop(0, count, lambda index, carry: (body(index), carry)[1], 0)


def norm_in(s, rb):
    def body(i):
        r = rows_of(i, rb)
        x = s.x[r, :].astype(F32)
        scale = lax.rsqrt(jnp.mean(x * x, axis=-1, keepdims=True) + EPSILON)
        n = (x * scale * s.gain[0:1, :]).astype(BF)
        s.a[r, :] = n
        s.n1t[:, r] = n.T

    loop(s.tokens // rb, body)


def masks(s):
    for m in range(s.micro):
        row = s.seg[m : m + 1, :].astype(F32)
        column = jnp.broadcast_to(row, (128, s.length)).T
        for i in range(s.length // 128):
            same = column == row[:, 128 * i : 128 * (i + 1)]
            s.mask[m, :, 128 * i : 128 * (i + 1)] = jnp.where(same, 0.0, NEGATIVE)


def offset_rows(s):
    classes = lax.broadcasted_iota(jnp.int32, (s.buckets, 2 * s.length), 0)
    onehot = (s.bucket[0:1, :] == classes).astype(F32)
    s.offs[...] = lax.dot_general(
        s.table_t[...], onehot, (((1,), (0,)), ((), ())), precision=PRECISE, preferred_element_type=F32
    )


def project(s, which, rb):
    weight, out, out_t = ((s.wq, s.q, None), (s.wk, s.k, s.kt), (s.wv, s.v, s.vt))[which]

    def body(i):
        r = rows_of(i, rb)
        p = nn(s.a[r, :], weight[...]).astype(BF)
        out[r, :] = p
        if out_t is not None:
            out_t[:, r] = p.T

    loop(s.tokens // rb, body)


def half_masks(dtype):
    lane = lax.broadcasted_iota(jnp.int32, (1, 128), 1)
    return [(lane < 64).astype(dtype), (lane >= 64).astype(dtype)]


def attend_pair(s, pair):
    length, wide = s.length, s.wide
    blocks = length // 128
    cols = rows_of(pair, 128)
    keep = half_masks(BF)
    for sub in range(2):
        head = 2 * pair + sub
        row = jnp.broadcast_to(s.offs[pl.ds(head, 1), :], (128, 2 * length))
        s.toep[...] = pltpu.roll(row, 2 * length - 127, 1, stride=1, stride_axis=0)
        hr = rows_of(head, 64)
        for m in range(s.micro):
            mr = slice(m * length, (m + 1) * length)
            key = s.k[mr, cols] * keep[sub]
            vt = s.vt[hr, mr]
            for b in range(length // wide):
                ir = slice(m * length + b * wide, m * length + (b + 1) * wide)
                il = slice(b * wide, (b + 1) * wide)
                scores = nt(key, s.q[ir, cols])
                bias = jnp.concatenate(
                    [s.toep[:, 128 * (blocks - 1 - j) + b * wide : 128 * (blocks - 1 - j) + (b + 1) * wide] for j in range(blocks)],
                    axis=0,
                )
                scores = scores + bias + s.mask[m, :, il]
                top = jnp.max(scores, axis=0, keepdims=True)
                e = jnp.exp(scores - top)
                low = (e * (1.0 / jnp.sum(e, axis=0, keepdims=True))).astype(BF)
                s.p[head * s.micro + m, :, il] = low
                s.ot[hr, ir] = nn(vt, low).astype(BF)


def turn(s, source, target, cb):
    def body(i):
        r = rows_of(i, cb)
        target[r, :] = source[:, r].T

    loop(s.tokens // cb, body)


def turn_back(s, source, target, cb):
    def body(i):
        r = rows_of(i, cb)
        target[:, r] = source[r, :].T

    loop(s.tokens // cb, body)


def out_project(s, rb):
    def body(i):
        r = rows_of(i, rb)
        att = s.ot[:, r].T
        mid = s.x[r, :].astype(F32) + nn(att, s.wo[...])
        s.mid[r, :] = mid
        s.y[r, :] = mid
        scale = lax.rsqrt(jnp.mean(mid * mid, axis=-1, keepdims=True) + EPSILON)
        n = (mid * scale * s.gain[1:2, :]).astype(BF)
        s.a[r, :] = n
        s.n2t[:, r] = n.T
        s.dn[r, :] = jnp.zeros_like(mid)
        s.ct[:, r] = s.c[r, :].T

    loop(s.tokens // rb, body)


C0 = 0.7978845608028654
C1 = 0.044715


def ffn_tile(s, tile, ft, rb, gb):
    cols = rows_of(tile, ft)

    def forward(i):
        r = rows_of(i, rb)
        n = s.a[r, :]
        cot = s.c[r, :]
        gate = nn(n, s.wg[:, cols])
        up = nn(n, s.wu[:, cols])
        dh = nt(cot, s.wd[cols, :])
        square = gate * gate
        t = jnp.tanh(gate * (C0 + (C0 * C1) * square))
        half = 0.5 + 0.5 * t
        act = gate * half
        slope = half + (0.5 * gate) * (1.0 - t * t) * (C0 + (3.0 * C0 * C1) * square)
        hid = (act * up).astype(BF)
        dg = (dh * up * slope).astype(BF)
        du = (dh * act).astype(BF)
        s.hid[r, :] = hid
        s.dg[r, :] = dg
        s.du[r, :] = du
        s.y[r, :] += nn(hid, s.wd[cols, :])
        s.dn[r, :] += nt(dg, s.wg[:, cols]) + nt(du, s.wu[:, cols])

    loop(s.tokens // rb, forward)

    def grads(i):
        r = rows_of(i, gb)
        s.wd[cols, r] = nn(s.ct[r, :], s.hid[...]).astype(BF).T
        s.wg[r, cols] = nn(s.n2t[r, :], s.dg[...]).astype(BF)
        s.wu[r, cols] = nn(s.n2t[r, :], s.du[...]).astype(BF)

    loop(s.width // gb, grads)


def ffn_close(s, rb):
    s.gsum[...] = jnp.zeros_like(s.gsum)

    def body(i):
        r = rows_of(i, rb)
        mid = s.mid[r, :]
        dn = s.dn[r, :]
        scale = lax.rsqrt(jnp.mean(mid * mid, axis=-1, keepdims=True) + EPSILON)
        gdn = dn * s.gain[1:2, :]
        dot = jnp.mean(gdn * mid, axis=-1, keepdims=True)
        dmid = s.c[r, :].astype(F32) + scale * gdn - mid * (scale * scale * scale * dot)
        s.gsum[1:2, :] += jnp.sum(dn * mid * scale, axis=0, keepdims=True)
        s.dn[r, :] = dmid
        s.a[r, :] = dmid.astype(BF)
        s.c[r, :] = s.y[r, :].astype(BF)

    loop(s.tokens // rb, body)


def out_backward(s, rb, gb):
    def body(i):
        r = rows_of(i, rb)
        d = nt(s.a[r, :], s.wo[...]).astype(BF)
        s.do[r, :] = d
        s.dot[:, r] = d.T

    loop(s.tokens // rb, body)

    def grads(i):
        r = rows_of(i, gb)
        s.wo[r, :] = nn(s.ot[r, :], s.a[...]).astype(BF)

    loop(s.width // gb, grads)


def attend_back(s, pair):
    length, wide = s.length, s.wide
    blocks = length // 128
    cols = rows_of(pair, 128)
    keep = half_masks(BF)
    lane = lax.broadcasted_iota(jnp.int32, (1, 128), 1) < 64
    parts = {}
    for sub in range(2):
        head = 2 * pair + sub
        hr = rows_of(head, 64)
        s.toep[...] = jnp.zeros_like(s.toep)
        for m in range(s.micro):
            mr = slice(m * length, (m + 1) * length)
            value = s.v[mr, cols] * keep[sub]
            kt = s.kt[hr, mr]
            for b in range(length // wide):
                ir = slice(m * length + b * wide, m * length + (b + 1) * wide)
                il = slice(b * wide, (b + 1) * wide)
                dp = nt(value, s.do[ir, cols])
                inner = jnp.sum(s.dot[hr, ir].astype(F32) * s.ot[hr, ir].astype(F32), axis=0, keepdims=True)
                ds = s.p[head * s.micro + m, :, il].astype(F32) * (dp - inner)
                for j in range(blocks):
                    at = 128 * (blocks - 1 - j) + b * wide
                    s.toep[:, at : at + wide] += ds[128 * j : 128 * (j + 1), :]
                low = ds.astype(BF)
                s.ds[:, il] = low
                s.dqt[hr, ir] = nn(kt, low).astype(BF)
            parts[sub, m, 0] = nn(s.ds[...], s.q[mr, cols])
            parts[sub, m, 1] = nn(s.p[head * s.micro + m, :, :], s.do[mr, cols])
            if sub == 1:
                s.k[mr, cols] = jnp.where(lane, parts[0, m, 0], parts[1, m, 0]).astype(BF)
                s.v[mr, cols] = jnp.where(lane, parts[0, m, 1], parts[1, m, 1]).astype(BF)
        fold = s.toep[...]
        rows = 64
        while rows >= 8:
            fold = fold[:rows, :] + pltpu.roll(fold[rows:, :], 2 * length - rows, 1)
            rows //= 2
        for r in range(8):
            s.goff[r, pl.ds(head, 1), :] = fold[r : r + 1, :]


def table_grad(s):
    total = None
    for r in range(8):
        part = pltpu.roll(s.goff[r, :, :], 127 - r, 1)
        total = part if total is None else total + part
    classes = lax.broadcasted_iota(jnp.int32, (s.buckets, 2 * s.length), 0)
    onehot = (s.bucket[0:1, :] == classes).astype(F32)
    return lax.dot_general(
        total, onehot, (((1,), (1,)), ((), ())), precision=PRECISE, preferred_element_type=F32
    )


def qkv_back_input(s, rb):
    def body(i):
        r = rows_of(i, rb)
        dn = nt(s.q[r, :], s.wq[...]) + nt(s.k[r, :], s.wk[...]) + nt(s.v[r, :], s.wv[...])
        x = s.x[r, :].astype(F32)
        scale = lax.rsqrt(jnp.mean(x * x, axis=-1, keepdims=True) + EPSILON)
        gdn = dn * s.gain[0:1, :]
        dot = jnp.mean(gdn * x, axis=-1, keepdims=True)
        s.gsum[0:1, :] += jnp.sum(dn * x * scale, axis=0, keepdims=True)
        s.x[r, :] = (s.dn[r, :] + scale * gdn - x * (scale * scale * scale * dot)).astype(BF)

    loop(s.tokens // rb, body)


def weight_back(s, which, grad, gb):
    weight = (s.wq, s.wk, s.wv)[which]

    def body(i):
        r = rows_of(i, gb)
        weight[r, :] = nn(s.n1t[r, :], grad[...]).astype(BF)

    loop(s.width // gb, body)


MESH = pl.DeviceIdType.MESH
NAMES = ("wq", "wk", "wv", "wo", "wg", "wu", "wd")


def place(s):
    s.z, s.row, s.col = lax.axis_index("dp"), lax.axis_index("row"), lax.axis_index("col")
    s.core, s.xx = lax.rem(s.row, 2), lax.div(s.row, 2)
    s.row_p = 2 * s.xx + 1 - s.core
    s.row_x = 2 * (1 - s.xx) + s.core
    s.row_px = 2 * (1 - s.xx) + 1 - s.core
    s.col_y = 1 - s.col
    s.to_p = (s.z, s.row_p, s.col)
    s.to_x = (s.z, s.row_x, s.col)
    s.to_y = (s.z, s.row, s.col_y)
    s.me = 2 * s.row + s.col
    s.plane = [(s.z, lax.rem(s.row + (i // 2), 4), lax.rem(s.col + i % 2, 2)) for i in range(1, 8)]
    s.stack = [(lax.rem(s.z + i, 4), s.row, s.col) for i in range(1, 4)]


def greet(s):
    barrier = pltpu.get_barrier_semaphore()
    for peer in s.plane + s.stack:
        pl.semaphore_signal(barrier, inc=1, device_id=peer, device_id_type=MESH)
    pl.semaphore_wait(barrier, 10)


def block(s, w, row, col, half=None):
    full = getattr(s, NAMES[w])
    rb, cb = full.shape[0] // 4, full.shape[1] // 2
    size = rb if half is None else rb // 2
    start = row * rb + (0 if half is None else half * (rb // 2))
    return full.at[pl.ds(pl.multiple_of(start, size), size), pl.ds(pl.multiple_of(col * cb, cb), cb)]


def strip(s, w, row, half=None):
    full = getattr(s, NAMES[w])
    rb = full.shape[0] // 4
    size = rb if half is None else rb // 2
    start = row * rb + (0 if half is None else half * (rb // 2))
    return full.at[pl.ds(pl.multiple_of(start, size), size), :]


def send(s, family, w, kind, src, dst, peer):
    return pltpu.make_async_remote_copy(
        src_ref=src, dst_ref=dst, send_sem=getattr(s, family + "_send").at[w, kind],
        recv_sem=getattr(s, family + "_recv").at[w, kind], device_id=peer, device_id_type=MESH)


def ag_copy(s, w, kind):
    piece = getattr(s, NAMES[w] + "_in")
    b = lambda r, c, h=None: block(s, w, r, c, h)
    own = b(s.row, s.col)
    if kind == 0:
        return send(s, "ag", w, 0, piece, own, s.to_x)
    if kind == 1:
        return send(s, "ag", w, 1, piece, own, s.to_y)
    if kind == 2:
        return send(s, "ag", w, 2, piece, own, s.to_p)
    if kind == 3:
        return send(s, "ag", w, 3, b(s.row_x, s.col), b(s.row_x, s.col), s.to_p)
    if kind == 4:
        return send(s, "ag", w, 4, b(s.row, s.col_y), b(s.row, s.col_y), s.to_p)
    if kind == 5:
        return send(s, "ag", w, 5, b(s.row_x, s.col, 0), b(s.row_x, s.col, 0), s.to_y)
    if kind == 6:
        return send(s, "ag", w, 6, b(s.row, s.col_y, 1), b(s.row, s.col_y, 1), s.to_x)
    return send(s, "ag", w, kind, b(s.row_x, s.col_y, kind - 7), b(s.row_x, s.col_y, kind - 7), s.to_p)


def ag_arrive(s, w, kind):
    b = lambda r, c, h=None: block(s, w, r, c, h)
    where = [
        lambda: b(s.row_x, s.col), lambda: b(s.row, s.col_y), lambda: b(s.row_p, s.col), lambda: b(s.row_px, s.col),
        lambda: b(s.row_p, s.col_y), lambda: b(s.row_x, s.col_y, 0), lambda: b(s.row_x, s.col_y, 1),
        lambda: b(s.row_px, s.col_y, 0), lambda: b(s.row_px, s.col_y, 1)][kind]()
    send(s, "ag", w, kind, where, where, s.to_p).wait_recv()


def ag_open(s, w):
    for kind in range(3):
        ag_copy(s, w, kind).start()
    pltpu.make_async_copy(getattr(s, NAMES[w] + "_in"), block(s, w, s.row, s.col), s.ag_own.at[w]).start()


def ag_relay(s, w):
    ag_arrive(s, w, 0)
    ag_copy(s, w, 5).start()
    ag_copy(s, w, 3).start()
    ag_arrive(s, w, 1)
    ag_copy(s, w, 6).start()
    ag_copy(s, w, 4).start()


def ag_corner(s, w):
    for kind in (5, 6):
        ag_arrive(s, w, kind)
        ag_copy(s, w, kind + 2).start()


def ag_close(s, w):
    for kind in (2, 3, 4, 7, 8):
        ag_arrive(s, w, kind)
    pltpu.make_async_copy(getattr(s, NAMES[w] + "_in"), block(s, w, s.row, s.col), s.ag_own.at[w]).wait()


def ag_sent(s, w):
    for kind in range(9):
        ag_copy(s, w, kind).wait_send()


def gain_copies(s):
    return [
        pltpu.make_async_remote_copy(
            src_ref=s.gain_in, dst_ref=s.gain_slots.at[s.me], send_sem=s.gain_send.at[i], recv_sem=s.gain_recv.at[s.me],
            device_id=peer, device_id_type=MESH)
        for i, peer in enumerate(s.plane)]


def gain_open(s):
    for copy in gain_copies(s):
        copy.start()


def gain_close(s):
    total = s.gain_in[...]
    for i in range(1, 8):
        slot = 2 * lax.rem(s.row + (i // 2), 4) + lax.rem(s.col + i % 2, 2)
        pltpu.make_async_remote_copy(
            src_ref=s.gain_in, dst_ref=s.gain_slots.at[slot], send_sem=s.gain_send.at[i - 1], recv_sem=s.gain_recv.at[slot],
            device_id=s.plane[i - 1], device_id_type=MESH).wait_recv()
        total = total + s.gain_slots[slot]
    s.gain[...] = total
    for copy in gain_copies(s):
        copy.wait_send()


def small_open(s, family, slots, peers, me):
    slots[me] = s.small[...]
    for i, peer in enumerate(peers):
        pltpu.make_async_remote_copy(
            src_ref=s.small, dst_ref=slots.at[me], send_sem=getattr(s, family + "_send").at[i],
            recv_sem=getattr(s, family + "_recv").at[me], device_id=peer, device_id_type=MESH).start()


def small_close(s, family, slots, peers, ids, me):
    for i, (peer, slot) in enumerate(zip(peers, ids)):
        copy = pltpu.make_async_remote_copy(
            src_ref=s.small, dst_ref=slots.at[slot], send_sem=getattr(s, family + "_send").at[i],
            recv_sem=getattr(s, family + "_recv").at[slot], device_id=peer, device_id_type=MESH)
        copy.wait_recv()
        copy.wait_send()
    total = slots[0]
    for i in range(1, len(ids) + 1):
        total = total + slots[i]
    s.small[...] = total


def plane_ids(s):
    return [2 * lax.rem(s.row + (i // 2), 4) + lax.rem(s.col + i % 2, 2) for i in range(1, 8)]


def stack_ids(s):
    return [lax.rem(s.z + i, 4) for i in range(1, 4)]


def rs_buf(s, name, w):
    return getattr(s, f"{name}{w}")


def rs_copy(s, w, kind):
    n = lambda name: rs_buf(s, name, w)
    if kind in (0, 1):
        return send(s, "rs", w, kind, strip(s, w, 2 * kind + 1 - s.core), n("pr").at[kind], s.to_p)
    if kind == 2:
        return send(s, "rs", w, 2, strip(s, w, s.row_x, 0), n("xa"), s.to_x)
    if kind in (3, 4):
        return send(s, "rs", w, kind, block(s, w, 2 * (kind - 3) + s.core, s.col_y, 1), n("yb").at[kind - 3], s.to_y)
    if kind == 5:
        return send(s, "rs", w, 5, block(s, w, s.row, s.col_y, 0), n("ya"), s.to_y)
    if kind == 6:
        return send(s, "rs", w, 6, block(s, w, s.row_x, s.col, 1), n("xb"), s.to_x)
    low = s.z - 1
    if kind == 7:
        return send(s, "rs", w, 7, block(s, w, s.row, s.col), n("zi"), (s.z_in, s.row, s.col))
    if kind == 8:
        return send(s, "rs", w, 8, block(s, w, s.row, s.col, 1 - low), n("zx"), (3 - s.z, s.row, s.col))
    if kind == 9:
        return send(s, "rs", w, 9, block(s, w, s.row, s.col, low), block(s, w, s.row_p, s.col, low), (3 - s.z, s.row, s.col))
    if kind == 10:
        return send(s, "rs", w, 10, block(s, w, s.row, s.col, low), block(s, w, s.row_p, s.col, low), (s.z_out, s.row, s.col))
    return send(s, "rs", w, 11, block(s, w, s.row_p, s.col, 1 - low), block(s, w, s.row_p, s.col, 1 - low), (s.z_out, s.row, s.col))


def rs_arrive(s, w, kind):
    n = lambda name: rs_buf(s, name, w)
    low = s.z - 1
    where = [
        lambda: n("pr").at[0], lambda: n("pr").at[1], lambda: n("xa"), lambda: n("yb").at[0], lambda: n("yb").at[1],
        lambda: n("ya"), lambda: n("xb"), lambda: n("zi"), lambda: n("zx"),
        lambda: block(s, w, s.row_p, s.col, 1 - low),
        lambda: block(s, w, s.row_p, s.col, s.z_in - 1),
        lambda: block(s, w, s.row_p, s.col, 2 - s.z_in)][kind]()
    send(s, "rs", w, kind, where, where, s.to_p).wait_recv()


def add_into(target, source, step):
    rows = target.shape[0]
    step = min(step, rows)

    def body(i):
        r = rows_of(i, step)
        target[r, :] = (target[r, :].astype(F32) + source[r, :].astype(F32)).astype(BF)

    loop(rows // step, body)


def rs_1(s, w):
    rs_copy(s, w, 0).start()
    rs_copy(s, w, 1).start()


def rs_2(s, w):
    for i in range(2):
        rs_arrive(s, w, i)
        add_into(strip(s, w, 2 * i + s.core), rs_buf(s, "pr", w).at[i], 32)
    rs_copy(s, w, 2).start()
    rs_copy(s, w, 3).start()
    rs_copy(s, w, 4).start()


def rs_3(s, w):
    rs_arrive(s, w, 2)
    add_into(strip(s, w, s.row, 0), rs_buf(s, "xa", w), 32)
    rs_copy(s, w, 5).start()
    for i in range(2):
        rs_arrive(s, w, 3 + i)
        add_into(block(s, w, 2 * i + s.core, s.col, 1), rs_buf(s, "yb", w).at[i], 32)
    rs_copy(s, w, 6).start()


def rs_4(s, w):
    rs_arrive(s, w, 5)
    add_into(block(s, w, s.row, s.col, 0), rs_buf(s, "ya", w), 32)
    rs_arrive(s, w, 6)
    add_into(block(s, w, s.row, s.col, 1), rs_buf(s, "xb", w), 32)
    for kind in range(7):
        rs_copy(s, w, kind).wait_send()

    @pl.when(s.outer)
    def _():
        rs_copy(s, w, 7).start()


def rs_5(s, w):
    @pl.when(s.inner)
    def _():
        rs_arrive(s, w, 7)
        add_into(block(s, w, s.row, s.col), rs_buf(s, "zi", w), 32)
        rs_copy(s, w, 8).start()


def rs_6(s, w):
    @pl.when(s.inner)
    def _():
        rs_arrive(s, w, 8)
        mine = block(s, w, s.row, s.col, s.z - 1)
        add_into(mine, rs_buf(s, "zx", w), 32)
        rs_copy(s, w, 9).start()
        rs_copy(s, w, 10).start()
        done = block(s, w, s.row_p, s.col, s.z - 1)
        done[...] = mine[...]


def rs_7(s, w):
    @pl.when(s.inner)
    def _():
        rs_arrive(s, w, 9)
        rs_copy(s, w, 11).start()
        for kind in (8, 9, 10):
            rs_copy(s, w, kind).wait_send()

    @pl.when(s.outer)
    def _():
        rs_arrive(s, w, 10)
        rs_copy(s, w, 7).wait_send()


def rs_8(s, w):
    @pl.when(s.inner)
    def _():
        rs_copy(s, w, 11).wait_send()

    @pl.when(s.outer)
    def _():
        rs_arrive(s, w, 11)


def rs_out(s, w):
    return pltpu.make_async_copy(block(s, w, s.row_p, s.col), getattr(s, NAMES[w] + "_out"), s.out_sems.at[w])


PIECES = ("w_query", "w_key", "w_value", "w_out", "w_gate", "w_up", "w_down")
Q, K, V, O, G, U, D = range(7)


def at_step(index, steps):
    for number, todo in enumerate(steps):
        if todo:

            @pl.when(index == number)
            def _():
                for act, weight in todo:
                    act(weight)


def layer(cfg, *refs):
    s = types.SimpleNamespace(**cfg)
    for name, ref in zip(cfg["names"], refs):
        setattr(s, name, ref)
    s.gsum = s.small.at[0:2]
    s.dqt = s.vt
    comm = s.comm
    load_x = pltpu.make_async_copy(s.x_in, s.x, s.io_sems.at[0])
    load_c = pltpu.make_async_copy(s.c_in, s.c, s.io_sems.at[1])
    load_x.start()
    load_c.start()
    if comm:
        place(s)
        s.inner = jnp.logical_and(s.z >= 1, s.z <= 2)
        s.outer = jnp.logical_not(s.inner)
        s.z_in, s.z_out = 1 + lax.div(s.z, 2), 3 * lax.div(s.z, 2)
        greet(s)
        gain_open(s)
        for w in (Q, K, V):
            ag_open(s, w)
    else:
        weights = [pltpu.make_async_copy(getattr(s, n + "_in"), getattr(s, n), s.out_sems.at[i]) for i, n in enumerate(NAMES)]
        for copy in weights:
            copy.start()
        s.gain[...] = s.gain_in[...]
    s.small[...] = jnp.zeros_like(s.small)
    offset_rows(s)
    opened = lambda w: comm and ag_open(s, w)
    relay = lambda w: comm and ag_relay(s, w)
    corner = lambda w: comm and ag_corner(s, w)
    close = lambda w: comm and ag_close(s, w)

    def forward(act, n2t, mid, y, ct, mask):
        s.act, s.n2t, s.mid, s.y, s.ct, s.mask = act, n2t, mid, y, ct, mask
        s.hid, s.dg, s.du = (act.at[:, i * s.ft : (i + 1) * s.ft] for i in range(3))
        masks(s)
        load_x.wait()
        load_c.wait()
        if comm:
            gain_close(s)
        else:
            for copy in weights:
                copy.wait()
        norm_in(s, 128)
        for w in (Q, K, V):
            relay(w)
        opened(O)
        for w in (Q, K, V):
            corner(w)
        opened(G)
        for w in (Q, K, V):
            close(w)
            project(s, w, 256)
        plan = [[], [(relay, O), (opened, U)], [(corner, O), (relay, G), (opened, D)], [(corner, G)], [(relay, U)], [(corner, U), (relay, D)]]

        def pair_step(p):
            if comm:
                at_step(p, plan)
            attend_pair(s, p)

        loop(s.heads // 2, pair_step)
        close(O)
        out_project(s, 256)
        corner(D)
        for w in (G, U, D):
            close(w)
        if comm:
            for w in range(7):
                ag_sent(s, w)
        loop(s.hidden // s.ft, lambda t: ffn_tile(s, t, s.ft, 256, 256))
        ffn_close(s, 128)

    tw = (s.tokens, s.width)
    wt = (s.width, s.tokens)
    pl.run_scoped(
        forward, pltpu.VMEM((s.tokens, 3 * s.ft), BF), pltpu.VMEM(wt, BF), pltpu.VMEM(tw, F32), pltpu.VMEM(tw, F32), pltpu.VMEM(wt, BF),
        pltpu.VMEM((s.micro, s.length, s.length), F32))

    put_y = pltpu.make_async_copy(s.c, s.y_out, s.io_sems.at[0])
    put_x = pltpu.make_async_copy(s.x, s.gi_out, s.io_sems.at[1])
    put_y.start()

    def backward(dot, *bufs):
        s.do, s.dot = s.c, dot
        for name, ref in zip(s.rs_names, bufs):
            setattr(s, name, ref)
        step = lambda fn: (lambda w: comm and fn(s, w))
        r1, r2, r3, r4, r5, r6, r7, r8 = map(step, (rs_1, rs_2, rs_3, rs_4, rs_5, rs_6, rs_7, rs_8))
        if comm:
            for peer in (s.to_p, s.to_x, s.to_y) + tuple(s.stack):
                pl.semaphore_signal(s.ready, inc=1, device_id=peer, device_id_type=MESH)
            pl.semaphore_wait(s.ready, 6)
        for w in (D, G, U):
            r1(w)
        put_y.wait()
        out_backward(s, 256, 256)
        r1(O)
        plan = [
            [(r2, D)], [(r2, G), (r3, D)], [(r2, U), (r3, G), (r4, D)], [(r2, O), (r3, U), (r4, G), (r5, D)],
            [(r3, O), (r4, U), (r5, G), (r6, D)], [(r4, O), (r5, U), (r6, G), (r7, D)]]

        def pair_step(p):
            if comm:
                at_step(p, plan)
            attend_back(s, p)

        loop(s.heads // 2, pair_step)
        for act, w in ((r5, O), (r6, U), (r7, G), (r8, D)):
            act(w)
        s.small[2 : 2 + s.heads, 0 : s.buckets] = table_grad(s)
        turn(s, s.dqt, s.q, 256)
        qkv_back_input(s, 256)
        put_x.start()
        if comm:
            small_open(s, "near", s.near_slots, s.plane, s.me)
        for act, w in ((r6, O), (r7, U), (r8, G)):
            act(w)
        for w, grad in ((Q, s.q), (K, s.k), (V, s.v)):
            weight_back(s, w, grad, 256)
            r1(w)
        for act, w in ((r7, O), (r8, U)):
            act(w)
        if comm:
            small_close(s, "near", s.near_slots, s.plane, plane_ids(s), s.me)
            small_open(s, "far", s.far_slots, s.stack, s.z)
        for act in (r2, r3, r4, r5, r6, r7, r8):
            for w in (Q, K, V):
                act(w)
            if act is r3:
                r8(O)
        if comm:
            small_close(s, "far", s.far_slots, s.stack, stack_ids(s), s.z)
            outs = [rs_out(s, w) for w in range(7)]
        else:
            outs = [pltpu.make_async_copy(getattr(s, n), getattr(s, n + "_out"), s.out_sems.at[i]) for i, n in enumerate(NAMES)]
        for copy in outs:
            copy.start()
        for copy in outs:
            copy.wait()

    bufs = [pltpu.VMEM(shape, BF) for shape in s.rs_shapes]
    pl.run_scoped(backward, pltpu.VMEM(wt, BF), *bufs)
    put_x.wait()
    s.small_out[...] = s.small[...]


def call_layer(comm, x, c, weights, gain, seg, bucket, table_t, full):
    tokens, width = x.shape
    micro, length = seg.shape
    heads, buckets = table_t.shape
    hidden = full[G][1]
    ft = 512
    vm, sem = pltpu.VMEM, pltpu.SemaphoreType.DMA
    tw, wt = (tokens, width), (width, tokens)
    scratch = dict(
        x=vm(tw, BF), c=vm(tw, BF), **{n: vm(shape, BF) for n, shape in zip(NAMES, full)},
        a=vm(tw, BF), n1t=vm(wt, BF), q=vm(tw, BF), k=vm(tw, BF), v=vm(tw, BF), kt=vm(wt, BF), vt=vm(wt, BF), ot=vm(wt, BF),
        dn=vm(tw, F32), toep=vm((128, 2 * length), F32), ds=vm((length, length), BF), p=vm((heads * micro, length, length), BF),
        offs=vm((heads, 2 * length), F32), goff=vm((8, heads, 2 * length), F32), gain=vm((8, width), F32), small=vm((16, width), F32),
        io_sems=sem((2,)), out_sems=sem((7,)),
    )
    rs_names, rs_shapes = [], []
    if comm:
        scratch.update(
            gain_slots=vm((8, 8, width), F32), near_slots=vm((8, 16, width), F32), far_slots=vm((4, 16, width), F32),
            ag_send=sem((7, 9)), ag_recv=sem((7, 9)), ag_own=sem((7,)), rs_send=sem((7, 12)), rs_recv=sem((7, 12)),
            gain_send=sem((7,)), gain_recv=sem((8,)), near_send=sem((7,)), near_recv=sem((8,)), far_send=sem((3,)), far_recv=sem((4,)),
            ready=pltpu.SemaphoreType.REGULAR,
        )
        for w, (rows, columns) in enumerate(full):
            rb, cb, hb = rows // 4, columns // 2, rows // 8
            for name, shape in (("pr", (2, rb, columns)), ("xa", (hb, columns)), ("yb", (2, hb, cb)), ("ya", (hb, cb)), ("xb", (hb, cb)), ("zi", (rb, cb)), ("zx", (hb, cb))):
                rs_names.append(f"{name}{w}")
                rs_shapes.append(shape)
    ins = ["x_in", "c_in"] + [n + "_in" for n in NAMES] + ["gain_in", "seg", "bucket", "table_t"]
    outs = ["y_out", "gi_out"] + [n + "_out" for n in NAMES] + ["small_out"]
    cfg = dict(
        comm=comm, tokens=tokens, width=width, micro=micro, length=length, hidden=hidden, heads=heads, buckets=buckets, ft=ft, wide=256,
        rs_names=rs_names, rs_shapes=rs_shapes, names=ins + outs + list(scratch))
    far, near = pl.BlockSpec(memory_space=pl.ANY), pl.BlockSpec(memory_space=pltpu.VMEM)
    sh = jax.ShapeDtypeStruct
    params = dict(vmem_limit_bytes=67043328)
    if comm:
        params.update(collective_id=0, has_side_effects=True)
    return pl.pallas_call(
        functools.partial(layer, cfg),
        out_shape=[sh(tw, BF)] * 2 + [sh(w.shape, BF) for w in weights] + [sh((16, width), F32)],
        in_specs=[far] * 9 + [near] * 4, out_specs=[far] * 9 + [near], scratch_shapes=list(scratch.values()),
        compiler_params=pltpu.CompilerParams(**params),
    )(x, c, *weights, gain, seg, bucket, table_t)


def open_block(gathered, row_count, column_count):
    _, rows, columns = gathered.shape
    grid = gathered.reshape(row_count, column_count, rows, columns).transpose(0, 2, 1, 3)
    return grid.reshape(row_count * rows, column_count * columns)


def close_block(full, row_count, column_count):
    rows, columns = full.shape[0] // row_count, full.shape[1] // column_count
    grid = full.reshape(row_count, rows, column_count, columns).transpose(0, 2, 1, 3)
    return grid.reshape(row_count * column_count, rows, columns)


def shards(block_input, segment_ids, bucket, gain_attn, w_query, w_key, w_value, w_out, bias_table, gain_ffn, w_gate, w_up, w_down, cotangent):
    row_count, column_count = lax.axis_size("row"), lax.axis_size("col")
    micro, length, width = block_input.shape
    tokens = micro * length
    pieces = [w_query, w_key, w_value, w_out, w_gate, w_up, w_down]
    full = [(p.shape[0] * row_count, p.shape[1] * column_count) for p in pieces]
    fits = row_count == 4 and column_count == 2 and lax.axis_size("dp") == 4
    mine = (lax.axis_index("row") * column_count + lax.axis_index("col")) * gain_attn.shape[0]
    turned = jnp.pad(bucket[::-1], (0, 1), constant_values=-1)[None]
    gains = jnp.stack([gain_attn, gain_ffn]).astype(F32)
    x, c = block_input.reshape(tokens, width), cotangent.reshape(tokens, width)
    plane = ("row", "col")
    if fits:
        gains = lax.dynamic_update_slice(jnp.zeros((8, width), F32), gains, (0, mine))
        weights = pieces
    else:
        gains = jnp.pad(lax.all_gather(gains, plane, axis=1, tiled=True), ((0, 6), (0, 0)))
        weights = [open_block(lax.all_gather(p[None], plane, axis=0, tiled=True), row_count, column_count) for p in pieces]
    out = call_layer(fits, x, c, weights, gains, segment_ids, turned, bias_table.T, full)
    y, grad_in, grads, small = out[0], out[1], out[2:9], out[9]
    if not fits:
        small = lax.psum(small, ("dp",) + plane)
        grads = [lax.psum_scatter(close_block(g, row_count, column_count), plane, scatter_dimension=0, tiled=True)[0] for g in grads]
        grads = [lax.psum(g, "dp") for g in grads]
    gain_one, gain_two = (lax.dynamic_slice(small, (i, mine), (1, gain_attn.shape[0]))[0] for i in range(2))
    gq, gk, gv, go, gg, gu, gd = (g.astype(F32) for g in grads)
    table = small[2 : 2 + bias_table.shape[1], : bias_table.shape[0]].T
    return (
        y.reshape(block_input.shape), grad_in.reshape(block_input.shape), gain_one, gq, gk, gv, go, table, gain_two, gg, gu, gd)


def solution(mesh):
    whole = P(None, ("dp", "row", "col"), None)
    split, gain = P("row", "col"), P(("row", "col"))
    return jax.shard_map(
        shards, mesh=mesh,
        in_specs=(whole, P(None, ("dp", "row", "col")), P(), gain, split, split, split, split, P(), gain, split, split, split, whole),
        out_specs=(whole, whole, gain, split, split, split, split, P(), gain, split, split, split),
        check_vma=False)
```

```python
import functools
import types

import jax
import jax.numpy as jnp
from jax import lax
from jax.experimental import pallas as pl
from jax.experimental.pallas import tpu as pltpu
from jax.sharding import PartitionSpec as P

F32 = jnp.float32
BF = jnp.bfloat16
EPSILON = 1e-06
NEGATIVE = -1e30
PRECISE = lax.Precision.HIGHEST
MESH = pl.DeviceIdType.MESH
CHUNKS = 2
GELU_0 = 0.7978845608028654
GELU_1 = 0.044715


def contract(left, right, dims, **more):
    return lax.dot_general(left, right, ((dims[:1], dims[1:]), ((), ())), preferred_element_type=F32, **more)


def nn(left, right):
    return contract(left, right, (1, 0))


def nt(left, right):
    return contract(left, right, (1, 1))


def rows_of(index, size):
    return pl.ds(pl.multiple_of(index * size, size), size)


def loop(count, body):
    lax.fori_loop(0, count, lambda index, carry: (body(index), carry)[1], 0)


def bucket_classes(s):
    return (s.turned[...] == lax.broadcasted_iota(jnp.int32, (s.buckets, 2 * s.length), 0)).astype(F32)


def offset_rows(s):
    twice = 2 * s.length
    s.turned[...] = jnp.full((1, twice), -1, jnp.int32)
    s.turned[:, 0 : twice - 1] = s.bucket[...]
    flip = (lax.broadcasted_iota(jnp.int32, (128, 128), 0) + lax.broadcasted_iota(jnp.int32, (128, 128), 1) == 127).astype(BF)
    parts = [nn(s.turned[:, i : i + 128].astype(F32).astype(BF), flip) for i in range(0, twice, 128)]
    turned = jnp.concatenate(parts[::-1], axis=1)
    s.turned[...] = pltpu.roll(turned, twice - 1, 1).astype(jnp.int32)
    s.offs[...] = contract(s.table[...], bucket_classes(s), (1, 0), precision=PRECISE)


def masks(s):
    for m in range(s.micro):
        row = s.seg[m : m + 1, :].astype(F32)
        column = jnp.broadcast_to(row, (128, s.length)).T
        for i in range(0, s.length, 128):
            s.mask[m, :, i : i + 128] = jnp.where(column == row[:, i : i + 128], 0.0, NEGATIVE)


def norm_in(s, rb):
    def body(i):
        r = rows_of(i, rb)
        x = s.x[r, :].astype(F32)
        scale = lax.rsqrt(jnp.mean(x * x, axis=-1, keepdims=True) + EPSILON)
        n = (x * scale * s.gain[0:1, :]).astype(BF)
        s.a[r, :] = n
        s.n1t[:, r] = n.T

    loop(s.tokens // rb, body)


def spot(s, pair):
    half = s.heads // 4
    return 2 * (pair % half) + pair // half


def project(s, which, rb):
    weight, out, out_t = ((s.wq, s.q, None), (s.wk, s.k, s.kt), (s.wv, s.v, s.vt))[which]

    def body(i):
        r = rows_of(i, rb)
        p = nn(s.a[r, :], weight[...]).astype(BF)
        for pair in range(s.heads // 2):
            at = 128 * spot(s, pair)
            out[r, at : at + 128] = p[:, 128 * pair : 128 * (pair + 1)]
        if out_t is not None:
            out_t[:, r] = p.T

    loop(s.tokens // rb, body)


def half_masks(dtype):
    lane = lax.broadcasted_iota(jnp.int32, (1, 128), 1)
    return [(lane < 64).astype(dtype), (lane >= 64).astype(dtype)]


def attend_pair(s, i):
    length = s.length
    blocks = length // 128
    pair = lax.div(i, 2) + (s.heads // 4) * lax.rem(i, 2)
    here = rows_of(i, 128)
    keep = half_masks(BF)
    for sub in range(2):
        head = 2 * pair + sub
        hr = rows_of(head, 64)
        row = jnp.broadcast_to(s.offs[pl.ds(head, 1), :], (128, 2 * length))
        s.toep[...] = pltpu.roll(row, 2 * length - 127, 1, stride=1, stride_axis=0)
        for m in range(s.micro):
            mr = slice(m * length, (m + 1) * length)
            scores = nt(s.k[mr, here] * keep[sub], s.q[mr, here])
            bias = jnp.concatenate([s.toep[:, 128 * j : 128 * j + length] for j in reversed(range(blocks))], axis=0)
            scores = scores + bias + s.mask[m]
            e = jnp.exp(scores - jnp.max(scores, axis=0, keepdims=True))
            low = (e * (1.0 / jnp.sum(e, axis=0, keepdims=True))).astype(BF)
            s.p[rows_of((2 * i + sub) * s.micro + m, length), :] = low
            s.ot[hr, mr] = nn(s.vt[hr, mr], low).astype(BF)


def out_project(s, rb):
    def body(i):
        r = rows_of(i, rb)
        mid = s.x[r, :].astype(F32) + nn(s.ot[:, r].T, s.wo[...])
        s.mid[r, :] = mid
        s.y[r, :] = mid
        scale = lax.rsqrt(jnp.mean(mid * mid, axis=-1, keepdims=True) + EPSILON)
        n = (mid * scale * s.gain[1:2, :]).astype(BF)
        s.k[r, :] = n
        s.n2t[:, r] = n.T
        s.dn[r, :] = jnp.zeros_like(mid)
        s.ct[:, r] = s.c[r, :].T

    loop(s.tokens // rb, body)


def ffn_rows(s, tile, ft, rb):
    cols = rows_of(tile, ft)

    def forward(i):
        r = rows_of(i, rb)
        n = s.k[r, :]
        gate = nn(n, s.wg[:, cols])
        up = nn(n, s.wu[:, cols])
        dh = nt(s.c[r, :], s.wd[cols, :])
        square = gate * gate
        t = jnp.tanh(gate * (GELU_0 + (GELU_0 * GELU_1) * square))
        half = 0.5 + 0.5 * t
        act = gate * half
        slope = half + (0.5 * gate) * (1.0 - t * t) * (GELU_0 + (3.0 * GELU_0 * GELU_1) * square)
        hid = (act * up).astype(BF)
        dg = (dh * up * slope).astype(BF)
        du = (dh * act).astype(BF)
        s.hid[r, :] = hid
        s.dg[r, :] = dg
        s.du[r, :] = du
        s.y[r, :] += nn(hid, s.wd[cols, :])
        s.dn[r, :] += nt(dg, s.wg[:, cols]) + nt(du, s.wu[:, cols])

    loop(s.tokens // rb, forward)


def ffn_grads(s, tile, ft, gb):
    cols = rows_of(tile, ft)

    def grads(i):
        r = rows_of(i, gb)
        s.wd[cols, r] = nn(s.ct[r, :], s.hid[...]).astype(BF).T
        s.wg[r, cols] = nn(s.n2t[r, :], s.dg[...]).astype(BF)
        s.wu[r, cols] = nn(s.n2t[r, :], s.du[...]).astype(BF)

    loop(s.width // gb, grads)


def ffn_close(s, rb):
    def body(i):
        r = rows_of(i, rb)
        mid = s.mid[r, :]
        dn = s.dn[r, :]
        scale = lax.rsqrt(jnp.mean(mid * mid, axis=-1, keepdims=True) + EPSILON)
        gdn = dn * s.gain[1:2, :]
        dot = jnp.mean(gdn * mid, axis=-1, keepdims=True)
        dmid = s.c[r, :].astype(F32) + scale * gdn - mid * (scale * scale * scale * dot)
        s.small[1:2, :] += jnp.sum(dn * mid * scale, axis=0, keepdims=True)
        s.dn[r, :] = dmid
        s.k[r, :] = dmid.astype(BF)
        s.c[r, :] = s.y[r, :].astype(BF)

    loop(s.tokens // rb, body)


def out_backward(s, rb):
    def body(i):
        r = rows_of(i, rb)
        d = nt(s.k[r, :], s.wo[...]).astype(BF)
        s.do[r, :] = d
        s.dot[:, r] = d.T

    loop(s.tokens // rb, body)


def out_grads(s, gb):
    def grads(i):
        r = rows_of(i, gb)
        s.wo[r, :] = nn(s.ot[r, :], s.k[...]).astype(BF)

    loop(s.width // gb, grads)


def attend_back(s, i):
    length = s.length
    blocks = length // 128
    pair = lax.div(i, 2) + (s.heads // 4) * lax.rem(i, 2)
    here, natural = rows_of(i, 128), rows_of(pair, 128)
    keep = half_masks(BF)
    left = lax.broadcasted_iota(jnp.int32, (1, 128), 1) < 64
    parts = {}
    for sub in range(2):
        head = 2 * pair + sub
        hr = rows_of(head, 64)
        for m in range(s.micro):
            mr = slice(m * length, (m + 1) * length)
            pr = rows_of((2 * i + sub) * s.micro + m, length)
            dp = nt(s.v[mr, here] * keep[sub], s.do[mr, natural])
            inner = jnp.sum(s.dot[hr, mr].astype(F32) * s.ot[hr, mr].astype(F32), axis=0, keepdims=True)
            ds = s.p[pr, :].astype(F32) * (dp - inner)
            if m == 0:
                s.toep[...] = jnp.zeros_like(s.toep)
            for j in range(blocks):
                at = 128 * (blocks - 1 - j)
                s.toep[:, at : at + length] += ds[128 * j : 128 * (j + 1), :]
            low = ds.astype(BF)
            s.ds[...] = low
            parts[sub, m, 2] = nn(s.kt[hr, mr], low)
            parts[sub, m, 0] = nn(s.ds[...], s.q[mr, here])
            parts[sub, m, 1] = nn(s.p[pr, :], s.do[mr, natural])
            if sub == 1:
                s.k[mr, here] = jnp.where(left, parts[0, m, 0], parts[1, m, 0]).astype(BF)
                s.v[mr, here] = jnp.where(left, parts[0, m, 1], parts[1, m, 1]).astype(BF)
                s.q[mr, here] = jnp.concatenate([parts[0, m, 2], parts[1, m, 2]], axis=0).astype(BF).T
        fold = s.toep[...]
        rows = 64
        while rows >= 8:
            fold = fold[:rows, :] + pltpu.roll(fold[rows:, :], 2 * length - rows, 1)
            rows //= 2
        for r in range(8):
            s.goff[r, pl.ds(head, 1), :] = fold[r : r + 1, :]


def slab(s, chunk, side):
    start = chunk * (4 * s.micro * s.length) + side * s.width
    return pl.ds(pl.multiple_of(start, 128), s.width)


def chunk_grads(s, chunk, gb):
    cols = rows_of(chunk, 256)

    def body(i):
        r = rows_of(i, gb)
        for w, grad in enumerate((s.q, s.k, s.v)):
            g = nn(s.n1t[r, :], grad[:, cols]).astype(BF)
            for side in range(2):
                start = chunk * (4 * s.micro * s.length) + side * s.width + i * gb
                s.p[pl.ds(pl.multiple_of(start, gb & -gb), gb), 128 * w : 128 * (w + 1)] = g[:, 128 * side : 128 * (side + 1)]

    loop(s.width // gb, body)


def table_grad(s):
    total = None
    for r in range(8):
        part = pltpu.roll(s.goff[r, :, :], 127 - r, 1)
        total = part if total is None else total + part
    return contract(total, bucket_classes(s), (1, 1), precision=PRECISE)


def qkv_back_input(s, rb):
    order = [spot(s, pair) for pair in range(s.heads // 2)]

    def body(i):
        r = rows_of(i, rb)
        dn = None
        for grad, weight in ((s.q, s.wq), (s.k, s.wk), (s.v, s.wv)):
            part = nt(jnp.concatenate([grad[r, 128 * at : 128 * (at + 1)] for at in order], axis=1), weight[...])
            dn = part if dn is None else dn + part
        x = s.x[r, :].astype(F32)
        scale = lax.rsqrt(jnp.mean(x * x, axis=-1, keepdims=True) + EPSILON)
        gdn = dn * s.gain[0:1, :]
        dot = jnp.mean(gdn * x, axis=-1, keepdims=True)
        s.small[0:1, :] += jnp.sum(dn * x * scale, axis=0, keepdims=True)
        s.x[r, :] = (s.dn[r, :] + scale * gdn - x * (scale * scale * scale * dot)).astype(BF)

    loop(s.tokens // rb, body)


OUT = 3


def ffn_unit(part, which):
    return 4 + 3 * part + which


def place(s):
    s.z, s.row, s.col = lax.axis_index("dp"), lax.axis_index("row"), lax.axis_index("col")
    s.core, s.xx = lax.rem(s.row, 2), lax.div(s.row, 2)
    s.row_p = 2 * s.xx + 1 - s.core
    s.row_x = 2 * (1 - s.xx) + s.core
    s.row_px = 2 * (1 - s.xx) + 1 - s.core
    s.col_y = 1 - s.col
    s.to_p, s.to_x = (s.z, s.row_p, s.col), (s.z, s.row_x, s.col)
    s.to_y, s.to_xy = (s.z, s.row, s.col_y), (s.z, s.row_x, s.col_y)
    s.me = 2 * s.row + s.col
    s.plane = [(s.z, lax.rem(s.row + (i // 2), 4), lax.rem(s.col + i % 2, 2)) for i in range(1, 8)]
    s.stack = [(lax.rem(s.z + i, 4), s.row, s.col) for i in range(1, 4)]
    s.plane_ids = [2 * row + col for _, row, col in s.plane]
    s.stack_ids = [z for z, _, _ in s.stack]
    s.inner = jnp.logical_and(s.z >= 1, s.z <= 2)
    s.outer = jnp.logical_not(s.inner)
    s.z_in, s.z_out = 1 + lax.div(s.z, 2), 3 * lax.div(s.z, 2)


def greet(s):
    barrier = pltpu.get_barrier_semaphore()
    for peer in s.plane + s.stack:
        pl.semaphore_signal(barrier, inc=1, device_id=peer, device_id_type=MESH)
    pl.semaphore_wait(barrier, len(s.plane) + len(s.stack))


def unit_shape(s, unit):
    rb, cb = s.width // 4, s.width // 2
    if unit <= OUT:
        return rb, cb
    part = s.hidden // CHUNKS
    return (part // 4, cb) if (unit - 4) % 3 == 2 else (rb, part // 2)


def span(start, size):
    return pl.ds(pl.multiple_of(start, size & -size), size)


def block(s, unit, row, col, half=None, grad=False):
    rb, cb = unit_shape(s, unit)
    size = rb if half is None else rb // 2
    down = row * rb + (0 if half is None else half * size)
    if unit < OUT and grad:
        return s.p.at[span(unit * (4 * s.micro * s.length) + col * s.width + down, size), 0:cb]
    if unit <= OUT:
        return (s.wq, s.wk, s.wv, s.wo)[unit].at[span(down, size), span(col * cb, cb)]
    part, which = divmod(unit - 4, 3)
    offset = part * (s.hidden // CHUNKS)
    if which == 2:
        return s.wd.at[span(offset + down, size), span(col * cb, cb)]
    return (s.wg, s.wu)[which].at[span(down, size), span(offset + col * cb, cb)]


def send(s, family, unit, kind, src, dst, peer):
    return pltpu.make_async_remote_copy(
        src_ref=src, dst_ref=dst, send_sem=getattr(s, family + "_send").at[unit, kind],
        recv_sem=getattr(s, family + "_recv").at[unit, kind], device_id=peer, device_id_type=MESH)


def own_source(s, unit, half=None):
    rb, cb = unit_shape(s, unit)
    if unit <= OUT:
        piece, start = s.pieces[unit], 0
    else:
        part, which = divmod(unit - 4, 3)
        if which < 2:
            return block(s, unit, s.row, s.col, half)
        piece, start = s.pieces[6], part * rb
    if half is None:
        return piece.at[start : start + rb, :]
    return piece.at[start + half * (rb // 2) : start + (half + 1) * (rb // 2), :]


def own_copies(s, unit):
    rb, cb = unit_shape(s, unit)
    own = block(s, unit, s.row, s.col)
    part, which = divmod(unit - 4, 3)
    if unit <= OUT or which == 2:
        return [pltpu.make_async_copy(own_source(s, unit), own, s.own_sems.at[unit, 0])]
    piece, half = s.pieces[4 + which], cb // 2
    size = s.hidden // 4
    offset = part * (s.hidden // CHUNKS)
    mine = (s.wg, s.wu)[which]
    return [
        pltpu.make_async_copy(
            piece.at[:, i * size + part * half : i * size + (part + 1) * half],
            mine.at[span(s.row * rb, rb), span(offset + s.col * cb + i * half, half)], s.own_sems.at[unit, i])
        for i in range(2)]


def ag_copy(s, unit, kind):
    b = functools.partial(block, s, unit)
    if kind < 3:
        return send(s, "ag", unit, kind, own_source(s, unit), b(s.row, s.col), (s.to_x, s.to_y, s.to_p)[kind])
    there, peer = [
        (b(s.row_x, s.col, 0), s.to_y), (b(s.row, s.col_y, 1), s.to_x), (b(s.row_x, s.col), s.to_p), (b(s.row, s.col_y), s.to_p),
        (b(s.row_x, s.col_y, 0), s.to_p), (b(s.row_x, s.col_y, 1), s.to_p)][kind - 3]
    return send(s, "ag", unit, kind, there, there, peer)


def ag_arrive(s, unit, kind):
    b = functools.partial(block, s, unit)
    where = [
        b(s.row_x, s.col), b(s.row, s.col_y), b(s.row_p, s.col), b(s.row_x, s.col_y, 0), b(s.row_x, s.col_y, 1),
        b(s.row_px, s.col), b(s.row_p, s.col_y), b(s.row_px, s.col_y, 0), b(s.row_px, s.col_y, 1)][kind]
    send(s, "ag", unit, kind, where, where, s.to_p).wait_recv()


def shuffled(unit):
    return unit > OUT and (unit - 4) % 3 < 2


def own_wait(s, unit):
    for copy in own_copies(s, unit):
        copy.wait()


def ag_open(s, unit):
    if shuffled(unit):
        own_wait(s, unit)
    for kind in range(3):
        ag_copy(s, unit, kind).start()


def ag_relay(s, unit):
    for kind in range(2):
        ag_arrive(s, unit, kind)
        ag_copy(s, unit, kind + 3).start()
        ag_copy(s, unit, kind + 5).start()


def ag_corner(s, unit):
    for kind in (3, 4):
        ag_arrive(s, unit, kind)
        ag_copy(s, unit, kind + 4).start()


def ag_close(s, unit):
    if not shuffled(unit):
        own_wait(s, unit)
    for kind in (2, 5, 6, 7, 8):
        ag_arrive(s, unit, kind)


def ag_sent(s, unit):
    for kind in range(9):
        ag_copy(s, unit, kind).wait_send()


def swap_copy(s, family, i, peer, slot):
    slots = getattr(s, family + "_slots")
    return pltpu.make_async_remote_copy(
        src_ref=getattr(s, family + "_from"), dst_ref=slots.at[slot], send_sem=getattr(s, family + "_send").at[i],
        recv_sem=getattr(s, family + "_recv").at[slot], device_id=peer, device_id_type=MESH)


def swap_open(s, family, peers, me):
    getattr(s, family + "_slots")[me] = getattr(s, family + "_from")[...]
    for i, peer in enumerate(peers):
        swap_copy(s, family, i, peer, me).start()


def swap_wait(s, family, peers, ids):
    for i, (peer, slot) in enumerate(zip(peers, ids)):
        copy = swap_copy(s, family, i, peer, slot)
        copy.wait_recv()
        copy.wait_send()


def swap_close(s, family, peers, ids):
    swap_wait(s, family, peers, ids)
    slots = getattr(s, family + "_slots")
    total = slots[0]
    for i in range(1, len(ids) + 1):
        total = total + slots[i]
    return total


def small_rows(s):
    return 2 * (s.width // 128) + s.heads


def small_pack(s, table):
    wide = s.width // 128
    for i in range(2):
        for j in range(wide):
            s.near_from[i * wide + j : i * wide + j + 1, :] = s.small[i : i + 1, 128 * j : 128 * (j + 1)]
    s.near_from[2 * wide : 2 * wide + s.heads, 0 : s.buckets] = table


def rs_copy(s, unit, kind):
    b = functools.partial(block, s, unit, grad=True)
    n = lambda name: getattr(s, f"{name}{unit}")
    low = s.z - 1
    if kind < 4:
        x, col = divmod(kind, 2)
        return send(s, "rs", unit, kind, b(2 * x + 1 - s.core, col), n("pr").at[x, col], s.to_p)
    if kind < 6:
        return send(s, "rs", unit, kind, b(s.row_x, kind - 4, 0), n("xa").at[kind - 4], s.to_x)
    if kind < 8:
        return send(s, "rs", unit, kind, b(2 * (kind - 6) + s.core, s.col_y, 1), n("yb").at[kind - 6], s.to_y)
    up, side = (s.z_out, s.row, s.col), (3 - s.z, s.row, s.col)
    src, dst, peer = [
        lambda: (b(s.row, s.col_y, 0), n("ya"), s.to_y),
        lambda: (b(s.row_x, s.col, 1), n("xb"), s.to_x),
        lambda: (b(s.row, s.col), n("zi"), (s.z_in, s.row, s.col)),
        lambda: (b(s.row, s.col, 1 - low), n("zx"), side),
        lambda: (b(s.row, s.col, low), b(s.row_p, s.col, low), side),
        lambda: (b(s.row, s.col, low), b(s.row_p, s.col, low), up),
        lambda: (b(s.row_p, s.col, 1 - low), b(s.row_p, s.col, 1 - low), up)][kind - 8]()
    return send(s, "rs", unit, kind, src, dst, peer)


def rs_arrive(s, unit, kind):
    b = functools.partial(block, s, unit, grad=True)
    n = lambda name: getattr(s, f"{name}{unit}")
    if kind < 4:
        where = n("pr").at[kind // 2, kind % 2]
    elif kind < 6:
        where = n("xa").at[kind - 4]
    elif kind < 8:
        where = n("yb").at[kind - 6]
    elif kind < 12:
        where = n(("ya", "xb", "zi", "zx")[kind - 8])
    else:
        where = b(s.row_p, s.col, (2 - s.z, s.z_in - 1, 2 - s.z_in)[kind - 12])
    send(s, "rs", unit, kind, where, where, s.to_p).wait_recv()
    return where


def add_into(target, source):
    rows = target.shape[0]
    step = 32 if rows % 32 == 0 else 16

    def body(i):
        r = rows_of(i, step)
        target[r, :] = (target[r, :].astype(F32) + source[r, :].astype(F32)).astype(BF)

    loop(rows // step, body)


def rs_1(s, unit):
    for kind in range(4):
        rs_copy(s, unit, kind).start()


def rs_2(s, unit):
    b = functools.partial(block, s, unit, grad=True)
    for kind in range(4):
        x, col = divmod(kind, 2)
        add_into(b(2 * x + s.core, col), rs_arrive(s, unit, kind))
    for kind in range(4, 8):
        rs_copy(s, unit, kind).start()


def rs_3(s, unit):
    b = functools.partial(block, s, unit, grad=True)
    for col in range(2):
        add_into(b(s.row, col, 0), rs_arrive(s, unit, 4 + col))
    rs_copy(s, unit, 8).start()
    for x in range(2):
        add_into(b(2 * x + s.core, s.col, 1), rs_arrive(s, unit, 6 + x))
    rs_copy(s, unit, 9).start()


def rs_4(s, unit):
    b = functools.partial(block, s, unit, grad=True)
    for half in range(2):
        add_into(b(s.row, s.col, half), rs_arrive(s, unit, 8 + half))
    for kind in range(10):
        rs_copy(s, unit, kind).wait_send()

    @pl.when(s.outer)
    def _():
        rs_copy(s, unit, 10).start()


def rs_5(s, unit):
    @pl.when(s.inner)
    def _():
        add_into(block(s, unit, s.row, s.col, grad=True), rs_arrive(s, unit, 10))
        rs_copy(s, unit, 11).start()


def rs_6(s, unit):
    @pl.when(s.inner)
    def _():
        mine = block(s, unit, s.row, s.col, s.z - 1, grad=True)
        add_into(mine, rs_arrive(s, unit, 11))
        rs_copy(s, unit, 12).start()
        rs_copy(s, unit, 13).start()
        done = block(s, unit, s.row_p, s.col, s.z - 1, grad=True)
        done[...] = mine[...]


def rs_7(s, unit):
    @pl.when(s.inner)
    def _():
        rs_arrive(s, unit, 12)
        rs_copy(s, unit, 14).start()
        for kind in (11, 12, 13):
            rs_copy(s, unit, kind).wait_send()

    @pl.when(s.outer)
    def _():
        rs_arrive(s, unit, 13)
        rs_copy(s, unit, 10).wait_send()


def rs_8(s, unit):
    @pl.when(s.inner)
    def _():
        rs_copy(s, unit, 14).wait_send()

    @pl.when(s.outer)
    def _():
        rs_arrive(s, unit, 14)

    rs_out(s, unit).start()


def rs_out(s, unit):
    return pltpu.make_async_copy(block(s, unit, s.row_p, s.col, grad=True), s.unit_out[unit], s.out_sems.at[unit])


NAMES = ("wq", "wk", "wv", "wo", "wg", "wu", "wd")
STEPS = (rs_1, rs_2, rs_3, rs_4, rs_5, rs_6, rs_7, rs_8)
G0, U0, D0, G1, U1, D1 = (ffn_unit(part, which) for part in range(2) for which in range(3))
UNITS = OUT + 1 + 3 * CHUNKS
EARLY = (G0, U0, D0)


class Reducer:
    def __init__(self, s):
        self.s, self.done = s, {unit: 0 for unit in range(UNITS)}

    def plan(self, *units):
        todo = []
        for unit in units:
            todo.append((STEPS[self.done[unit]], unit))
            self.done[unit] += 1
        return todo

    def run(self, *units):
        act_all(self.s, self.plan(*units))


def act_all(s, todo):
    for act, unit in todo if s.comm else ():
        act(s, unit)


def at_step(s, index, steps):
    for number, todo in enumerate(steps):
        if todo and s.comm:

            @pl.when(index == number)
            def _():
                act_all(s, todo)


def gather(*names):
    kinds = dict(o=ag_open, r=ag_relay, c=ag_corner, x=ag_close, s=ag_sent)
    return [(kinds[kind], unit) for kind, unit in names]


def gains_in(s):
    for i, gain in enumerate((s.gain_one, s.gain_two)):
        if s.comm:
            s.gain_from[i : i + 1, 0 : gain.shape[1]] = gain[...].astype(F32)
        else:
            s.gain[i : i + 1, :] = gain[...].astype(F32)


def gains_spread(s):
    swap_wait(s, "gain", s.plane, s.plane_ids)
    count = s.gain_one.shape[1]
    wide = (128, s.width)
    lane, spot = lax.broadcasted_iota(jnp.int32, wide, 0), lax.broadcasted_iota(jnp.int32, wide, 1)
    total = None
    for i in range(8):
        part = nn(s.gain_slots[i].astype(BF), jnp.logical_and(spot == lane + count * i, lane < count).astype(BF))
        total = part if total is None else total + part
    s.gain[...] = total


def layer(cfg, *refs):
    s = types.SimpleNamespace(**cfg)
    for name, ref in zip(cfg["names"], refs):
        setattr(s, name, ref)
    s.pieces = [getattr(s, n + "_in") for n in NAMES]
    comm = s.comm
    load_x = pltpu.make_async_copy(s.x_in, s.x, s.io_sems.at[0])
    load_c = pltpu.make_async_copy(s.c_in, s.c, s.io_sems.at[1])
    load_x.start()
    load_c.start()
    Q, K, V, O = range(4)
    if comm:
        place(s)
        s.unit_out = [getattr(s, f"unit{u}_out") for u in range(UNITS)]
        greet(s)
        for unit in range(UNITS):
            for copy in own_copies(s, unit):
                copy.start()
        act_all(s, gather(("o", Q), ("o", K)))
        s.gain_from[...] = jnp.zeros_like(s.gain_from)
        gains_in(s)
        swap_open(s, "gain", s.plane, s.me)
    else:
        weights = [pltpu.make_async_copy(piece, getattr(s, n), s.load_sems.at[i]) for i, (n, piece) in enumerate(zip(NAMES, s.pieces))]
        for copy in weights:
            copy.start()
        gains_in(s)
    s.small[...] = jnp.zeros_like(s.small)
    s.near_from[...] = jnp.zeros_like(s.near_from)
    offset_rows(s)
    tw, wt = (s.tokens, s.width), (s.width, s.tokens)
    vm = pltpu.VMEM

    def attention(a, mask):
        s.a, s.mask = a, mask
        masks(s)
        load_x.wait()
        if comm:
            gains_spread(s)
        else:
            for copy in weights:
                copy.wait()
        norm_in(s, 128)
        act_all(s, gather(("r", Q), ("o", V), ("r", K), ("c", Q), ("o", O), ("r", V), ("c", K), ("o", G0), ("x", Q)))
        project(s, Q, 256)
        act_all(s, gather(("c", V), ("x", K)))
        project(s, K, 256)
        act_all(s, gather(("r", O), ("o", U0), ("x", V)))
        project(s, V, 256)
        plan = [
            gather(("c", O), ("r", G0)), gather(("o", D0)), gather(("c", G0), ("r", U0), ("o", G1)), gather(("c", U0)),
            gather(("r", D0), ("o", U1)), gather(("c", D0), ("r", G1), ("o", D1))]

        def step(i):
            at_step(s, i, plan)
            attend_pair(s, i)

        loop(s.heads // 2, step)

    pl.run_scoped(attention, vm(tw, BF), vm((s.micro, s.length, s.length), F32))
    reducer = Reducer(s)
    reduce = reducer.run
    s.n2t = s.vt

    def feed(act, mid, y, ct):
        s.mid, s.y, s.ct = mid, y, ct
        s.hid, s.dg, s.du = (act.at[:, i * s.ft : (i + 1) * s.ft] for i in range(3))
        load_c.wait()
        act_all(s, gather(("x", O)))
        out_project(s, 256)
        act_all(s, gather(("c", G1), ("r", U1), ("x", G0), ("x", U0), ("x", D0)))
        plan = reducer.plan
        ahead, amid = [[], gather(("c", U1), ("r", D1))], [gather(*[("s", u) for u in EARLY]), gather(("c", D1))]
        ahead.append(gather(("x", G1), ("x", U1), ("x", D1)) + plan(G0, U0, D0))
        amid.append(gather(*[("s", u) for u in (G1, U1, D1)]) + plan(G0, U0))
        ahead.append(plan(G0, D0))
        amid.append(plan(U0, G0))

        def step(t):
            at_step(s, t, ahead)
            ffn_rows(s, t, s.ft, 256)
            at_step(s, t, amid)
            ffn_grads(s, t, s.ft, s.gb)

        loop(s.hidden // s.ft, step)
        ffn_close(s, 128)

    pl.run_scoped(feed, vm((s.tokens, 3 * s.ft), BF), vm(tw, F32), vm(tw, F32), vm(wt, BF))
    put_y = pltpu.make_async_copy(s.c, s.y_out, s.io_sems.at[0])
    put_x = pltpu.make_async_copy(s.x, s.gi_out, s.io_sems.at[1])
    put_y.start()

    def back(dot, *bufs):
        s.do, s.dot = s.c, dot
        for name, ref in zip(s.rs_names, bufs):
            setattr(s, name, ref)
        if comm:
            for peer in [s.to_p, s.to_x, s.to_y] + s.stack:
                pl.semaphore_signal(s.ready, inc=1, device_id=peer, device_id_type=MESH)
            pl.semaphore_wait(s.ready, 6)
        reduce(G1, U1, D1, D0, U0, G0)
        put_y.wait()
        out_backward(s, 256)
        act_all(s, gather(("s", Q), ("s", K), ("s", V), ("s", O)))
        out_grads(s, 256)
        reduce(O, G1, D0, U0, G0)
        plan = reducer.plan
        reducer.done.update({0: 1, 1: 1, 2: 1})
        ahead = [
            plan(U1, G1), plan(D1, D0, U0, G0), plan(U1, G1, O, D0, U0, G0), plan(D1, G1, U1, U0, 0), plan(O, G1, U1, D1, D0),
            plan(O, G1, U1, D1, D0, 0, 1)]

        def step(i):
            at_step(s, i, ahead)
            attend_back(s, i)

            @pl.when(lax.rem(i, 2) == 1)
            def _():
                chunk = lax.div(i, 2)
                chunk_grads(s, chunk, 384)
                at_step(s, chunk, [[(rs_1, unit)] for unit in range(3)])

        loop(s.heads // 2, step)
        reduce(2, 1, 0, O, D1, U1, G1)
        table = table_grad(s)
        qkv_back_input(s, 256)
        put_x.start()
        small_pack(s, table)
        if comm:
            swap_open(s, "near", s.plane, s.me)
            left = lambda: [u for u in (2, 1, 0, O, D1, U1, G1) + EARLY if reducer.done[u] < 8]
            reduce(*left())
            s.far_from[...] = swap_close(s, "near", s.plane, s.plane_ids)
            swap_open(s, "far", s.stack, s.z)
            while left():
                reduce(*left())
            s.small_out[...] = swap_close(s, "far", s.stack, s.stack_ids)
            for unit in range(UNITS):
                rs_out(s, unit).wait()
        else:
            s.small_out[...] = s.near_from[...]
            outs = [pltpu.make_async_copy(getattr(s, n), getattr(s, n + "_out"), s.load_sems.at[i + 3]) for i, n in enumerate(NAMES[3:])]
            for copy in outs:
                copy.start()
            for copy in outs:
                copy.wait()
            half = s.heads // 4
            for w, n in enumerate(NAMES[:3]):
                for pair in range(s.heads // 2):
                    copy = pltpu.make_async_copy(
                        s.p.at[slab(s, pair % half, pair // half), 128 * w : 128 * (w + 1)],
                        getattr(s, n + "_out").at[:, 128 * pair : 128 * (pair + 1)], s.load_sems.at[w])
                    copy.start()
                    copy.wait()

    pl.run_scoped(back, vm(wt, BF), *[vm(shape, BF) for shape in s.rs_shapes])
    put_x.wait()


def call_layer(comm, x, c, weights, gains, seg, bucket, table, full):
    tokens, width = x.shape
    micro, length = seg.shape
    heads, buckets = table.shape
    hidden = full[4][1]
    ft, vm, sem = 512, pltpu.VMEM, pltpu.SemaphoreType.DMA
    tw, wt, tiny = (tokens, width), (width, tokens), (2 * (width // 128) + heads, 128)
    s = types.SimpleNamespace(
        comm=comm, tokens=tokens, width=width, micro=micro, length=length, hidden=hidden, heads=heads, buckets=buckets, ft=ft, gb=256,
        rs_names=[], rs_shapes=[])
    scratch = dict(
        x=vm(tw, BF), c=vm(tw, BF), **{n: vm(shape, BF) for n, shape in zip(NAMES, full)},
        n1t=vm(wt, BF), q=vm(tw, BF), k=vm(tw, BF), v=vm(tw, BF), kt=vm(wt, BF), vt=vm(wt, BF), ot=vm(wt, BF),
        dn=vm(tw, F32), toep=vm((128, 2 * length), F32), ds=vm((length, length), BF), p=vm((heads * micro * length, length), BF),
        offs=vm((heads, 2 * length), F32), goff=vm((8, heads, 2 * length), F32), gain=vm((8, width), F32), small=vm((2, width), F32), near_from=vm(tiny, F32),
        turned=vm((1, 2 * length), jnp.int32), io_sems=sem((2,)), load_sems=sem((7,)), out_sems=sem((UNITS,)),
    )
    out_shape = [(tw, BF)] * 2
    if comm:
        scratch.update(
            gain_from=vm((8, 128), F32), far_from=vm(tiny, F32),
            gain_slots=vm((8, 8, 128), F32), near_slots=vm((8, *tiny), F32), far_slots=vm((4, *tiny), F32),
            ag_send=sem((UNITS, 9)), ag_recv=sem((UNITS, 9)), own_sems=sem((UNITS, 2)), rs_send=sem((UNITS, 15)), rs_recv=sem((UNITS, 15)),
            gain_send=sem((7,)), gain_recv=sem((8,)), near_send=sem((7,)), near_recv=sem((8,)), far_send=sem((3,)), far_recv=sem((4,)),
            ready=pltpu.SemaphoreType.REGULAR,
        )
        for unit in range(UNITS):
            rb, cb = unit_shape(s, unit)
            hb = rb // 2
            shapes = dict(pr=(2, 2, rb, cb), xa=(2, hb, cb), yb=(2, hb, cb), ya=(hb, cb), xb=(hb, cb), zi=(rb, cb), zx=(hb, cb))
            for name, shape in shapes.items():
                if unit in EARLY:
                    scratch[f"{name}{unit}"] = vm(shape, BF)
                else:
                    s.rs_names.append(f"{name}{unit}")
                    s.rs_shapes.append(shape)
            out_shape.append(((rb, cb), BF))
        grad_names = [f"unit{unit}_out" for unit in range(UNITS)]
    else:
        out_shape += [(shape, BF) for shape in full]
        grad_names = [n + "_out" for n in NAMES]
    ins = ["x_in", "c_in"] + [n + "_in" for n in NAMES] + ["gain_one", "gain_two", "seg", "bucket", "table"]
    outs = ["y_out", "gi_out"] + grad_names + ["small_out"]
    out_shape.append((tiny, F32))
    names = ins + outs + list(scratch)
    far, near = pl.BlockSpec(memory_space=pl.ANY), pl.BlockSpec(memory_space=pltpu.VMEM)
    params = dict(vmem_limit_bytes=67043328)
    if comm:
        params.update(collective_id=0, has_side_effects=True)

    def body(*refs):
        cfg = dict(vars(s), names=names)
        layer(cfg, *refs)

    return pl.pallas_call(
        body, out_shape=[jax.ShapeDtypeStruct(*o) for o in out_shape],
        in_specs=[far] * 9 + [near] * 5, out_specs=[far] * (len(outs) - 1) + [near], scratch_shapes=list(scratch.values()),
        compiler_params=pltpu.CompilerParams(**params),
    )(x, c, *weights, *gains, seg, bucket, table)


def finish_kernel(cfg, *refs):
    s = types.SimpleNamespace(**cfg)
    small, srcs, outs = refs[0], refs[1 : 3 + UNITS], refs[3 + UNITS : 3 + UNITS + 12]
    bufs = refs[15 + UNITS : 15 + 2 + 2 * UNITS]
    wide, (in_sems, out_sems) = refs[17 + 2 * UNITS : -2], refs[-2:]
    loads = [pltpu.make_async_copy(src, buf, in_sems.at[i]) for i, (src, buf) in enumerate(zip(srcs, bufs))]
    for i in list(range(2, len(loads))) + [0, 1]:
        loads[i].start()
    row, col = lax.axis_index("row"), lax.axis_index("col")
    y, gi, gain_one, gq, gk, gv, go, table, gain_two, gg, gu, gd = outs
    rows = s.width // 128
    at = lax.rem(s.width - s.gain_count * (2 * row + col), s.width)
    for i, out in enumerate((gain_one, gain_two)):
        full = jnp.concatenate([small[i * rows + j : i * rows + j + 1, :] for j in range(rows)], axis=1)
        out[...] = pltpu.roll(jnp.broadcast_to(full, (8, s.width)), at, 1)[0:1, 0 : s.gain_count]
    table[...] = small[2 * rows : 2 * rows + s.heads, 0 : s.buckets]
    units = bufs[2:]
    stores = []

    def leave(buf, out):
        stores.append(pltpu.make_async_copy(buf, out, out_sems.at[len(stores)]))
        stores[-1].start()

    wq, wk, wv, wo, wg, wu, wd = wide
    for unit in range(3):
        loads[2 + unit].wait()
        for w, buf in enumerate((wq, wk, wv)):
            buf[:, 128 * unit : 128 * (unit + 1)] = units[unit][:, 128 * w : 128 * (w + 1)].astype(F32)
    for buf, out in ((wq, gq), (wk, gk), (wv, gv)):
        leave(buf, out)
    loads[2 + OUT].wait()
    wo[...] = units[OUT][...].astype(F32)
    leave(wo, go)
    for which, buf, out in ((0, wg, gg), (1, wu, gu), (2, wd, gd)):
        for part in range(CHUNKS):
            unit = ffn_unit(part, which)
            loads[2 + unit].wait()
            rows, cols = units[unit].shape
            if which == 2:
                buf[part * rows : (part + 1) * rows, :] = units[unit][...].astype(F32)
            else:
                size = buf.shape[1] // 2
                for i in range(2):
                    at = i * size + part * (cols // 2)
                    buf[:, at : at + cols // 2] = units[unit][:, i * (cols // 2) : (i + 1) * (cols // 2)].astype(F32)
        leave(buf, out)
    for i, out in enumerate((y, gi)):
        loads[i].wait()
        leave(bufs[i], out)
    for copy in stores:
        copy.wait()


def finish(small, arrays, gain_count, heads, buckets, blocks):
    vm, sh = pltpu.VMEM, jax.ShapeDtypeStruct
    far, near = pl.BlockSpec(memory_space=pl.ANY), pl.BlockSpec(memory_space=pltpu.VMEM)
    y, gi = arrays[:2]
    b = [sh(shape, F32) for shape in blocks]
    gain = sh((1, gain_count), F32)
    cfg = dict(width=y.shape[1], gain_count=gain_count, heads=heads, buckets=buckets)
    return pl.pallas_call(
        functools.partial(finish_kernel, cfg),
        out_shape=[sh(y.shape, BF), sh(gi.shape, BF), gain, *b[:4], sh((heads, buckets), F32), gain, *b[4:]],
        in_specs=[near] + [far] * len(arrays), out_specs=[far, far, near, far, far, far, far, near, near, far, far, far],
        scratch_shapes=[vm(a.shape, BF) for a in arrays] + [vm(shape, F32) for shape in blocks]
        + [pltpu.SemaphoreType.DMA((len(arrays),)), pltpu.SemaphoreType.DMA((9,))],
        compiler_params=pltpu.CompilerParams(vmem_limit_bytes=67043328),
    )(small, *arrays)


def open_block(gathered, row_count, column_count):
    _, rows, columns = gathered.shape
    grid = gathered.reshape(row_count, column_count, rows, columns).transpose(0, 2, 1, 3)
    return grid.reshape(row_count * rows, column_count * columns)


def close_block(full, row_count, column_count):
    rows, columns = full.shape[0] // row_count, full.shape[1] // column_count
    grid = full.reshape(row_count, rows, column_count, columns).transpose(0, 2, 1, 3)
    return grid.reshape(row_count * column_count, rows, columns)


def shards(block_input, segment_ids, bucket, gain_attn, w_query, w_key, w_value, w_out, bias_table, gain_ffn, w_gate, w_up, w_down, cotangent):
    row_count, column_count = lax.axis_size("row"), lax.axis_size("col")
    micro, length, width = block_input.shape
    tokens, gain_count = micro * length, gain_attn.shape[0]
    buckets, heads = bias_table.shape
    pieces = [w_query, w_key, w_value, w_out, w_gate, w_up, w_down]
    full = [(p.shape[0] * row_count, p.shape[1] * column_count) for p in pieces]
    fits = row_count == 4 and column_count == 2 and lax.axis_size("dp") == 4
    x, c = block_input.reshape(tokens, width), cotangent.reshape(tokens, width)
    gains = [gain_attn[None], gain_ffn[None]]
    plane = ("row", "col")
    if fits:
        out = call_layer(True, x, c, pieces, gains, segment_ids, bucket[None], bias_table.T, full)
        y, gi, one, gq, gk, gv, go, table, two, gg, gu, gd = finish(
            out[-1], out[:-1], gain_count, heads, buckets, [p.shape for p in pieces])
        return y.reshape(block_input.shape), gi.reshape(block_input.shape), one[0], gq, gk, gv, go, table.T, two[0], gg, gu, gd
    gains = [lax.all_gather(g, plane, axis=1, tiled=True) for g in gains]
    weights = [open_block(lax.all_gather(p[None], plane, axis=0, tiled=True), row_count, column_count) for p in pieces]
    out = call_layer(False, x, c, weights, gains, segment_ids, bucket[None], bias_table.T, full)
    y, gi, grads, small = out[0], out[1], out[2:9], out[9]
    small = lax.psum(small, ("dp",) + plane)
    grads = [lax.psum_scatter(close_block(g, row_count, column_count), plane, scatter_dimension=0, tiled=True)[0] for g in grads]
    gq, gk, gv, go, gg, gu, gd = (lax.psum(g, "dp").astype(F32) for g in grads)
    mine = (lax.axis_index("row") * column_count + lax.axis_index("col")) * gain_count
    one, two = (lax.dynamic_slice(small[i * (width // 128) : (i + 1) * (width // 128)].reshape(-1), (mine,), (gain_count,)) for i in range(2))
    table = small[2 * (width // 128) :, :buckets].T
    return y.reshape(block_input.shape), gi.reshape(block_input.shape), one, gq, gk, gv, go, table, two, gg, gu, gd


def solution(mesh):
    whole = P(None, ("dp", "row", "col"), None)
    split, gain = P("row", "col"), P(("row", "col"))
    return jax.shard_map(
        shards, mesh=mesh,
        in_specs=(whole, P(None, ("dp", "row", "col")), P(), gain, split, split, split, split, P(), gain, split, split, split, whole),
        out_specs=(whole, whole, gain, split, split, split, split, P(), gain, split, split, split),
        check_vma=False)
```

```python
import functools
import types

import jax
import jax.numpy as jnp
from jax import lax
from jax.experimental import pallas as pl
from jax.experimental.pallas import tpu as pltpu
from jax.sharding import PartitionSpec as P

F32 = jnp.float32
BF = jnp.bfloat16
EPSILON = 1e-06
NEGATIVE = -1e30
PRECISE = lax.Precision.HIGHEST
MESH = pl.DeviceIdType.MESH
CHUNKS = 4
GELU_0 = 0.7978845608028654
GELU_1 = 0.044715


def contract(left, right, dims, **more):
    return lax.dot_general(left, right, ((dims[:1], dims[1:]), ((), ())), preferred_element_type=F32, **more)


def nn(left, right):
    return contract(left, right, (1, 0))


def nt(left, right):
    return contract(left, right, (1, 1))


def rows_of(index, size):
    return pl.ds(pl.multiple_of(index * size, size), size)


def loop(count, body):
    lax.fori_loop(0, count, lambda index, carry: (body(index), carry)[1], 0)


def bucket_classes(s):
    return (s.turned[...] == lax.broadcasted_iota(jnp.int32, (s.buckets, 2 * s.length), 0)).astype(F32)


def offset_rows(s):
    twice = 2 * s.length
    s.turned[...] = jnp.full((1, twice), -1, jnp.int32)
    s.turned[:, 0 : twice - 1] = s.bucket[...]
    flip = (lax.broadcasted_iota(jnp.int32, (128, 128), 0) + lax.broadcasted_iota(jnp.int32, (128, 128), 1) == 127).astype(BF)
    parts = [nn(s.turned[:, i : i + 128].astype(F32).astype(BF), flip) for i in range(0, twice, 128)]
    turned = jnp.concatenate(parts[::-1], axis=1)
    s.turned[...] = pltpu.roll(turned, twice - 1, 1).astype(jnp.int32)
    s.offs[...] = contract(s.table[...], bucket_classes(s), (1, 0), precision=PRECISE)


def masks(s):
    for m in range(s.micro):
        row = s.seg[m : m + 1, :].astype(F32)
        column = jnp.broadcast_to(row, (128, s.length)).T
        for i in range(0, s.length, 128):
            s.mask[m, :, i : i + 128] = jnp.where(column == row[:, i : i + 128], 0.0, NEGATIVE)


def norm_in(s, rb):
    def body(i):
        r = rows_of(i, rb)
        x = s.x[r, :].astype(F32)
        scale = lax.rsqrt(jnp.mean(x * x, axis=-1, keepdims=True) + EPSILON)
        n = (x * scale * s.gain[0:1, :]).astype(BF)
        s.a[r, :] = n
        s.n1t[:, r] = n.T

    loop(s.tokens // rb, body)


def spot(s, pair):
    half = s.heads // 4
    return 2 * (pair % half) + pair // half


def project(s, which, side, rb):
    weight, out, out_t = ((s.wq, s.q, None), (s.wk, s.k, s.kt), (s.wv, s.v, s.vt))[which]
    wide = s.width // 2
    cols = pl.ds(pl.multiple_of(side * wide, 128), wide)

    def body(i):
        r = rows_of(i, rb)
        p = nn(s.a[r, :], weight[:, cols]).astype(BF)
        for j in range(s.heads // 4):
            out[r, rows_of(2 * j + side, 128)] = p[:, 128 * j : 128 * (j + 1)]
        if out_t is not None:
            out_t[cols, r] = p.T

    loop(s.tokens // rb, body)


def half_masks(dtype):
    lane = lax.broadcasted_iota(jnp.int32, (1, 128), 1)
    return [(lane < 64).astype(dtype), (lane >= 64).astype(dtype)]


def attend_pair(s, side, late, j):
    length = s.length
    blocks = length // 128
    pair, i = (s.heads // 4) * side + j, 2 * j + side
    here = rows_of(i, 128)
    keep = half_masks(BF)
    for sub in range(2):
        s.hook("attend", late + 2 * j + sub)
        head = 2 * pair + sub
        hr = rows_of(head, 64)
        row = jnp.broadcast_to(s.offs[pl.ds(head, 1), :], (128, 2 * length))
        s.toep[...] = pltpu.roll(row, 2 * length - 127, 1, stride=1, stride_axis=0)
        for m in range(s.micro):
            mr = slice(m * length, (m + 1) * length)
            scores = nt(s.k[mr, here] * keep[sub], s.q[mr, here])
            bias = jnp.concatenate([s.toep[:, 128 * b : 128 * b + length] for b in reversed(range(blocks))], axis=0)
            scores = scores + bias + s.mask[m]
            e = jnp.exp(scores - jnp.max(scores, axis=0, keepdims=True))
            low = (e * (1.0 / jnp.sum(e, axis=0, keepdims=True))).astype(BF)
            s.p[rows_of((2 * i + sub) * s.micro + m, length), :] = low
            s.ot[hr, mr] = nn(s.vt[hr, mr], low).astype(BF)


def out_project(s, rb):
    def body(i):
        r = rows_of(i, rb)
        mid = s.x[r, :].astype(F32) + nn(s.ot[:, r].T, s.wo[...])
        s.mid[r, :] = mid
        s.y[r, :] = mid
        scale = lax.rsqrt(jnp.mean(mid * mid, axis=-1, keepdims=True) + EPSILON)
        n = (mid * scale * s.gain[1:2, :]).astype(BF)
        s.k[r, :] = n
        s.n2t[:, r] = n.T
        s.dn[r, :] = jnp.zeros_like(mid)
        s.ct[:, r] = s.c[r, :].T

    loop(s.tokens // rb, body)


def ffn_rows(s, tile, ft, rb):
    cols = rows_of(tile, ft)

    def forward(i):
        s.hook("feed", 5 * tile + i)
        r = rows_of(i, rb)
        n = s.k[r, :]
        gate = nn(n, s.wg[:, cols])
        up = nn(n, s.wu[:, cols])
        dh = nt(s.c[r, :], s.wd[cols, :])
        square = gate * gate
        t = jnp.tanh(gate * (GELU_0 + (GELU_0 * GELU_1) * square))
        half = 0.5 + 0.5 * t
        act = gate * half
        slope = half + (0.5 * gate) * (1.0 - t * t) * (GELU_0 + (3.0 * GELU_0 * GELU_1) * square)
        hid = (act * up).astype(BF)
        dg = (dh * up * slope).astype(BF)
        du = (dh * act).astype(BF)
        s.hid[r, :] = hid
        s.dg[r, :] = dg
        s.du[r, :] = du
        s.y[r, :] += nn(hid, s.wd[cols, :])
        s.dn[r, :] += nt(dg, s.wg[:, cols]) + nt(du, s.wu[:, cols])

    loop(s.tokens // rb, forward)


def ffn_grads(s, tile, ft, gb):
    cols = rows_of(tile, ft)

    def grads(i):
        r = rows_of(i, gb)
        s.wd[cols, r] = nn(s.ct[r, :], s.hid[...]).astype(BF).T
        s.wg[r, cols] = nn(s.n2t[r, :], s.dg[...]).astype(BF)
        s.wu[r, cols] = nn(s.n2t[r, :], s.du[...]).astype(BF)

    loop(s.width // gb, grads)


def ffn_close(s, rb):
    def body(i):
        r = rows_of(i, rb)
        mid = s.mid[r, :]
        dn = s.dn[r, :]
        scale = lax.rsqrt(jnp.mean(mid * mid, axis=-1, keepdims=True) + EPSILON)
        gdn = dn * s.gain[1:2, :]
        dot = jnp.mean(gdn * mid, axis=-1, keepdims=True)
        dmid = s.c[r, :].astype(F32) + scale * gdn - mid * (scale * scale * scale * dot)
        s.small[1:2, :] += jnp.sum(dn * mid * scale, axis=0, keepdims=True)
        s.dn[r, :] = dmid
        s.k[r, :] = dmid.astype(BF)
        s.c[r, :] = s.y[r, :].astype(BF)

    loop(s.tokens // rb, body)


def out_backward(s, rb):
    def body(i):
        s.hook("outback", i)
        r = rows_of(i, rb)
        d = nt(s.k[r, :], s.wo[...]).astype(BF)
        s.do[r, :] = d
        s.dot[:, r] = d.T

    loop(s.tokens // rb, body)


def out_grads(s, gb):
    def grads(i):
        r = rows_of(i, gb)
        s.wo[r, :] = nn(s.ot[r, :], s.k[...]).astype(BF)

    loop(s.width // gb, grads)


def attend_back(s, i):
    length = s.length
    blocks = length // 128
    pair = lax.div(i, 2) + (s.heads // 4) * lax.rem(i, 2)
    here, natural = rows_of(i, 128), rows_of(pair, 128)
    keep = half_masks(BF)
    left = lax.broadcasted_iota(jnp.int32, (1, 128), 1) < 64
    parts = {}
    for sub in range(2):
        s.hook("back", 2 * i + sub)
        head = 2 * pair + sub
        hr = rows_of(head, 64)
        for m in range(s.micro):
            mr = slice(m * length, (m + 1) * length)
            pr = rows_of((2 * i + sub) * s.micro + m, length)
            dp = nt(s.v[mr, here] * keep[sub], s.do[mr, natural])
            inner = jnp.sum(s.dot[hr, mr].astype(F32) * s.ot[hr, mr].astype(F32), axis=0, keepdims=True)
            ds = s.p[pr, :].astype(F32) * (dp - inner)
            if m == 0:
                s.toep[...] = jnp.zeros_like(s.toep)
            for j in range(blocks):
                at = 128 * (blocks - 1 - j)
                s.toep[:, at : at + length] += ds[128 * j : 128 * (j + 1), :]
            low = ds.astype(BF)
            s.ds[...] = low
            parts[sub, m, 2] = nn(s.kt[hr, mr], low)
            parts[sub, m, 0] = nn(s.ds[...], s.q[mr, here])
            parts[sub, m, 1] = nn(s.p[pr, :], s.do[mr, natural])
            if sub == 1:
                s.k[mr, here] = jnp.where(left, parts[0, m, 0], parts[1, m, 0]).astype(BF)
                s.v[mr, here] = jnp.where(left, parts[0, m, 1], parts[1, m, 1]).astype(BF)
                s.q[mr, here] = jnp.concatenate([parts[0, m, 2], parts[1, m, 2]], axis=0).astype(BF).T
        fold = s.toep[...]
        rows = 64
        while rows >= 8:
            fold = fold[:rows, :] + pltpu.roll(fold[rows:, :], 2 * length - rows, 1)
            rows //= 2
        for r in range(8):
            s.goff[r, pl.ds(head, 1), :] = fold[r : r + 1, :]


def slab(s, chunk, side):
    start = chunk * (4 * s.micro * s.length) + side * s.width
    return pl.ds(pl.multiple_of(start, 128), s.width)


def chunk_grads(s, chunk, gb):
    cols = rows_of(chunk, 256)

    def body(i):
        r = rows_of(i, gb)
        for w, grad in enumerate((s.q, s.k, s.v)):
            g = nn(s.n1t[r, :], grad[:, cols]).astype(BF)
            for side in range(2):
                start = chunk * (4 * s.micro * s.length) + side * s.width + i * gb
                s.p[pl.ds(pl.multiple_of(start, gb & -gb), gb), 128 * w : 128 * (w + 1)] = g[:, 128 * side : 128 * (side + 1)]

    loop(s.width // gb, body)


def table_grad(s):
    total = None
    for r in range(8):
        part = pltpu.roll(s.goff[r, :, :], 127 - r, 1)
        total = part if total is None else total + part
    return contract(total, bucket_classes(s), (1, 1), precision=PRECISE)


def qkv_back_input(s, rb):
    order = [spot(s, pair) for pair in range(s.heads // 2)]

    def body(i):
        s.hook("input", i + 1)
        r = rows_of(i, rb)
        dn = None
        for grad, weight in ((s.q, s.wq), (s.k, s.wk), (s.v, s.wv)):
            part = nt(jnp.concatenate([grad[r, 128 * at : 128 * (at + 1)] for at in order], axis=1), weight[...])
            dn = part if dn is None else dn + part
        x = s.x[r, :].astype(F32)
        scale = lax.rsqrt(jnp.mean(x * x, axis=-1, keepdims=True) + EPSILON)
        gdn = dn * s.gain[0:1, :]
        dot = jnp.mean(gdn * x, axis=-1, keepdims=True)
        s.small[0:1, :] += jnp.sum(dn * x * scale, axis=0, keepdims=True)
        s.x[r, :] = (s.dn[r, :] + scale * gdn - x * (scale * scale * scale * dot)).astype(BF)

    loop(s.tokens // rb, body)


OUT = 3


def ffn_unit(part, which):
    return 4 + 3 * part + which


def place(s):
    s.z, s.row, s.col = lax.axis_index("dp"), lax.axis_index("row"), lax.axis_index("col")
    s.core, s.xx = lax.rem(s.row, 2), lax.div(s.row, 2)
    s.row_p = 2 * s.xx + 1 - s.core
    s.row_x = 2 * (1 - s.xx) + s.core
    s.row_px = 2 * (1 - s.xx) + 1 - s.core
    s.col_y = 1 - s.col
    s.to_p, s.to_x = (s.z, s.row_p, s.col), (s.z, s.row_x, s.col)
    s.to_y, s.to_xy = (s.z, s.row, s.col_y), (s.z, s.row_x, s.col_y)
    s.me = 2 * s.row + s.col
    s.plane = [(s.z, lax.rem(s.row + (i // 2), 4), lax.rem(s.col + i % 2, 2)) for i in range(1, 8)]
    s.stack = [(lax.rem(s.z + i, 4), s.row, s.col) for i in range(1, 4)]
    s.plane_ids = [2 * row + col for _, row, col in s.plane]
    s.stack_ids = [z for z, _, _ in s.stack]
    s.inner = jnp.logical_and(s.z >= 1, s.z <= 2)
    s.outer = jnp.logical_not(s.inner)
    s.z_in, s.z_out = 1 + lax.div(s.z, 2), 3 * lax.div(s.z, 2)


def greet(s):
    barrier = pltpu.get_barrier_semaphore()
    for peer in s.plane + s.stack:
        pl.semaphore_signal(barrier, inc=1, device_id=peer, device_id_type=MESH)
    pl.semaphore_wait(barrier, len(s.plane) + len(s.stack))


def unit_shape(s, unit):
    rb, cb = s.width // 4, s.width // 2
    if unit <= OUT:
        return rb, cb
    part = s.hidden // CHUNKS
    return (part // 4, cb) if (unit - 4) % 3 == 2 else (rb, part // 2)


def span(start, size):
    return pl.ds(pl.multiple_of(start, size & -size), size)


def block(s, unit, row, col, half=None, grad=False):
    rb, cb = unit_shape(s, unit)
    size = rb if half is None else rb // 2
    down = row * rb + (0 if half is None else half * size)
    if unit < OUT and grad:
        return s.p.at[span(unit * (4 * s.micro * s.length) + col * s.width + down, size), 0:cb]
    if unit <= OUT:
        return (s.wq, s.wk, s.wv, s.wo)[unit].at[span(down, size), span(col * cb, cb)]
    part, which = divmod(unit - 4, 3)
    offset = part * (s.hidden // CHUNKS)
    if which == 2:
        return s.wd.at[span(offset + down, size), span(col * cb, cb)]
    return (s.wg, s.wu)[which].at[span(down, size), span(offset + col * cb, cb)]


def send(s, family, unit, kind, src, dst, peer):
    return pltpu.make_async_remote_copy(
        src_ref=src, dst_ref=dst, send_sem=getattr(s, family + "_send").at[unit, kind],
        recv_sem=getattr(s, family + "_recv").at[unit, kind], device_id=peer, device_id_type=MESH)


def own_source(s, unit, half=None):
    rb, cb = unit_shape(s, unit)
    if unit <= OUT:
        piece, start = s.pieces[unit], 0
    else:
        part, which = divmod(unit - 4, 3)
        if which < 2:
            return block(s, unit, s.row, s.col, half)
        piece, start = s.pieces[6], part * rb
    if half is None:
        return piece.at[start : start + rb, :]
    return piece.at[start + half * (rb // 2) : start + (half + 1) * (rb // 2), :]


def own_copies(s, unit):
    rb, cb = unit_shape(s, unit)
    own = block(s, unit, s.row, s.col)
    part, which = divmod(unit - 4, 3)
    if unit <= OUT or which == 2:
        return [pltpu.make_async_copy(own_source(s, unit), own, s.own_sems.at[unit, 0])]
    piece, half = s.pieces[4 + which], cb // 2
    size = s.hidden // 4
    offset = part * (s.hidden // CHUNKS)
    mine = (s.wg, s.wu)[which]
    return [
        pltpu.make_async_copy(
            piece.at[:, i * size + part * half : i * size + (part + 1) * half],
            mine.at[span(s.row * rb, rb), span(offset + s.col * cb + i * half, half)], s.own_sems.at[unit, i])
        for i in range(2)]


def ag_copy(s, unit, kind):
    b = functools.partial(block, s, unit)
    if kind < 3:
        return send(s, "ag", unit, kind, own_source(s, unit), b(s.row, s.col), (s.to_x, s.to_y, s.to_p)[kind])
    there, peer = [
        (b(s.row_x, s.col, 0), s.to_y), (b(s.row, s.col_y, 1), s.to_x), (b(s.row_x, s.col), s.to_p), (b(s.row, s.col_y), s.to_p),
        (b(s.row_x, s.col_y, 0), s.to_p), (b(s.row_x, s.col_y, 1), s.to_p)][kind - 3]
    return send(s, "ag", unit, kind, there, there, peer)


def ag_arrive(s, unit, kind):
    b = functools.partial(block, s, unit)
    where = [
        b(s.row_x, s.col), b(s.row, s.col_y), b(s.row_p, s.col), b(s.row_x, s.col_y, 0), b(s.row_x, s.col_y, 1),
        b(s.row_px, s.col), b(s.row_p, s.col_y), b(s.row_px, s.col_y, 0), b(s.row_px, s.col_y, 1)][kind]
    send(s, "ag", unit, kind, where, where, s.to_p).wait_recv()


def shuffled(unit):
    return unit > OUT and (unit - 4) % 3 < 2


def own_wait(s, unit):
    for copy in own_copies(s, unit):
        copy.wait()


def ag_open(s, unit):
    if shuffled(unit):
        own_wait(s, unit)
    for kind in range(3):
        ag_copy(s, unit, kind).start()


def ag_relay(s, unit):
    for kind in range(2):
        ag_arrive(s, unit, kind)
        ag_copy(s, unit, kind + 3).start()
        ag_copy(s, unit, kind + 5).start()


def ag_corner(s, unit):
    for kind in (3, 4):
        ag_arrive(s, unit, kind)
        ag_copy(s, unit, kind + 4).start()


def ag_near(s, unit):
    if not shuffled(unit):
        own_wait(s, unit)
    for kind in (2, 5):
        ag_arrive(s, unit, kind)


def ag_far(s, unit):
    for kind in (6, 7, 8):
        ag_arrive(s, unit, kind)


def ag_close(s, unit):
    ag_near(s, unit)
    ag_far(s, unit)


def ag_sent(s, unit):
    for kind in range(9):
        ag_copy(s, unit, kind).wait_send()


def swap_copy(s, family, i, peer, slot):
    slots = getattr(s, family + "_slots")
    return pltpu.make_async_remote_copy(
        src_ref=getattr(s, family + "_from"), dst_ref=slots.at[slot], send_sem=getattr(s, family + "_send").at[i],
        recv_sem=getattr(s, family + "_recv").at[slot], device_id=peer, device_id_type=MESH)


def swap_open(s, family, peers, me):
    getattr(s, family + "_slots")[me] = getattr(s, family + "_from")[...]
    for i, peer in enumerate(peers):
        swap_copy(s, family, i, peer, me).start()


def swap_wait(s, family, peers, ids):
    for i, (peer, slot) in enumerate(zip(peers, ids)):
        copy = swap_copy(s, family, i, peer, slot)
        copy.wait_recv()
        copy.wait_send()


def swap_close(s, family, peers, ids):
    swap_wait(s, family, peers, ids)
    slots = getattr(s, family + "_slots")
    total = slots[0]
    for i in range(1, len(ids) + 1):
        total = total + slots[i]
    return total


def small_rows(s):
    return 2 * (s.width // 128) + s.heads


def small_pack(s, table):
    wide = s.width // 128
    for i in range(2):
        for j in range(wide):
            s.near_from[i * wide + j : i * wide + j + 1, :] = s.small[i : i + 1, 128 * j : 128 * (j + 1)]
    s.near_from[2 * wide : 2 * wide + s.heads, 0 : s.buckets] = table


DIRECT = 2


def quarter(s, unit, row, index):
    rb, cb = unit_shape(s, unit)
    return s.p.at[span(unit * (4 * s.micro * s.length) + s.col * s.width + row * rb + index * (rb // 4), rb // 4), 0:cb]


def rs_copy(s, unit, kind):
    b = functools.partial(block, s, unit, grad=True)
    n = lambda name: getattr(s, f"{name}{unit}")
    low = s.z - 1
    if unit == DIRECT and kind >= 10:
        peer, there = s.stack[(kind - 10) % 3], s.stack_ids[(kind - 10) % 3]
        if kind < 13:
            return send(s, "rs", unit, kind, quarter(s, unit, s.row, there), n("zq").at[kind - 10], peer)
        return send(s, "rs", unit, kind, quarter(s, unit, s.row, s.z), quarter(s, unit, s.row_p, s.z), peer)
    if kind < 4:
        x, col = divmod(kind, 2)
        return send(s, "rs", unit, kind, b(2 * x + 1 - s.core, col), n("pr").at[x, col], s.to_p)
    if kind < 6:
        return send(s, "rs", unit, kind, b(s.row_x, kind - 4, 0), n("xa").at[kind - 4], s.to_x)
    if kind < 8:
        return send(s, "rs", unit, kind, b(2 * (kind - 6) + s.core, s.col_y, 1), n("yb").at[kind - 6], s.to_y)
    up, side = (s.z_out, s.row, s.col), (3 - s.z, s.row, s.col)
    src, dst, peer = [
        lambda: (b(s.row, s.col_y, 0), n("ya"), s.to_y),
        lambda: (b(s.row_x, s.col, 1), n("xb"), s.to_x),
        lambda: (b(s.row, s.col), n("zi"), (s.z_in, s.row, s.col)),
        lambda: (b(s.row, s.col, 1 - low), n("zx"), side),
        lambda: (b(s.row, s.col, low), b(s.row_p, s.col, low), side),
        lambda: (b(s.row, s.col, low), b(s.row_p, s.col, low), up),
        lambda: (b(s.row_p, s.col, 1 - low), b(s.row_p, s.col, 1 - low), up)][kind - 8]()
    return send(s, "rs", unit, kind, src, dst, peer)


def rs_arrive(s, unit, kind):
    b = functools.partial(block, s, unit, grad=True)
    n = lambda name: getattr(s, f"{name}{unit}")
    if unit == DIRECT and kind >= 13:
        where = quarter(s, unit, s.row_p, lax.rem(s.z + 4 - (kind - 12), 4))
    elif unit == DIRECT and kind >= 10:
        where = n("zq").at[kind - 10]
    elif kind < 4:
        where = n("pr").at[kind // 2, kind % 2]
    elif kind < 6:
        where = n("xa").at[kind - 4]
    elif kind < 8:
        where = n("yb").at[kind - 6]
    elif kind < 12:
        where = n(("ya", "xb", "zi", "zx")[kind - 8])
    else:
        where = b(s.row_p, s.col, (2 - s.z, s.z_in - 1, 2 - s.z_in)[kind - 12])
    send(s, "rs", unit, kind, where, where, s.to_p).wait_recv()
    return where


def add_into(target, source):
    rows = target.shape[0]
    step = 32 if rows % 32 == 0 else 16

    def body(i):
        r = rows_of(i, step)
        target[r, :] = target[r, :] + source[r, :]

    loop(rows // step, body)


def rs_1(s, unit):
    for kind in range(4):
        rs_copy(s, unit, kind).start()


def rs_2(s, unit):
    b = functools.partial(block, s, unit, grad=True)
    for kind in range(4):
        x, col = divmod(kind, 2)
        add_into(b(2 * x + s.core, col), rs_arrive(s, unit, kind))
    for kind in range(4, 8):
        rs_copy(s, unit, kind).start()


def rs_3(s, unit):
    b = functools.partial(block, s, unit, grad=True)
    for col in range(2):
        add_into(b(s.row, col, 0), rs_arrive(s, unit, 4 + col))
    rs_copy(s, unit, 8).start()
    for x in range(2):
        add_into(b(2 * x + s.core, s.col, 1), rs_arrive(s, unit, 6 + x))
    rs_copy(s, unit, 9).start()


def rs_4(s, unit):
    b = functools.partial(block, s, unit, grad=True)
    for half in range(2):
        add_into(b(s.row, s.col, half), rs_arrive(s, unit, 8 + half))
    for kind in range(10):
        rs_copy(s, unit, kind).wait_send()
    if unit == DIRECT:
        for kind in (11, 10, 12):
            rs_copy(s, unit, kind).start()
        return

    @pl.when(s.outer)
    def _():
        rs_copy(s, unit, 10).start()


def rs_5(s, unit):
    if unit == DIRECT:
        mine = quarter(s, unit, s.row, s.z)
        for kind in (10, 12, 11):
            add_into(mine, rs_arrive(s, unit, kind))
        for kind in (14, 13, 15):
            rs_copy(s, unit, kind).start()
        quarter(s, unit, s.row_p, s.z)[...] = mine[...]
        return

    @pl.when(s.inner)
    def _():
        add_into(block(s, unit, s.row, s.col, grad=True), rs_arrive(s, unit, 10))
        rs_copy(s, unit, 11).start()


def rs_6(s, unit):
    if unit == DIRECT:
        for kind in (13, 15, 14):
            rs_arrive(s, unit, kind)
        for kind in range(10, 16):
            rs_copy(s, unit, kind).wait_send()
        rs_out(s, unit).start()
        return

    @pl.when(s.inner)
    def _():
        mine = block(s, unit, s.row, s.col, s.z - 1, grad=True)
        add_into(mine, rs_arrive(s, unit, 11))
        rs_copy(s, unit, 12).start()
        rs_copy(s, unit, 13).start()
        done = block(s, unit, s.row_p, s.col, s.z - 1, grad=True)
        done[...] = mine[...]


def rs_7(s, unit):
    @pl.when(s.inner)
    def _():
        rs_arrive(s, unit, 12)
        rs_copy(s, unit, 14).start()
        for kind in (11, 12, 13):
            rs_copy(s, unit, kind).wait_send()

    @pl.when(s.outer)
    def _():
        rs_arrive(s, unit, 13)
        rs_copy(s, unit, 10).wait_send()


def rs_8(s, unit):
    @pl.when(s.inner)
    def _():
        rs_copy(s, unit, 14).wait_send()

    @pl.when(s.outer)
    def _():
        rs_arrive(s, unit, 14)

    rs_out(s, unit).start()


def rs_out(s, unit):
    return pltpu.make_async_copy(block(s, unit, s.row_p, s.col, grad=True), s.unit_out[unit], s.out_sems.at[unit])


PLAN = {
    ("start", 0): (("o", 0), ("o", 1), ("o", 2)),
    ("project", 0): (("r", 0), ("n", 0), ("o", 3)),
    ("project", 1): (("r", 1), ("n", 1)),
    ("project", 2): (("o", 4), ("r", 2), ("n", 2), ("c", 0)),
    ("attend", 0): (("o", 5),),
    ("attend", 1): (("r", 3),),
    ("attend", 2): (("c", 1), ("o", 6)),
    ("attend", 4): (("r", 4), ("o", 7)),
    ("attend", 5): (("c", 2),),
    ("project", 3): (("r", 5), ("f", 0), ("o", 8)),
    ("project", 4): (("c", 3), ("f", 1)),
    ("project", 5): (("o", 9), ("r", 6), ("f", 2)),
    ("attend", 6): (("c", 4), ("o", 10)),
    ("attend", 7): (("r", 7),),
    ("attend", 8): (("c", 5),),
    ("attend", 9): (("o", 11),),
    ("attend", 10): (("r", 8),),
    ("attend", 11): (("r", 9),),
    ("feed_in", 0): (("c", 6), ("o", 12), ("x", 3)),
    ("feed", 0): (("c", 7), ("r", 10), ("r", 11), ("o", 13), ("x", 4), ("x", 5), ("x", 6)),
    ("feed", 1): (("c", 8), ("c", 9), ("o", 14), ("o", 15), ("r", 12)),
    ("feed", 4): (("c", 10), ("c", 11)),
    ("feed", 5): (("r", 13), ("r", 14), (1, 4), (1, 5), (1, 6), ("x", 7), ("x", 8), ("x", 9)),
    ("feed", 6): (("c", 12), ("r", 15), (2, 4)),
    ("feed", 9): (("c", 13), ("c", 14), (2, 5), (2, 6)),
    ("feed", 10): (("c", 15), (3, 4), (1, 7), (1, 8), (1, 9), ("x", 10), ("x", 11), ("x", 12)),
    ("feed", 11): ((3, 5), (2, 7), (2, 8), (3, 6)),
    ("feed", 14): ((4, 4), (2, 9), (4, 5)),
    ("feed", 15): ((3, 7), ("x", 13), ("x", 14), ("x", 15)),
    ("feed", 16): ((5, 4), (4, 6), (3, 8), (3, 9), (5, 5)),
    ("feed", 19): ((4, 7),),
    ("close", 0): ((6, 4), (6, 5), (5, 6), (4, 8), (4, 9)),
    ("outback", 0): ((5, 7), (1, 10), (1, 11), (1, 12), (1, 13), (1, 14), (1, 15)),
    ("outback", 1): ((7, 4),),
    ("outback", 2): ((7, 5),),
    ("outback", 3): ((6, 6), (5, 8), (2, 10), (2, 11), (6, 7)),
    ("outgrad", 0): ((5, 9), (2, 12), (2, 13), (8, 4)),
    ("outgrad", 1): ((1, 3), (8, 5), (7, 6), (2, 14), (2, 15)),
    ("back", 1): ((7, 7), (6, 8), (3, 10)),
    ("back", 2): ((6, 9), (3, 11), (2, 3), (8, 6)),
    ("back", 3): ((3, 12),),
    ("chunk", 0): ((1, 0), (8, 7), (7, 8), (7, 9), (3, 13), (3, 14)),
    ("back", 5): ((3, 15),),
    ("back", 6): ((4, 10), (4, 11), (2, 0)),
    ("back", 7): ((8, 8), (8, 9)),
    ("chunk", 1): ((1, 1), (4, 12), (4, 13), (3, 3), (5, 10), (4, 14)),
    ("back", 9): ((5, 11), (4, 15)),
    ("back", 10): ((2, 1),),
    ("back", 11): ((6, 10), (5, 12), (4, 3), (3, 0)),
    ("chunk", 2): ((1, 2), (6, 11), (5, 13), (5, 14), (7, 10)),
    ("input", 1): ((3, 1), (6, 12), (5, 15)),
    ("input", 2): ((4, 0), (2, 2)),
    ("input", 3): ((7, 11), (5, 3), (8, 10), (6, 13)),
    ("input", 4): ((6, 14), (4, 1), (7, 12)),
    ("tail", 0): ((6, 15), (8, 11), (5, 0), (3, 2), (6, 3), (7, 13), (7, 14), (8, 12), (7, 15), (5, 1), (4, 2), (6, 0), (8, 13), (7, 3), (8, 14), (6, 1), (8, 15), (8, 3), (5, 2), (7, 0), (7, 1), (8, 0), (8, 1), (6, 2)),
}


NAMES = ("wq", "wk", "wv", "wo", "wg", "wu", "wd")
UNITS = OUT + 1 + 3 * CHUNKS
EARLY = tuple(range(4, 10))
ACTS = {"o": ag_open, "r": ag_relay, "c": ag_corner, "x": ag_close, "n": ag_near, "f": ag_far, 1: rs_1, 2: rs_2, 3: rs_3, 4: rs_4, 5: rs_5, 6: rs_6, 7: rs_7, 8: rs_8}


def act_all(s, todo):
    for act, unit in todo if s.comm else ():
        ACTS[act](s, unit)


def hook(s, phase, index):
    entries = sorted((number, todo) for (name, number), todo in PLAN.items() if name == phase)
    if not s.comm:
        return
    if isinstance(index, int):
        for number, todo in entries:
            if number == index:
                act_all(s, todo)
        return

    def pick(some):
        if len(some) == 1:
            pl.when(index == some[0][0])(functools.partial(act_all, s, some[0][1]))
        elif some:
            middle = len(some) // 2
            pl.when(index < some[middle][0])(lambda: pick(some[:middle]))
            pl.when(index >= some[middle][0])(lambda: pick(some[middle:]))

    pick(entries)


def gains_in(s):
    for i, gain in enumerate((s.gain_one, s.gain_two)):
        if s.comm:
            s.gain_from[i : i + 1, 0 : gain.shape[1]] = gain[...].astype(F32)
        else:
            s.gain[i : i + 1, :] = gain[...].astype(F32)


def gains_spread(s):
    swap_wait(s, "gain", s.plane, s.plane_ids)
    count = s.gain_one.shape[1]
    wide = (128, s.width)
    lane, spot = lax.broadcasted_iota(jnp.int32, wide, 0), lax.broadcasted_iota(jnp.int32, wide, 1)
    total = None
    for i in range(8):
        part = nn(s.gain_slots[i].astype(BF), jnp.logical_and(spot == lane + count * i, lane < count).astype(BF))
        total = part if total is None else total + part
    s.gain[...] = total


def layer(cfg, *refs):
    s = types.SimpleNamespace(**cfg)
    for name, ref in zip(cfg["names"], refs):
        setattr(s, name, ref)
    s.pieces = [getattr(s, n + "_in") for n in NAMES]
    comm = s.comm
    s.hook = functools.partial(hook, s)
    load_x = pltpu.make_async_copy(s.x_in, s.x, s.io_sems.at[0])
    load_c = pltpu.make_async_copy(s.c_in, s.c, s.io_sems.at[1])
    tiny_loads = [
        pltpu.make_async_copy(getattr(s, name + "_in"), getattr(s, name), s.tiny_sems.at[i])
        for i, name in enumerate(("gain_one", "gain_two", "seg", "bucket", "table"))]
    for copy in tiny_loads + [load_x, load_c]:
        copy.start()
    Q, K, V, O = range(4)
    if comm:
        place(s)
        s.unit_out = [getattr(s, f"unit{u}_out") for u in range(UNITS)]
        greet(s)
        for unit in range(UNITS):
            for copy in own_copies(s, unit):
                copy.start()
        s.hook("start", 0)
        for copy in tiny_loads:
            copy.wait()
        s.gain_from[...] = jnp.zeros_like(s.gain_from)
        gains_in(s)
        swap_open(s, "gain", s.plane, s.me)
    else:
        weights = [pltpu.make_async_copy(piece, getattr(s, n), s.load_sems.at[i]) for i, (n, piece) in enumerate(zip(NAMES, s.pieces))]
        for copy in weights:
            copy.start()
        for copy in tiny_loads:
            copy.wait()
        gains_in(s)
    s.small[...] = jnp.zeros_like(s.small)
    s.near_from[...] = jnp.zeros_like(s.near_from)
    offset_rows(s)
    tw, wt = (s.tokens, s.width), (s.width, s.tokens)
    vm = pltpu.VMEM

    def attention(a, mask, toep):
        s.a, s.mask, s.toep = a, mask, toep
        masks(s)
        load_x.wait()
        if comm:
            gains_spread(s)
        else:
            for copy in weights:
                copy.wait()
        norm_in(s, 128)
        pairs = s.heads // 4
        for part in range(2):
            side = (s.col if part == 0 else s.col_y) if comm else part
            for w in (Q, K, V):
                s.hook("project", 3 * part + w)
                project(s, w, side, 256)
            loop(pairs, functools.partial(attend_pair, s, side, 2 * pairs * part))

    skew = vm((128, 2 * s.length), F32)
    pl.run_scoped(attention, vm(tw, BF), vm((s.micro, s.length, s.length), F32), skew)
    s.n2t = s.vt

    def feed(act, mid, y, ct):
        s.mid, s.y, s.ct = mid, y, ct
        s.hid, s.dg, s.du = (act.at[:, i * s.ft : (i + 1) * s.ft] for i in range(3))
        load_c.wait()
        s.hook("feed_in", 0)
        out_project(s, 256)

        def step(t):
            ffn_rows(s, t, s.ft, s.rb)
            s.hook("feed", 5 * t + 4)
            if comm:
                for part in range(CHUNKS):

                    @pl.when(t == part)
                    def _():
                        for which in range(3):
                            ag_sent(s, ffn_unit(part, which))

            ffn_grads(s, t, s.ft, s.gb)

        loop(s.hidden // s.ft, step)
        s.hook("close", 0)
        ffn_close(s, 128)

    pl.run_scoped(feed, vm((s.tokens, 3 * s.ft), BF), vm(tw, F32), vm(tw, F32), vm(wt, BF))
    put_y = pltpu.make_async_copy(s.c, s.y_out, s.io_sems.at[0])
    put_x = pltpu.make_async_copy(s.x, s.gi_out, s.io_sems.at[1])
    put_y.start()

    def back(toep, ds, goff, *bufs):
        s.toep, s.ds, s.goff = toep, ds, goff
        s.do, s.dot = s.c, s.vt
        for name, ref in zip(s.rs_names, bufs):
            setattr(s, name, ref)
        if comm:
            for peer in [s.to_p, s.to_x, s.to_y] + s.stack:
                pl.semaphore_signal(s.ready, inc=1, device_id=peer, device_id_type=MESH)
            pl.semaphore_wait(s.ready, 6)
        put_y.wait()
        out_backward(s, 256)
        s.hook("outgrad", 0)
        if comm:
            for unit in range(4):
                ag_sent(s, unit)
        out_grads(s, 256)
        s.hook("outgrad", 1)

        def step(i):
            attend_back(s, i)

            @pl.when(lax.rem(i, 2) == 1)
            def _():
                chunk_grads(s, lax.div(i, 2), 384)
                s.hook("chunk", lax.div(i, 2))

        loop(s.heads // 2, step)
        s.hook("input", 0)
        table = table_grad(s)
        qkv_back_input(s, 256)
        put_x.start()
        small_pack(s, table)
        if comm:
            swap_open(s, "near", s.plane, s.me)
            s.far_from[...] = swap_close(s, "near", s.plane, s.plane_ids)
            swap_open(s, "far", s.stack, s.z)
            s.hook("tail", 0)
            s.small_sum[...] = swap_close(s, "far", s.stack, s.stack_ids)
            for unit in range(UNITS):
                rs_out(s, unit).wait()
        else:
            s.small_sum[...] = s.near_from[...]
            outs = [pltpu.make_async_copy(getattr(s, n), getattr(s, n + "_out"), s.load_sems.at[i + 3]) for i, n in enumerate(NAMES[3:])]
            for copy in outs:
                copy.start()
            for copy in outs:
                copy.wait()
            half = s.heads // 4
            for w, n in enumerate(NAMES[:3]):
                for pair in range(s.heads // 2):
                    copy = pltpu.make_async_copy(
                        s.p.at[slab(s, pair % half, pair // half), 128 * w : 128 * (w + 1)],
                        getattr(s, n + "_out").at[:, 128 * pair : 128 * (pair + 1)], s.load_sems.at[w])
                    copy.start()
                    copy.wait()

    pl.run_scoped(
        back, skew, vm((s.length, s.length), BF), vm((8, s.heads, 2 * s.length), F32), *[vm(shape, BF) for shape in s.rs_shapes])
    put_small = pltpu.make_async_copy(s.small_sum, s.small_out, s.tiny_sems.at[5])
    put_small.start()
    put_x.wait()
    put_small.wait()


def call_layer(comm, x, c, weights, gains, seg, bucket, table, full):
    tokens, width = x.shape
    micro, length = seg.shape
    heads, buckets = table.shape
    hidden = full[4][1]
    ft, vm, sem = 512, pltpu.VMEM, pltpu.SemaphoreType.DMA
    tw, wt, tiny = (tokens, width), (width, tokens), (2 * (width // 128) + heads, 128)
    s = types.SimpleNamespace(
        comm=comm, tokens=tokens, width=width, micro=micro, length=length, hidden=hidden, heads=heads, buckets=buckets, ft=ft, gb=768, rb=512,
        rs_names=[], rs_shapes=[])
    scratch = dict(
        x=vm(tw, BF), c=vm(tw, BF), **{n: vm(shape, BF) for n, shape in zip(NAMES, full)},
        n1t=vm(wt, BF), q=vm(tw, BF), k=vm(tw, BF), v=vm(tw, BF), kt=vm(wt, BF), vt=vm(wt, BF), ot=vm(wt, BF),
        dn=vm(tw, F32), p=vm((heads * micro * length, length), BF),
        offs=vm((heads, 2 * length), F32), gain=vm((8, width), F32), small=vm((2, width), F32), near_from=vm(tiny, F32),
        turned=vm((1, 2 * length), jnp.int32), io_sems=sem((2,)), load_sems=sem((7,)), out_sems=sem((UNITS,)),
    )
    out_shape = [(tw, BF)] * 2
    if comm:
        scratch.update(
            gain_from=vm((8, 128), F32), far_from=vm(tiny, F32),
            gain_slots=vm((8, 8, 128), F32), near_slots=vm((8, *tiny), F32), far_slots=vm((4, *tiny), F32),
            ag_send=sem((UNITS, 9)), ag_recv=sem((UNITS, 9)), own_sems=sem((UNITS, 2)), rs_send=sem((UNITS, 16)), rs_recv=sem((UNITS, 16)),
            gain_send=sem((7,)), gain_recv=sem((8,)), near_send=sem((7,)), near_recv=sem((8,)), far_send=sem((3,)), far_recv=sem((4,)),
            ready=pltpu.SemaphoreType.REGULAR,
        )
        for unit in range(UNITS):
            rb, cb = unit_shape(s, unit)
            hb = rb // 2
            shapes = dict(pr=(2, 2, rb, cb), xa=(2, hb, cb), yb=(2, hb, cb), ya=(hb, cb), xb=(hb, cb), zi=(rb, cb), zx=(hb, cb))
            if unit == DIRECT:
                del shapes["zi"], shapes["zx"]
                shapes["zq"] = (3, rb // 4, cb)
            for name, shape in shapes.items():
                if unit in EARLY:
                    scratch[f"{name}{unit}"] = vm(shape, BF)
                else:
                    s.rs_names.append(f"{name}{unit}")
                    s.rs_shapes.append(shape)
            out_shape.append(((rb, cb), BF))
        grad_names = [f"unit{unit}_out" for unit in range(UNITS)]
    else:
        out_shape += [(shape, BF) for shape in full]
        grad_names = [n + "_out" for n in NAMES]
    tiny_ins = dict(gain_one=gains[0], gain_two=gains[1], seg=seg, bucket=bucket, table=table)
    for name, array in tiny_ins.items():
        scratch[name] = vm(array.shape, array.dtype)
    scratch.update(tiny_sems=sem((6,)), small_sum=vm(tiny, F32))
    ins = ["x_in", "c_in"] + [n + "_in" for n in NAMES] + [name + "_in" for name in tiny_ins]
    outs = ["y_out", "gi_out"] + grad_names + ["small_out"]
    out_shape.append((tiny, F32))
    names = ins + outs + list(scratch)
    far = pl.BlockSpec(memory_space=pl.ANY)
    params = dict(vmem_limit_bytes=67043328)
    if comm:
        params.update(collective_id=0, has_side_effects=True)

    def body(*refs):
        cfg = dict(vars(s), names=names)
        layer(cfg, *refs)

    return pl.pallas_call(
        body, out_shape=[jax.ShapeDtypeStruct(*o) for o in out_shape],
        in_specs=[far] * len(ins), out_specs=[far] * len(outs), scratch_shapes=list(scratch.values()),
        compiler_params=pltpu.CompilerParams(**params),
    )(x, c, *weights, *gains, seg, bucket, table)


def finish_kernel(cfg, *refs):
    s = types.SimpleNamespace(**cfg)
    srcs, outs = refs[: 3 + UNITS], refs[3 + UNITS : 3 + UNITS + 12]
    bufs = refs[15 + UNITS : 15 + 3 + 2 * UNITS]
    wide, tiny, (in_sems, out_sems) = refs[18 + 2 * UNITS : -5], refs[-5:-2], refs[-2:]
    loads = [pltpu.make_async_copy(src, buf, in_sems.at[i]) for i, (src, buf) in enumerate(zip(srcs, bufs))]
    for i in [len(loads) - 1] + list(range(2, len(loads) - 1)) + [0, 1]:
        loads[i].start()
    row, col = lax.axis_index("row"), lax.axis_index("col")
    y, gi, gain_one, gq, gk, gv, go, table, gain_two, gg, gu, gd = outs
    small, units = bufs[-1], bufs[2:-1]
    stores = []

    def leave(buf, out):
        stores.append(pltpu.make_async_copy(buf, out, out_sems.at[len(stores)]))
        stores[-1].start()

    loads[-1].wait()
    rows = s.width // 128
    at = lax.rem(s.width - s.gain_count * (2 * row + col), s.width)
    for i, out in enumerate((gain_one, gain_two)):
        full = jnp.concatenate([small[i * rows + j : i * rows + j + 1, :] for j in range(rows)], axis=1)
        tiny[i][...] = pltpu.roll(jnp.broadcast_to(full, (8, s.width)), at, 1)[0:1, 0 : s.gain_count]
        leave(tiny[i], out)
    tiny[2][...] = small[2 * rows : 2 * rows + s.heads, 0 : s.buckets]
    leave(tiny[2], table)
    wq, wk, wv, wo, wg, wu, wd = wide
    for unit in range(3):
        loads[2 + unit].wait()
        for w, buf in enumerate((wq, wk, wv)):
            buf[:, 128 * unit : 128 * (unit + 1)] = units[unit][:, 128 * w : 128 * (w + 1)].astype(F32)
    for buf, out in ((wq, gq), (wk, gk), (wv, gv)):
        leave(buf, out)
    loads[2 + OUT].wait()
    wo[...] = units[OUT][...].astype(F32)
    leave(wo, go)
    for which, buf, out in ((0, wg, gg), (1, wu, gu), (2, wd, gd)):
        for part in range(CHUNKS):
            unit = ffn_unit(part, which)
            loads[2 + unit].wait()
            rows, cols = units[unit].shape
            if which == 2:
                buf[part * rows : (part + 1) * rows, :] = units[unit][...].astype(F32)
            else:
                size = buf.shape[1] // 2
                for i in range(2):
                    at = i * size + part * (cols // 2)
                    buf[:, at : at + cols // 2] = units[unit][:, i * (cols // 2) : (i + 1) * (cols // 2)].astype(F32)
        leave(buf, out)
    for i, out in enumerate((y, gi)):
        loads[i].wait()
        leave(bufs[i], out)
    for copy in stores:
        copy.wait()


def finish(arrays, gain_count, heads, buckets, blocks):
    vm, sh = pltpu.VMEM, jax.ShapeDtypeStruct
    far = pl.BlockSpec(memory_space=pl.ANY)
    y, gi = arrays[:2]
    b = [sh(shape, F32) for shape in blocks]
    gain = sh((1, gain_count), F32)
    cfg = dict(width=y.shape[1], gain_count=gain_count, heads=heads, buckets=buckets)
    return pl.pallas_call(
        functools.partial(finish_kernel, cfg),
        out_shape=[sh(y.shape, BF), sh(gi.shape, BF), gain, *b[:4], sh((heads, buckets), F32), gain, *b[4:]],
        in_specs=[far] * len(arrays), out_specs=[far] * 12,
        scratch_shapes=[vm(a.shape, a.dtype) for a in arrays] + [vm(shape, F32) for shape in blocks]
        + [vm(gain.shape, F32)] * 2 + [vm((heads, buckets), F32)]
        + [pltpu.SemaphoreType.DMA((len(arrays),)), pltpu.SemaphoreType.DMA((12,))],
        compiler_params=pltpu.CompilerParams(vmem_limit_bytes=67043328),
    )(*arrays)


def open_block(gathered, row_count, column_count):
    _, rows, columns = gathered.shape
    grid = gathered.reshape(row_count, column_count, rows, columns).transpose(0, 2, 1, 3)
    return grid.reshape(row_count * rows, column_count * columns)


def close_block(full, row_count, column_count):
    rows, columns = full.shape[0] // row_count, full.shape[1] // column_count
    grid = full.reshape(row_count, rows, column_count, columns).transpose(0, 2, 1, 3)
    return grid.reshape(row_count * column_count, rows, columns)


def shards(block_input, segment_ids, bucket, gain_attn, w_query, w_key, w_value, w_out, bias_table, gain_ffn, w_gate, w_up, w_down, cotangent):
    row_count, column_count = lax.axis_size("row"), lax.axis_size("col")
    micro, length, width = block_input.shape
    tokens, gain_count = micro * length, gain_attn.shape[0]
    buckets, heads = bias_table.shape
    pieces = [w_query, w_key, w_value, w_out, w_gate, w_up, w_down]
    full = [(p.shape[0] * row_count, p.shape[1] * column_count) for p in pieces]
    fits = row_count == 4 and column_count == 2 and lax.axis_size("dp") == 4
    x, c = block_input.reshape(tokens, width), cotangent.reshape(tokens, width)
    gains = [gain_attn[None], gain_ffn[None]]
    plane = ("row", "col")
    if fits:
        out = call_layer(True, x, c, pieces, gains, segment_ids, bucket[None], bias_table.T, full)
        y, gi, one, gq, gk, gv, go, table, two, gg, gu, gd = finish(
            out, gain_count, heads, buckets, [p.shape for p in pieces])
        return y.reshape(block_input.shape), gi.reshape(block_input.shape), one[0], gq, gk, gv, go, table.T, two[0], gg, gu, gd
    gains = [lax.all_gather(g, plane, axis=1, tiled=True) for g in gains]
    weights = [open_block(lax.all_gather(p[None], plane, axis=0, tiled=True), row_count, column_count) for p in pieces]
    out = call_layer(False, x, c, weights, gains, segment_ids, bucket[None], bias_table.T, full)
    y, gi, grads, small = out[0], out[1], out[2:9], out[9]
    small = lax.psum(small, ("dp",) + plane)
    grads = [lax.psum_scatter(close_block(g, row_count, column_count), plane, scatter_dimension=0, tiled=True)[0] for g in grads]
    gq, gk, gv, go, gg, gu, gd = (lax.psum(g, "dp").astype(F32) for g in grads)
    mine = (lax.axis_index("row") * column_count + lax.axis_index("col")) * gain_count
    one, two = (lax.dynamic_slice(small[i * (width // 128) : (i + 1) * (width // 128)].reshape(-1), (mine,), (gain_count,)) for i in range(2))
    table = small[2 * (width // 128) :, :buckets].T
    return y.reshape(block_input.shape), gi.reshape(block_input.shape), one, gq, gk, gv, go, table, two, gg, gu, gd


def solution(mesh):
    whole = P(None, ("dp", "row", "col"), None)
    split, gain = P("row", "col"), P(("row", "col"))
    return jax.shard_map(
        shards, mesh=mesh,
        in_specs=(whole, P(None, ("dp", "row", "col")), P(), gain, split, split, split, split, P(), gain, split, split, split, whole),
        out_specs=(whole, whole, gain, split, split, split, split, P(), gain, split, split, split),
        check_vma=False)
```

```python
import functools
import types

import jax
import jax.numpy as jnp
from jax import lax
from jax.experimental import pallas as pl
from jax.experimental.pallas import tpu as pltpu
from jax.sharding import PartitionSpec as P

F32 = jnp.float32
BF = jnp.bfloat16
EPSILON = 1e-06
NEGATIVE = -1e30
PRECISE = lax.Precision.HIGHEST
MESH = pl.DeviceIdType.MESH
CHUNKS = 4
GELU_0 = 0.7978845608028654
GELU_1 = 0.044715


def contract(left, right, dims, **more):
    return lax.dot_general(left, right, ((dims[:1], dims[1:]), ((), ())), preferred_element_type=F32, **more)


def nn(left, right):
    return contract(left, right, (1, 0))


def nt(left, right):
    return contract(left, right, (1, 1))


def rows_of(index, size):
    return pl.ds(pl.multiple_of(index * size, size), size)


def loop(count, body):
    lax.fori_loop(0, count, lambda index, carry: (body(index), carry)[1], 0)


def bucket_classes(s):
    return (s.turned[...] == lax.broadcasted_iota(jnp.int32, (s.buckets, 2 * s.length), 0)).astype(F32)


def offset_rows(s):
    twice = 2 * s.length
    s.turned[...] = jnp.full((1, twice), -1, jnp.int32)
    s.turned[:, 0 : twice - 1] = s.bucket[...]
    flip = (lax.broadcasted_iota(jnp.int32, (128, 128), 0) + lax.broadcasted_iota(jnp.int32, (128, 128), 1) == 127).astype(BF)
    parts = [nn(s.turned[:, i : i + 128].astype(F32).astype(BF), flip) for i in range(0, twice, 128)]
    turned = jnp.concatenate(parts[::-1], axis=1)
    s.turned[...] = pltpu.roll(turned, twice - 1, 1).astype(jnp.int32)
    s.offs[...] = contract(s.table[...], bucket_classes(s), (1, 0), precision=PRECISE)


def masks(s):
    for m in range(s.micro):
        row = s.seg[m : m + 1, :].astype(F32)
        column = jnp.broadcast_to(row, (128, s.length)).T
        for i in range(0, s.length, 128):
            s.mask[m, :, i : i + 128] = jnp.where(column == row[:, i : i + 128], 0.0, NEGATIVE)


def norm_in(s, rb):
    def body(i):
        r = rows_of(i, rb)
        x = s.x[r, :].astype(F32)
        scale = lax.rsqrt(jnp.mean(x * x, axis=-1, keepdims=True) + EPSILON)
        n = (x * scale * s.gain[0:1, :]).astype(BF)
        s.a[r, :] = n
        s.n1t[:, r] = n.T

    loop(s.tokens // rb, body)


def spot(s, pair):
    half = s.heads // 4
    return 2 * (pair % half) + pair // half


def project(s, which, side, rb):
    weight, out, out_t = ((s.wq, s.q, None), (s.wk, s.k, s.kt), (s.wv, s.v, s.vt))[which]
    wide = s.width // 2
    cols = pl.ds(pl.multiple_of(side * wide, 128), wide)

    def body(i):
        r = rows_of(i, rb)
        p = nn(s.a[r, :], weight[:, cols]).astype(BF)
        for j in range(s.heads // 4):
            out[r, rows_of(2 * j + side, 128)] = p[:, 128 * j : 128 * (j + 1)]
        if out_t is not None:
            out_t[cols, r] = p.T

    loop(s.tokens // rb, body)


def half_masks(dtype):
    lane = lax.broadcasted_iota(jnp.int32, (1, 128), 1)
    return [(lane < 64).astype(dtype), (lane >= 64).astype(dtype)]


def attend_pair(s, side, late, j):
    length = s.length
    blocks = length // 128
    pair, i = (s.heads // 4) * side + j, 2 * j + side
    here = rows_of(i, 128)
    keep = half_masks(BF)
    for sub in range(2):
        s.hook("attend", late + 2 * j + sub)
        head = 2 * pair + sub
        hr = rows_of(head, 64)
        row = jnp.broadcast_to(s.offs[pl.ds(head, 1), :], (128, 2 * length))
        s.toep[...] = pltpu.roll(row, 2 * length - 127, 1, stride=1, stride_axis=0)
        for m in range(s.micro):
            mr = slice(m * length, (m + 1) * length)
            scores = nt(s.k[mr, here] * keep[sub], s.q[mr, here])
            bias = jnp.concatenate([s.toep[:, 128 * b : 128 * b + length] for b in reversed(range(blocks))], axis=0)
            scores = scores + bias + s.mask[m]
            e = jnp.exp(scores - jnp.max(scores, axis=0, keepdims=True))
            low = (e * (1.0 / jnp.sum(e, axis=0, keepdims=True))).astype(BF)
            s.p[rows_of((2 * i + sub) * s.micro + m, length), :] = low
            s.ot[hr, mr] = nn(s.vt[hr, mr], low).astype(BF)


def out_project(s, rb):
    def body(i):
        r = rows_of(i, rb)
        mid = s.x[r, :].astype(F32) + nn(s.ot[:, r].T, s.wo[...])
        s.mid[r, :] = mid
        s.y[r, :] = mid
        scale = lax.rsqrt(jnp.mean(mid * mid, axis=-1, keepdims=True) + EPSILON)
        n = (mid * scale * s.gain[1:2, :]).astype(BF)
        s.k[r, :] = n
        s.n2t[:, r] = n.T
        s.dn[r, :] = jnp.zeros_like(mid)
        s.ct[:, r] = s.c[r, :].T

    loop(s.tokens // rb, body)


def ffn_rows(s, tile, ft, rb):
    cols = rows_of(tile, ft)

    def forward(i):
        s.hook("feed", 5 * tile + i)
        r = rows_of(i, rb)
        n = s.k[r, :]
        gate = nn(n, s.wg[:, cols])
        up = nn(n, s.wu[:, cols])
        dh = nt(s.c[r, :], s.wd[cols, :])
        square = gate * gate
        t = jnp.tanh(gate * (GELU_0 + (GELU_0 * GELU_1) * square))
        half = 0.5 + 0.5 * t
        act = gate * half
        slope = half + (0.5 * gate) * (1.0 - t * t) * (GELU_0 + (3.0 * GELU_0 * GELU_1) * square)
        hid = (act * up).astype(BF)
        dg = (dh * up * slope).astype(BF)
        du = (dh * act).astype(BF)
        s.hid[r, :] = hid
        s.dg[r, :] = dg
        s.du[r, :] = du
        s.y[r, :] += nn(hid, s.wd[cols, :])
        s.dn[r, :] += nt(dg, s.wg[:, cols]) + nt(du, s.wu[:, cols])

    loop(s.tokens // rb, forward)


def ffn_grads(s, tile, ft, gb):
    cols = rows_of(tile, ft)

    def grads(i):
        r = rows_of(i, gb)
        s.wd[cols, r] = nn(s.ct[r, :], s.hid[...]).astype(BF).T
        s.wg[r, cols] = nn(s.n2t[r, :], s.dg[...]).astype(BF)
        s.wu[r, cols] = nn(s.n2t[r, :], s.du[...]).astype(BF)

    loop(s.width // gb, grads)


def ffn_close(s, rb):
    def body(i):
        r = rows_of(i, rb)
        mid = s.mid[r, :]
        dn = s.dn[r, :]
        scale = lax.rsqrt(jnp.mean(mid * mid, axis=-1, keepdims=True) + EPSILON)
        gdn = dn * s.gain[1:2, :]
        dot = jnp.mean(gdn * mid, axis=-1, keepdims=True)
        dmid = s.c[r, :].astype(F32) + scale * gdn - mid * (scale * scale * scale * dot)
        s.small[1:2, :] += jnp.sum(dn * mid * scale, axis=0, keepdims=True)
        s.dn[r, :] = dmid
        s.k[r, :] = dmid.astype(BF)
        s.c[r, :] = s.y[r, :].astype(BF)

    loop(s.tokens // rb, body)


def out_backward(s, rb):
    def body(i):
        s.hook("outback", i)
        r = rows_of(i, rb)
        d = nt(s.k[r, :], s.wo[...]).astype(BF)
        s.do[r, :] = d
        s.dot[:, r] = d.T

    loop(s.tokens // rb, body)


def out_grads(s, gb):
    def grads(i):
        r = rows_of(i, gb)
        s.wo[r, :] = nn(s.ot[r, :], s.k[...]).astype(BF)

    loop(s.width // gb, grads)


def attend_back(s, i):
    length = s.length
    blocks = length // 128
    pair = lax.div(i, 2) + (s.heads // 4) * lax.rem(i, 2)
    here, natural = rows_of(i, 128), rows_of(pair, 128)
    keep = half_masks(BF)
    left = lax.broadcasted_iota(jnp.int32, (1, 128), 1) < 64
    parts = {}
    for sub in range(2):
        s.hook("back", 2 * i + sub)
        head = 2 * pair + sub
        hr = rows_of(head, 64)
        for m in range(s.micro):
            mr = slice(m * length, (m + 1) * length)
            pr = rows_of((2 * i + sub) * s.micro + m, length)
            dp = nt(s.v[mr, here] * keep[sub], s.do[mr, natural])
            inner = jnp.sum(s.dot[hr, mr].astype(F32) * s.ot[hr, mr].astype(F32), axis=0, keepdims=True)
            ds = s.p[pr, :].astype(F32) * (dp - inner)
            if m == 0:
                s.toep[...] = jnp.zeros_like(s.toep)
            for j in range(blocks):
                at = 128 * (blocks - 1 - j)
                s.toep[:, at : at + length] += ds[128 * j : 128 * (j + 1), :]
            low = ds.astype(BF)
            s.ds[...] = low
            parts[sub, m, 2] = nn(s.kt[hr, mr], low)
            parts[sub, m, 0] = nn(s.ds[...], s.q[mr, here])
            parts[sub, m, 1] = nn(s.p[pr, :], s.do[mr, natural])
            if sub == 1:
                s.k[mr, here] = jnp.where(left, parts[0, m, 0], parts[1, m, 0]).astype(BF)
                s.v[mr, here] = jnp.where(left, parts[0, m, 1], parts[1, m, 1]).astype(BF)
                s.q[mr, here] = jnp.concatenate([parts[0, m, 2], parts[1, m, 2]], axis=0).astype(BF).T
        fold = s.toep[...]
        rows = 64
        while rows >= 8:
            fold = fold[:rows, :] + pltpu.roll(fold[rows:, :], 2 * length - rows, 1)
            rows //= 2
        for r in range(8):
            s.goff[r, pl.ds(head, 1), :] = fold[r : r + 1, :]


def slab(s, chunk, side):
    start = chunk * (4 * s.micro * s.length) + side * s.width
    return pl.ds(pl.multiple_of(start, 128), s.width)


def chunk_grads(s, chunk, gb):
    cols = rows_of(chunk, 256)

    def body(i):
        r = rows_of(i, gb)
        for w, grad in enumerate((s.q, s.k, s.v)):
            g = nn(s.n1t[r, :], grad[:, cols]).astype(BF)
            for side in range(2):
                start = chunk * (4 * s.micro * s.length) + side * s.width + i * gb
                s.p[pl.ds(pl.multiple_of(start, gb & -gb), gb), 128 * w : 128 * (w + 1)] = g[:, 128 * side : 128 * (side + 1)]

    loop(s.width // gb, body)


def table_grad(s):
    total = None
    for r in range(8):
        part = pltpu.roll(s.goff[r, :, :], 127 - r, 1)
        total = part if total is None else total + part
    return contract(total, bucket_classes(s), (1, 1), precision=PRECISE)


def qkv_back_input(s, rb):
    order = [spot(s, pair) for pair in range(s.heads // 2)]

    def body(i):
        s.hook("input", i + 1)
        r = rows_of(i, rb)
        dn = None
        for grad, weight in ((s.q, s.wq), (s.k, s.wk), (s.v, s.wv)):
            part = nt(jnp.concatenate([grad[r, 128 * at : 128 * (at + 1)] for at in order], axis=1), weight[...])
            dn = part if dn is None else dn + part
        x = s.x[r, :].astype(F32)
        scale = lax.rsqrt(jnp.mean(x * x, axis=-1, keepdims=True) + EPSILON)
        gdn = dn * s.gain[0:1, :]
        dot = jnp.mean(gdn * x, axis=-1, keepdims=True)
        s.small[0:1, :] += jnp.sum(dn * x * scale, axis=0, keepdims=True)
        s.x[r, :] = (s.dn[r, :] + scale * gdn - x * (scale * scale * scale * dot)).astype(BF)

    loop(s.tokens // rb, body)


OUT = 3


def ffn_unit(part, which):
    return 4 + 3 * part + which


def place(s):
    s.z, s.row, s.col = lax.axis_index("dp"), lax.axis_index("row"), lax.axis_index("col")
    s.core, s.xx = lax.rem(s.row, 2), lax.div(s.row, 2)
    s.row_p = 2 * s.xx + 1 - s.core
    s.row_x = 2 * (1 - s.xx) + s.core
    s.row_px = 2 * (1 - s.xx) + 1 - s.core
    s.col_y = 1 - s.col
    s.to_p, s.to_x = (s.z, s.row_p, s.col), (s.z, s.row_x, s.col)
    s.to_y, s.to_xy = (s.z, s.row, s.col_y), (s.z, s.row_x, s.col_y)
    s.me = 2 * s.row + s.col
    s.plane = [(s.z, lax.rem(s.row + (i // 2), 4), lax.rem(s.col + i % 2, 2)) for i in range(1, 8)]
    s.stack = [(lax.rem(s.z + i, 4), s.row, s.col) for i in range(1, 4)]
    s.plane_ids = [2 * row + col for _, row, col in s.plane]
    s.stack_ids = [z for z, _, _ in s.stack]
    s.inner = jnp.logical_and(s.z >= 1, s.z <= 2)
    s.outer = jnp.logical_not(s.inner)
    s.z_in, s.z_out = 1 + lax.div(s.z, 2), 3 * lax.div(s.z, 2)


def greet(s):
    barrier = pltpu.get_barrier_semaphore()
    for peer in s.plane + s.stack:
        pl.semaphore_signal(barrier, inc=1, device_id=peer, device_id_type=MESH)
    pl.semaphore_wait(barrier, len(s.plane) + len(s.stack))


def unit_shape(s, unit):
    rb, cb = s.width // 4, s.width // 2
    if unit <= OUT:
        return rb, cb
    part = s.hidden // CHUNKS
    return (part // 4, cb) if (unit - 4) % 3 == 2 else (rb, part // 2)


def span(start, size):
    return pl.ds(pl.multiple_of(start, size & -size), size)


def block(s, unit, row, col, half=None, grad=False):
    rb, cb = unit_shape(s, unit)
    size = rb if half is None else rb // 2
    down = row * rb + (0 if half is None else half * size)
    if unit < OUT and grad:
        return s.p.at[span(unit * (4 * s.micro * s.length) + col * s.width + down, size), 0:cb]
    if unit <= OUT:
        return (s.wq, s.wk, s.wv, s.wo)[unit].at[span(down, size), span(col * cb, cb)]
    part, which = divmod(unit - 4, 3)
    offset = part * (s.hidden // CHUNKS)
    if which == 2:
        return s.wd.at[span(offset + down, size), span(col * cb, cb)]
    return (s.wg, s.wu)[which].at[span(down, size), span(offset + col * cb, cb)]


def send(s, family, unit, kind, src, dst, peer):
    return pltpu.make_async_remote_copy(
        src_ref=src, dst_ref=dst, send_sem=getattr(s, family + "_send").at[unit, kind],
        recv_sem=getattr(s, family + "_recv").at[unit, kind], device_id=peer, device_id_type=MESH)


def own_source(s, unit, half=None):
    rb, cb = unit_shape(s, unit)
    if unit <= OUT:
        piece, start = s.pieces[unit], 0
    else:
        part, which = divmod(unit - 4, 3)
        if which < 2:
            return block(s, unit, s.row, s.col, half)
        piece, start = s.pieces[6], part * rb
    if half is None:
        return piece.at[start : start + rb, :]
    return piece.at[start + half * (rb // 2) : start + (half + 1) * (rb // 2), :]


def own_copies(s, unit):
    rb, cb = unit_shape(s, unit)
    own = block(s, unit, s.row, s.col)
    part, which = divmod(unit - 4, 3)
    if unit <= OUT or which == 2:
        return [pltpu.make_async_copy(own_source(s, unit), own, s.own_sems.at[unit, 0])]
    piece, half = s.pieces[4 + which], cb // 2
    size = s.hidden // 4
    offset = part * (s.hidden // CHUNKS)
    mine = (s.wg, s.wu)[which]
    return [
        pltpu.make_async_copy(
            piece.at[:, i * size + part * half : i * size + (part + 1) * half],
            mine.at[span(s.row * rb, rb), span(offset + s.col * cb + i * half, half)], s.own_sems.at[unit, i])
        for i in range(2)]


def ag_copy(s, unit, kind):
    b = functools.partial(block, s, unit)
    if kind < 3:
        return send(s, "ag", unit, kind, own_source(s, unit), b(s.row, s.col), (s.to_x, s.to_y, s.to_p)[kind])
    there, peer = [
        (b(s.row_x, s.col, 0), s.to_y), (b(s.row, s.col_y, 1), s.to_x), (b(s.row_x, s.col), s.to_p), (b(s.row, s.col_y), s.to_p),
        (b(s.row_x, s.col_y, 0), s.to_p), (b(s.row_x, s.col_y, 1), s.to_p)][kind - 3]
    return send(s, "ag", unit, kind, there, there, peer)


def ag_arrive(s, unit, kind):
    b = functools.partial(block, s, unit)
    where = [
        b(s.row_x, s.col), b(s.row, s.col_y), b(s.row_p, s.col), b(s.row_x, s.col_y, 0), b(s.row_x, s.col_y, 1),
        b(s.row_px, s.col), b(s.row_p, s.col_y), b(s.row_px, s.col_y, 0), b(s.row_px, s.col_y, 1)][kind]
    send(s, "ag", unit, kind, where, where, s.to_p).wait_recv()


def shuffled(unit):
    return unit > OUT and (unit - 4) % 3 < 2


def own_wait(s, unit):
    for copy in own_copies(s, unit):
        copy.wait()


def ag_open(s, unit):
    if shuffled(unit):
        own_wait(s, unit)
    for kind in range(3):
        ag_copy(s, unit, kind).start()


def ag_relay(s, unit):
    for kind in range(2):
        ag_arrive(s, unit, kind)
        ag_copy(s, unit, kind + 3).start()
        ag_copy(s, unit, kind + 5).start()


def ag_corner(s, unit):
    for kind in (3, 4):
        ag_arrive(s, unit, kind)
        ag_copy(s, unit, kind + 4).start()


def ag_near(s, unit):
    if not shuffled(unit):
        own_wait(s, unit)
    for kind in (2, 5):
        ag_arrive(s, unit, kind)


def ag_far(s, unit):
    for kind in (6, 7, 8):
        ag_arrive(s, unit, kind)


def ag_close(s, unit):
    ag_near(s, unit)
    ag_far(s, unit)


def ag_sent(s, unit):
    for kind in range(9):
        ag_copy(s, unit, kind).wait_send()


def swap_copy(s, family, i, peer, slot):
    slots = getattr(s, family + "_slots")
    return pltpu.make_async_remote_copy(
        src_ref=getattr(s, family + "_from"), dst_ref=slots.at[slot], send_sem=getattr(s, family + "_send").at[i],
        recv_sem=getattr(s, family + "_recv").at[slot], device_id=peer, device_id_type=MESH)


def swap_open(s, family, peers, me):
    getattr(s, family + "_slots")[me] = getattr(s, family + "_from")[...]
    for i, peer in enumerate(peers):
        swap_copy(s, family, i, peer, me).start()


def swap_wait(s, family, peers, ids):
    for i, (peer, slot) in enumerate(zip(peers, ids)):
        copy = swap_copy(s, family, i, peer, slot)
        copy.wait_recv()
        copy.wait_send()


def swap_close(s, family, peers, ids):
    swap_wait(s, family, peers, ids)
    slots = getattr(s, family + "_slots")
    total = slots[0]
    for i in range(1, len(ids) + 1):
        total = total + slots[i]
    return total


def small_rows(s):
    return 2 * (s.width // 128) + s.heads


def small_pack(s, table):
    wide = s.width // 128
    for i in range(2):
        for j in range(wide):
            s.near_from[i * wide + j : i * wide + j + 1, :] = s.small[i : i + 1, 128 * j : 128 * (j + 1)]
    s.near_from[2 * wide : 2 * wide + s.heads, 0 : s.buckets] = table


def small_turn(s, unit):
    s.far_from[...] = swap_close(s, "near", s.plane, s.plane_ids)
    swap_open(s, "far", s.stack, s.z)


DIRECT = 2


def quarter(s, unit, row, index):
    rb, cb = unit_shape(s, unit)
    return s.p.at[span(unit * (4 * s.micro * s.length) + s.col * s.width + row * rb + index * (rb // 4), rb // 4), 0:cb]


def rs_copy(s, unit, kind):
    b = functools.partial(block, s, unit, grad=True)
    n = lambda name: getattr(s, f"{name}{unit}")
    low = s.z - 1
    if unit == DIRECT and kind >= 10:
        peer, there = s.stack[(kind - 10) % 3], s.stack_ids[(kind - 10) % 3]
        if kind < 13:
            return send(s, "rs", unit, kind, quarter(s, unit, s.row, there), n("zq").at[kind - 10], peer)
        return send(s, "rs", unit, kind, quarter(s, unit, s.row, s.z), quarter(s, unit, s.row_p, s.z), peer)
    if kind < 4:
        x, col = divmod(kind, 2)
        return send(s, "rs", unit, kind, b(2 * x + 1 - s.core, col), n("pr").at[x, col], s.to_p)
    if kind < 6:
        return send(s, "rs", unit, kind, b(s.row_x, kind - 4, 0), n("xa").at[kind - 4], s.to_x)
    if kind < 8:
        return send(s, "rs", unit, kind, b(2 * (kind - 6) + s.core, s.col_y, 1), n("yb").at[kind - 6], s.to_y)
    up, side = (s.z_out, s.row, s.col), (3 - s.z, s.row, s.col)
    src, dst, peer = [
        lambda: (b(s.row, s.col_y, 0), n("ya"), s.to_y),
        lambda: (b(s.row_x, s.col, 1), n("xb"), s.to_x),
        lambda: (b(s.row, s.col), n("zi"), (s.z_in, s.row, s.col)),
        lambda: (b(s.row, s.col, 1 - low), n("zx"), side),
        lambda: (b(s.row, s.col, low), b(s.row_p, s.col, low), side),
        lambda: (b(s.row, s.col, low), b(s.row_p, s.col, low), up),
        lambda: (b(s.row_p, s.col, 1 - low), b(s.row_p, s.col, 1 - low), up)][kind - 8]()
    return send(s, "rs", unit, kind, src, dst, peer)


def rs_arrive(s, unit, kind):
    b = functools.partial(block, s, unit, grad=True)
    n = lambda name: getattr(s, f"{name}{unit}")
    if unit == DIRECT and kind >= 13:
        where = quarter(s, unit, s.row_p, lax.rem(s.z + 4 - (kind - 12), 4))
    elif unit == DIRECT and kind >= 10:
        where = n("zq").at[kind - 10]
    elif kind < 4:
        where = n("pr").at[kind // 2, kind % 2]
    elif kind < 6:
        where = n("xa").at[kind - 4]
    elif kind < 8:
        where = n("yb").at[kind - 6]
    elif kind < 12:
        where = n(("ya", "xb", "zi", "zx")[kind - 8])
    else:
        where = b(s.row_p, s.col, (2 - s.z, s.z_in - 1, 2 - s.z_in)[kind - 12])
    send(s, "rs", unit, kind, where, where, s.to_p).wait_recv()
    return where


def add_into(target, source):
    rows = target.shape[0]
    step = 32 if rows % 32 == 0 else 16

    def body(i):
        r = rows_of(i, step)
        target[r, :] = target[r, :] + source[r, :]

    loop(rows // step, body)


def rs_1(s, unit):
    for kind in range(4):
        rs_copy(s, unit, kind).start()


def rs_2(s, unit):
    b = functools.partial(block, s, unit, grad=True)
    for kind in range(4):
        x, col = divmod(kind, 2)
        add_into(b(2 * x + s.core, col), rs_arrive(s, unit, kind))
    for kind in range(4, 8):
        rs_copy(s, unit, kind).start()


def rs_3(s, unit):
    b = functools.partial(block, s, unit, grad=True)
    for col in range(2):
        add_into(b(s.row, col, 0), rs_arrive(s, unit, 4 + col))
    rs_copy(s, unit, 8).start()
    for x in range(2):
        add_into(b(2 * x + s.core, s.col, 1), rs_arrive(s, unit, 6 + x))
    rs_copy(s, unit, 9).start()


def rs_4(s, unit):
    b = functools.partial(block, s, unit, grad=True)
    for half in range(2):
        add_into(b(s.row, s.col, half), rs_arrive(s, unit, 8 + half))
    for kind in range(10):
        rs_copy(s, unit, kind).wait_send()
    if unit == DIRECT:
        for kind in (11, 10, 12):
            rs_copy(s, unit, kind).start()
        return

    @pl.when(s.outer)
    def _():
        rs_copy(s, unit, 10).start()


def rs_5(s, unit):
    if unit == DIRECT:
        mine = quarter(s, unit, s.row, s.z)
        for kind in (10, 12, 11):
            add_into(mine, rs_arrive(s, unit, kind))
        for kind in (14, 13, 15):
            rs_copy(s, unit, kind).start()
        quarter(s, unit, s.row_p, s.z)[...] = mine[...]
        return

    @pl.when(s.inner)
    def _():
        add_into(block(s, unit, s.row, s.col, grad=True), rs_arrive(s, unit, 10))
        rs_copy(s, unit, 11).start()


def rs_6(s, unit):
    if unit == DIRECT:
        for kind in (13, 15, 14):
            rs_arrive(s, unit, kind)
        for kind in range(10, 16):
            rs_copy(s, unit, kind).wait_send()
        rs_out(s, unit).start()
        return

    @pl.when(s.inner)
    def _():
        mine = block(s, unit, s.row, s.col, s.z - 1, grad=True)
        add_into(mine, rs_arrive(s, unit, 11))
        rs_copy(s, unit, 12).start()
        rs_copy(s, unit, 13).start()
        done = block(s, unit, s.row_p, s.col, s.z - 1, grad=True)
        done[...] = mine[...]


def rs_7(s, unit):
    @pl.when(s.inner)
    def _():
        rs_arrive(s, unit, 12)
        rs_copy(s, unit, 14).start()
        for kind in (11, 12, 13):
            rs_copy(s, unit, kind).wait_send()

    @pl.when(s.outer)
    def _():
        rs_arrive(s, unit, 13)
        rs_copy(s, unit, 10).wait_send()


def rs_8(s, unit):
    @pl.when(s.inner)
    def _():
        rs_copy(s, unit, 14).wait_send()

    @pl.when(s.outer)
    def _():
        rs_arrive(s, unit, 14)

    rs_out(s, unit).start()


def rs_out(s, unit):
    return pltpu.make_async_copy(block(s, unit, s.row_p, s.col, grad=True), s.unit_out[unit], s.out_sems.at[unit])


PLAN = {
    ("start", 0): (("o", 0), ("o", 1), ("o", 2)),
    ("project", 0): (("r", 0), ("n", 0), ("o", 3)),
    ("project", 1): (("r", 1), ("n", 1)),
    ("project", 2): (("o", 4), ("r", 2), ("n", 2)),
    ("attend", 0): (("c", 0),),
    ("attend", 1): (("o", 5),),
    ("attend", 2): (("r", 3),),
    ("attend", 3): (("c", 1),),
    ("attend", 4): (("o", 6),),
    ("attend", 5): (("r", 4),),
    ("project", 3): (("c", 2), ("o", 7), ("f", 0)),
    ("project", 4): (("r", 5), ("f", 1)),
    ("project", 5): (("c", 3), ("o", 8), ("f", 2)),
    ("attend", 6): (("o", 9),),
    ("attend", 7): (("c", 4), ("r", 6)),
    ("attend", 9): (("r", 7),),
    ("attend", 10): (("c", 5), ("o", 10)),
    ("attend", 11): (("r", 8),),
    ("feed_in", 0): (("o", 11), ("x", 3)),
    ("feed", 0): (("c", 6), ("c", 7), ("r", 9), ("o", 12), ("x", 4), ("x", 5), ("x", 6), ("r", 10)),
    ("feed", 1): (("c", 8), ("r", 11), ("o", 13)),
    ("feed", 4): (("c", 9), ("r", 12), ("o", 14)),
    ("feed", 5): (("c", 10), ("c", 11), ("o", 15), (1, 4), (1, 5), (1, 6), ("x", 7), ("x", 8), ("x", 9)),
    ("feed", 6): (("c", 12), ("r", 13), (2, 4), (2, 5), (2, 6), ("r", 14)),
    ("feed", 9): (("c", 13), ("r", 15)),
    ("feed", 10): ((3, 4), (1, 7), (1, 8), (1, 9), ("x", 10), ("x", 11), ("x", 12)),
    ("feed", 11): ((3, 5), (3, 6), (2, 7), (2, 8), (2, 9), ("c", 14)),
    ("feed", 14): (("c", 15), (4, 4), (4, 5)),
    ("feed", 15): ((4, 6), (1, 10), (1, 11), ("x", 13), ("x", 14), ("x", 15), (3, 7)),
    ("feed", 16): ((5, 4), (3, 8), (2, 10), (2, 11), (5, 5)),
    ("feed", 19): ((6, 4), (5, 6), (4, 7), (4, 8), (3, 9)),
    ("close", 0): ((6, 5), (3, 10)),
    ("outback", 0): ((7, 4), (6, 6), (5, 7), (4, 9), (3, 11), (1, 12), (1, 13), (1, 14), (1, 15)),
    ("outback", 1): ((7, 5), (5, 8), (4, 10), (2, 12)),
    ("outback", 2): ((2, 13), (2, 14)),
    ("outback", 3): ((8, 4), (7, 6), (4, 11), (2, 15)),
    ("outgrad", 0): ((6, 7), (5, 9)),
    ("outgrad", 1): ((1, 3), (8, 5), (6, 8), (5, 10), (3, 12)),
    ("back", 1): ((8, 6),),
    ("back", 2): ((7, 7), (6, 9), (5, 11), (3, 13), (2, 3)),
    ("back", 3): ((7, 8), (3, 14), (6, 10)),
    ("chunk", 0): ((1, 0), (8, 7), (7, 9), (6, 11), (4, 12), (4, 13), (3, 15), (8, 8)),
    ("back", 5): ((7, 10), (2, 0)),
    ("back", 6): ((3, 3),),
    ("back", 7): ((8, 9), (7, 11), (5, 12), (4, 14), (4, 15)),
    ("chunk", 1): ((1, 1), (8, 10), (5, 13), (3, 0), (8, 11), (6, 12)),
    ("back", 9): ((5, 14), (4, 3), (2, 1)),
    ("back", 10): ((5, 15),),
    ("back", 11): ((7, 12), (6, 13), (4, 0)),
    ("chunk", 2): ((1, 2), (6, 14), (6, 15), (5, 3), (3, 1), (8, 12), (7, 13)),
    ("input", 1): ((2, 2),),
    ("input", 2): ((5, 0),),
    ("input", 3): ((7, 14), (7, 15), (4, 1)),
    ("input", 4): ((8, 13), (6, 3)),
    ("tail", 0): ((6, 0), (3, 2), (8, 14), (8, 15), (7, 3), (5, 1), (7, 0), (4, 2), ("w", 0), (8, 3), (6, 1), (8, 0), (5, 2), (7, 1), (8, 1), (6, 2)),
}


NAMES = ("wq", "wk", "wv", "wo", "wg", "wu", "wd")
UNITS = OUT + 1 + 3 * CHUNKS
EARLY = tuple(range(4, 12))
ACTS = {"o": ag_open, "r": ag_relay, "c": ag_corner, "x": ag_close, "n": ag_near, "f": ag_far, "w": small_turn, 1: rs_1, 2: rs_2, 3: rs_3, 4: rs_4, 5: rs_5, 6: rs_6, 7: rs_7, 8: rs_8}


def act_all(s, todo):
    for act, unit in todo if s.comm else ():
        ACTS[act](s, unit)


def hook(s, phase, index):
    entries = sorted((number, todo) for (name, number), todo in PLAN.items() if name == phase)
    if not s.comm:
        return
    if isinstance(index, int):
        for number, todo in entries:
            if number == index:
                act_all(s, todo)
        return

    def pick(some):
        if len(some) == 1:
            pl.when(index == some[0][0])(functools.partial(act_all, s, some[0][1]))
        elif some:
            middle = len(some) // 2
            pl.when(index < some[middle][0])(lambda: pick(some[:middle]))
            pl.when(index >= some[middle][0])(lambda: pick(some[middle:]))

    pick(entries)


def gains_in(s):
    for i, gain in enumerate((s.gain_one, s.gain_two)):
        if s.comm:
            s.gain_from[i : i + 1, 0 : gain.shape[1]] = gain[...].astype(F32)
        else:
            s.gain[i : i + 1, :] = gain[...].astype(F32)


def gains_spread(s):
    swap_wait(s, "gain", s.plane, s.plane_ids)
    count = s.gain_one.shape[1]
    wide = (128, s.width)
    lane, spot = lax.broadcasted_iota(jnp.int32, wide, 0), lax.broadcasted_iota(jnp.int32, wide, 1)
    total = None
    for i in range(8):
        part = nn(s.gain_slots[i].astype(BF), jnp.logical_and(spot == lane + count * i, lane < count).astype(BF))
        total = part if total is None else total + part
    s.gain[...] = total


def layer(cfg, *refs):
    s = types.SimpleNamespace(**cfg)
    for name, ref in zip(cfg["names"], refs):
        setattr(s, name, ref)
    s.pieces = [getattr(s, n + "_in") for n in NAMES]
    comm = s.comm
    s.hook = functools.partial(hook, s)
    load_x = pltpu.make_async_copy(s.x_in, s.x, s.io_sems.at[2])
    load_c = pltpu.make_async_copy(s.c_in, s.c, s.io_sems.at[1])
    tiny_loads = [
        pltpu.make_async_copy(getattr(s, name + "_in"), getattr(s, name), s.tiny_sems.at[i])
        for i, name in enumerate(("gain_one", "gain_two", "seg", "bucket", "table"))]
    for copy in tiny_loads + [load_x, load_c]:
        copy.start()
    Q, K, V, O = range(4)
    if comm:
        place(s)
        s.unit_out = [getattr(s, f"unit{u}_out") for u in range(UNITS)]
        greet(s)
        for copy in tiny_loads:
            copy.wait()
        s.gain_from[...] = jnp.zeros_like(s.gain_from)
        gains_in(s)
        swap_open(s, "gain", s.plane, s.me)
        s.hook("start", 0)
        for unit in range(UNITS):
            for copy in own_copies(s, unit):
                copy.start()
    else:
        weights = [pltpu.make_async_copy(piece, getattr(s, n), s.load_sems.at[i]) for i, (n, piece) in enumerate(zip(NAMES, s.pieces))]
        for copy in weights:
            copy.start()
        for copy in tiny_loads:
            copy.wait()
        gains_in(s)
    s.small[...] = jnp.zeros_like(s.small)
    s.near_from[...] = jnp.zeros_like(s.near_from)
    offset_rows(s)
    tw, wt = (s.tokens, s.width), (s.width, s.tokens)
    vm = pltpu.VMEM

    def attention(a, mask, toep):
        s.a, s.mask, s.toep = a, mask, toep
        masks(s)
        load_x.wait()
        if comm:
            gains_spread(s)
        else:
            for copy in weights:
                copy.wait()
        norm_in(s, 128)
        pairs = s.heads // 4
        for part in range(2):
            side = (s.col if part == 0 else s.col_y) if comm else part
            for w in (Q, K, V):
                s.hook("project", 3 * part + w)
                project(s, w, side, 256)
            loop(pairs, functools.partial(attend_pair, s, side, 2 * pairs * part))

    skew = vm((128, 2 * s.length), F32)
    pl.run_scoped(attention, vm(tw, BF), vm((s.micro, s.length, s.length), F32), skew)
    s.n2t = s.vt

    def feed(act, mid, y, ct):
        s.mid, s.y, s.ct = mid, y, ct
        s.dg, s.du = (act.at[:, i * s.ft : (i + 1) * s.ft] for i in range(2))
        s.hid = s.x.at[:, 0 : s.ft]
        load_c.wait()
        s.hook("feed_in", 0)
        out_project(s, 256)

        def step(t):
            ffn_rows(s, t, s.ft, s.rb)
            s.hook("feed", 5 * t + 4)
            if comm:
                for part in range(CHUNKS):

                    @pl.when(t == part)
                    def _():
                        for which in range(3):
                            ag_sent(s, ffn_unit(part, which))

            ffn_grads(s, t, s.ft, s.gb)

        loop(s.hidden // s.ft, step)
        s.hook("close", 0)
        ffn_close(s, 128)

    pl.run_scoped(feed, vm((s.tokens, 2 * s.ft), BF), vm(tw, F32), vm(tw, F32), vm(wt, BF))
    put_y = pltpu.make_async_copy(s.c, s.y_out, s.io_sems.at[0])
    put_x = pltpu.make_async_copy(s.x, s.gi_out, s.io_sems.at[1])
    put_y.start()
    load_x.start()

    def back(toep, ds, goff, *bufs):
        s.toep, s.ds, s.goff = toep, ds, goff
        s.do, s.dot = s.c, s.vt
        for name, ref in zip(s.rs_names, bufs):
            setattr(s, name, ref)
        if comm:
            for peer in [s.to_p, s.to_x, s.to_y] + s.stack:
                pl.semaphore_signal(s.ready, inc=1, device_id=peer, device_id_type=MESH)
            pl.semaphore_wait(s.ready, 6)
        put_y.wait()
        out_backward(s, 256)
        s.hook("outgrad", 0)
        if comm:
            for unit in range(4):
                ag_sent(s, unit)
        out_grads(s, 256)
        s.hook("outgrad", 1)

        def step(i):
            attend_back(s, i)

            @pl.when(lax.rem(i, 2) == 1)
            def _():
                chunk_grads(s, lax.div(i, 2), 384)
                s.hook("chunk", lax.div(i, 2))

        loop(s.heads // 2, step)
        s.hook("input", 0)
        table = table_grad(s)
        load_x.wait()
        qkv_back_input(s, 256)
        put_x.start()
        small_pack(s, table)
        if comm:
            swap_open(s, "near", s.plane, s.me)
            s.hook("tail", 0)
            s.small_sum[...] = swap_close(s, "far", s.stack, s.stack_ids)
            for unit in range(UNITS):
                rs_out(s, unit).wait()
        else:
            s.small_sum[...] = s.near_from[...]
            outs = [pltpu.make_async_copy(getattr(s, n), getattr(s, n + "_out"), s.load_sems.at[i + 3]) for i, n in enumerate(NAMES[3:])]
            for copy in outs:
                copy.start()
            for copy in outs:
                copy.wait()
            half = s.heads // 4
            for w, n in enumerate(NAMES[:3]):
                for pair in range(s.heads // 2):
                    copy = pltpu.make_async_copy(
                        s.p.at[slab(s, pair % half, pair // half), 128 * w : 128 * (w + 1)],
                        getattr(s, n + "_out").at[:, 128 * pair : 128 * (pair + 1)], s.load_sems.at[w])
                    copy.start()
                    copy.wait()

    pl.run_scoped(
        back, skew, vm((s.length, s.length), BF), vm((8, s.heads, 2 * s.length), F32), *[vm(shape, BF) for shape in s.rs_shapes])
    put_small = pltpu.make_async_copy(s.small_sum, s.small_out, s.tiny_sems.at[5])
    put_small.start()
    put_x.wait()
    put_small.wait()


def call_layer(comm, x, c, weights, gains, seg, bucket, table, full):
    tokens, width = x.shape
    micro, length = seg.shape
    heads, buckets = table.shape
    hidden = full[4][1]
    ft, vm, sem = 512, pltpu.VMEM, pltpu.SemaphoreType.DMA
    tw, wt, tiny = (tokens, width), (width, tokens), (2 * (width // 128) + heads, 128)
    s = types.SimpleNamespace(
        comm=comm, tokens=tokens, width=width, micro=micro, length=length, hidden=hidden, heads=heads, buckets=buckets, ft=ft, gb=768, rb=512,
        rs_names=[], rs_shapes=[])
    scratch = dict(
        x=vm(tw, BF), c=vm(tw, BF), **{n: vm(shape, BF) for n, shape in zip(NAMES, full)},
        n1t=vm(wt, BF), q=vm(tw, BF), k=vm(tw, BF), v=vm(tw, BF), kt=vm(wt, BF), vt=vm(wt, BF), ot=vm(wt, BF),
        dn=vm(tw, F32), p=vm((heads * micro * length, length), BF),
        offs=vm((heads, 2 * length), F32), gain=vm((8, width), F32), small=vm((2, width), F32), near_from=vm(tiny, F32),
        turned=vm((1, 2 * length), jnp.int32), io_sems=sem((3,)), load_sems=sem((7,)), out_sems=sem((UNITS,)),
    )
    out_shape = [(tw, BF)] * 2
    if comm:
        scratch.update(
            gain_from=vm((8, 128), F32), far_from=vm(tiny, F32),
            gain_slots=vm((8, 8, 128), F32), near_slots=vm((8, *tiny), F32), far_slots=vm((4, *tiny), F32),
            ag_send=sem((UNITS, 9)), ag_recv=sem((UNITS, 9)), own_sems=sem((UNITS, 2)), rs_send=sem((UNITS, 16)), rs_recv=sem((UNITS, 16)),
            gain_send=sem((7,)), gain_recv=sem((8,)), near_send=sem((7,)), near_recv=sem((8,)), far_send=sem((3,)), far_recv=sem((4,)),
            ready=pltpu.SemaphoreType.REGULAR,
        )
        for unit in range(UNITS):
            rb, cb = unit_shape(s, unit)
            hb = rb // 2
            shapes = dict(pr=(2, 2, rb, cb), xa=(2, hb, cb), yb=(2, hb, cb), ya=(hb, cb), xb=(hb, cb), zi=(rb, cb), zx=(hb, cb))
            if unit == DIRECT:
                del shapes["zi"], shapes["zx"]
                shapes["zq"] = (3, rb // 4, cb)
            for name, shape in shapes.items():
                if unit in EARLY:
                    scratch[f"{name}{unit}"] = vm(shape, BF)
                else:
                    s.rs_names.append(f"{name}{unit}")
                    s.rs_shapes.append(shape)
            out_shape.append(((rb, cb), BF))
        grad_names = [f"unit{unit}_out" for unit in range(UNITS)]
    else:
        out_shape += [(shape, BF) for shape in full]
        grad_names = [n + "_out" for n in NAMES]
    tiny_ins = dict(gain_one=gains[0], gain_two=gains[1], seg=seg, bucket=bucket, table=table)
    for name, array in tiny_ins.items():
        scratch[name] = vm(array.shape, array.dtype)
    scratch.update(tiny_sems=sem((6,)), small_sum=vm(tiny, F32))
    ins = ["x_in", "c_in"] + [n + "_in" for n in NAMES] + [name + "_in" for name in tiny_ins]
    outs = ["y_out", "gi_out"] + grad_names + ["small_out"]
    out_shape.append((tiny, F32))
    names = ins + outs + list(scratch)
    far = pl.BlockSpec(memory_space=pl.ANY)
    params = dict(vmem_limit_bytes=67043328)
    if comm:
        params.update(collective_id=0, has_side_effects=True)

    def body(*refs):
        cfg = dict(vars(s), names=names)
        layer(cfg, *refs)

    return pl.pallas_call(
        body, out_shape=[jax.ShapeDtypeStruct(*o) for o in out_shape],
        in_specs=[far] * len(ins), out_specs=[far] * len(outs), scratch_shapes=list(scratch.values()),
        compiler_params=pltpu.CompilerParams(**params),
    )(x, c, *weights, *gains, seg, bucket, table)


def finish_kernel(cfg, *refs):
    s = types.SimpleNamespace(**cfg)
    srcs, outs = refs[: 3 + UNITS], refs[3 + UNITS : 3 + UNITS + 12]
    bufs = refs[15 + UNITS : 15 + 3 + 2 * UNITS]
    wide, tiny, (in_sems, out_sems) = refs[18 + 2 * UNITS : -5], refs[-5:-2], refs[-2:]
    loads = [pltpu.make_async_copy(src, buf, in_sems.at[i]) for i, (src, buf) in enumerate(zip(srcs, bufs))]
    for i in [len(loads) - 1] + list(range(2, len(loads) - 1)) + [0, 1]:
        loads[i].start()
    row, col = lax.axis_index("row"), lax.axis_index("col")
    y, gi, gain_one, gq, gk, gv, go, table, gain_two, gg, gu, gd = outs
    small, units = bufs[-1], bufs[2:-1]
    stores = []

    def leave(buf, out):
        stores.append(pltpu.make_async_copy(buf, out, out_sems.at[len(stores)]))
        stores[-1].start()

    loads[-1].wait()
    rows = s.width // 128
    at = lax.rem(s.width - s.gain_count * (2 * row + col), s.width)
    for i, out in enumerate((gain_one, gain_two)):
        full = jnp.concatenate([small[i * rows + j : i * rows + j + 1, :] for j in range(rows)], axis=1)
        tiny[i][...] = pltpu.roll(jnp.broadcast_to(full, (8, s.width)), at, 1)[0:1, 0 : s.gain_count]
        leave(tiny[i], out)
    tiny[2][...] = small[2 * rows : 2 * rows + s.heads, 0 : s.buckets]
    leave(tiny[2], table)
    wq, wk, wv, wo, wg, wu, wd = wide
    for unit in range(3):
        loads[2 + unit].wait()
        for w, buf in enumerate((wq, wk, wv)):
            buf[:, 128 * unit : 128 * (unit + 1)] = units[unit][:, 128 * w : 128 * (w + 1)].astype(F32)
    for buf, out in ((wq, gq), (wk, gk), (wv, gv)):
        leave(buf, out)
    loads[2 + OUT].wait()
    wo[...] = units[OUT][...].astype(F32)
    leave(wo, go)
    for which, buf, out in ((0, wg, gg), (1, wu, gu), (2, wd, gd)):
        for part in range(CHUNKS):
            unit = ffn_unit(part, which)
            loads[2 + unit].wait()
            rows, cols = units[unit].shape
            if which == 2:
                buf[part * rows : (part + 1) * rows, :] = units[unit][...].astype(F32)
            else:
                size = buf.shape[1] // 2
                for i in range(2):
                    at = i * size + part * (cols // 2)
                    buf[:, at : at + cols // 2] = units[unit][:, i * (cols // 2) : (i + 1) * (cols // 2)].astype(F32)
        leave(buf, out)
    for i, out in enumerate((y, gi)):
        loads[i].wait()
        leave(bufs[i], out)
    for copy in stores:
        copy.wait()


def finish(arrays, gain_count, heads, buckets, blocks):
    vm, sh = pltpu.VMEM, jax.ShapeDtypeStruct
    far = pl.BlockSpec(memory_space=pl.ANY)
    y, gi = arrays[:2]
    b = [sh(shape, F32) for shape in blocks]
    gain = sh((1, gain_count), F32)
    cfg = dict(width=y.shape[1], gain_count=gain_count, heads=heads, buckets=buckets)
    return pl.pallas_call(
        functools.partial(finish_kernel, cfg),
        out_shape=[sh(y.shape, BF), sh(gi.shape, BF), gain, *b[:4], sh((heads, buckets), F32), gain, *b[4:]],
        in_specs=[far] * len(arrays), out_specs=[far] * 12,
        scratch_shapes=[vm(a.shape, a.dtype) for a in arrays] + [vm(shape, F32) for shape in blocks]
        + [vm(gain.shape, F32)] * 2 + [vm((heads, buckets), F32)]
        + [pltpu.SemaphoreType.DMA((len(arrays),)), pltpu.SemaphoreType.DMA((12,))],
        compiler_params=pltpu.CompilerParams(vmem_limit_bytes=67043328),
    )(*arrays)


def open_block(gathered, row_count, column_count):
    _, rows, columns = gathered.shape
    grid = gathered.reshape(row_count, column_count, rows, columns).transpose(0, 2, 1, 3)
    return grid.reshape(row_count * rows, column_count * columns)


def close_block(full, row_count, column_count):
    rows, columns = full.shape[0] // row_count, full.shape[1] // column_count
    grid = full.reshape(row_count, rows, column_count, columns).transpose(0, 2, 1, 3)
    return grid.reshape(row_count * column_count, rows, columns)


def shards(block_input, segment_ids, bucket, gain_attn, w_query, w_key, w_value, w_out, bias_table, gain_ffn, w_gate, w_up, w_down, cotangent):
    row_count, column_count = lax.axis_size("row"), lax.axis_size("col")
    micro, length, width = block_input.shape
    tokens, gain_count = micro * length, gain_attn.shape[0]
    buckets, heads = bias_table.shape
    pieces = [w_query, w_key, w_value, w_out, w_gate, w_up, w_down]
    full = [(p.shape[0] * row_count, p.shape[1] * column_count) for p in pieces]
    fits = row_count == 4 and column_count == 2 and lax.axis_size("dp") == 4
    x, c = block_input.reshape(tokens, width), cotangent.reshape(tokens, width)
    gains = [gain_attn[None], gain_ffn[None]]
    plane = ("row", "col")
    if fits:
        out = call_layer(True, x, c, pieces, gains, segment_ids, bucket[None], bias_table.T, full)
        y, gi, one, gq, gk, gv, go, table, two, gg, gu, gd = finish(
            out, gain_count, heads, buckets, [p.shape for p in pieces])
        return y.reshape(block_input.shape), gi.reshape(block_input.shape), one[0], gq, gk, gv, go, table.T, two[0], gg, gu, gd
    gains = [lax.all_gather(g, plane, axis=1, tiled=True) for g in gains]
    weights = [open_block(lax.all_gather(p[None], plane, axis=0, tiled=True), row_count, column_count) for p in pieces]
    out = call_layer(False, x, c, weights, gains, segment_ids, bucket[None], bias_table.T, full)
    y, gi, grads, small = out[0], out[1], out[2:9], out[9]
    small = lax.psum(small, ("dp",) + plane)
    grads = [lax.psum_scatter(close_block(g, row_count, column_count), plane, scatter_dimension=0, tiled=True)[0] for g in grads]
    gq, gk, gv, go, gg, gu, gd = (lax.psum(g, "dp").astype(F32) for g in grads)
    mine = (lax.axis_index("row") * column_count + lax.axis_index("col")) * gain_count
    one, two = (lax.dynamic_slice(small[i * (width // 128) : (i + 1) * (width // 128)].reshape(-1), (mine,), (gain_count,)) for i in range(2))
    table = small[2 * (width // 128) :, :buckets].T
    return y.reshape(block_input.shape), gi.reshape(block_input.shape), one, gq, gk, gv, go, table, two, gg, gu, gd


def solution(mesh):
    whole = P(None, ("dp", "row", "col"), None)
    split, gain = P("row", "col"), P(("row", "col"))
    return jax.shard_map(
        shards, mesh=mesh,
        in_specs=(whole, P(None, ("dp", "row", "col")), P(), gain, split, split, split, split, P(), gain, split, split, split, whole),
        out_specs=(whole, whole, gain, split, split, split, split, P(), gain, split, split, split),
        check_vma=False)
```

```python
import functools
import types

import jax
import jax.numpy as jnp
from jax import lax
from jax.experimental import pallas as pl
from jax.experimental.pallas import tpu as pltpu
from jax.sharding import PartitionSpec as P

F32 = jnp.float32
BF = jnp.bfloat16
EPSILON = 1e-06
NEGATIVE = -1e30
PRECISE = lax.Precision.HIGHEST
MESH = pl.DeviceIdType.MESH
CHUNKS = 4
GELU_0 = 0.7978845608028654
GELU_1 = 0.044715


def contract(left, right, dims, **more):
    return lax.dot_general(left, right, ((dims[:1], dims[1:]), ((), ())), preferred_element_type=F32, **more)


def nn(left, right):
    return contract(left, right, (1, 0))


def nt(left, right):
    return contract(left, right, (1, 1))


def rows_of(index, size):
    return pl.ds(pl.multiple_of(index * size, size), size)


def loop(count, body):
    lax.fori_loop(0, count, lambda index, carry: (body(index), carry)[1], 0)


def bucket_classes(s):
    return (s.turned[...] == lax.broadcasted_iota(jnp.int32, (s.buckets, 2 * s.length), 0)).astype(F32)


def offset_rows(s):
    twice = 2 * s.length
    s.turned[...] = jnp.full((1, twice), -1, jnp.int32)
    s.turned[:, 0 : twice - 1] = s.bucket[...]
    flip = (lax.broadcasted_iota(jnp.int32, (128, 128), 0) + lax.broadcasted_iota(jnp.int32, (128, 128), 1) == 127).astype(BF)
    parts = [nn(s.turned[:, i : i + 128].astype(F32).astype(BF), flip) for i in range(0, twice, 128)]
    turned = jnp.concatenate(parts[::-1], axis=1)
    s.turned[...] = pltpu.roll(turned, twice - 1, 1).astype(jnp.int32)
    s.offs[...] = contract(s.table[...], bucket_classes(s), (1, 0), precision=PRECISE)


def masks(s):
    for m in range(s.micro):
        row = s.seg[m : m + 1, :].astype(F32)
        column = jnp.broadcast_to(row, (128, s.length)).T
        for i in range(0, s.length, 128):
            s.mask[m, :, i : i + 128] = jnp.where(column == row[:, i : i + 128], 0.0, NEGATIVE)


def norm_in(s, rb):
    def body(i):
        r = rows_of(i, rb)
        x = s.x[r, :].astype(F32)
        scale = lax.rsqrt(jnp.mean(x * x, axis=-1, keepdims=True) + EPSILON)
        n = (x * scale * s.gain[0:1, :]).astype(BF)
        s.a[r, :] = n
        s.n1t[:, r] = n.T

    loop(s.tokens // rb, body)


def spot(s, pair):
    half = s.heads // 4
    return 2 * (pair % half) + pair // half


def project(s, which, side, rb):
    weight, out, out_t = ((s.wq, s.q, None), (s.wk, s.k, s.kt), (s.wv, s.v, s.vt))[which]
    wide = s.width // 2
    cols = pl.ds(pl.multiple_of(side * wide, 128), wide)

    def body(i):
        r = rows_of(i, rb)
        p = nn(s.a[r, :], weight[:, cols]).astype(BF)
        for j in range(s.heads // 4):
            out[r, rows_of(2 * j + side, 128)] = p[:, 128 * j : 128 * (j + 1)]
        if out_t is not None:
            out_t[cols, r] = p.T

    loop(s.tokens // rb, body)


def half_masks(dtype):
    lane = lax.broadcasted_iota(jnp.int32, (1, 128), 1)
    return [(lane < 64).astype(dtype), (lane >= 64).astype(dtype)]


def attend_pair(s, side, late, j):
    length = s.length
    blocks = length // 128
    pair, i = (s.heads // 4) * side + j, 2 * j + side
    here = rows_of(i, 128)
    keep = half_masks(BF)
    for sub in range(2):
        s.hook("attend", late + 2 * j + sub)
        head = 2 * pair + sub
        hr = rows_of(head, 64)
        row = jnp.broadcast_to(s.offs[pl.ds(head, 1), :], (128, 2 * length))
        s.toep[...] = pltpu.roll(row, 2 * length - 127, 1, stride=1, stride_axis=0)
        for m in range(s.micro):
            mr = slice(m * length, (m + 1) * length)
            scores = nt(s.k[mr, here] * keep[sub], s.q[mr, here])
            bias = jnp.concatenate([s.toep[:, 128 * b : 128 * b + length] for b in reversed(range(blocks))], axis=0)
            scores = scores + bias + s.mask[m]
            e = jnp.exp(scores - jnp.max(scores, axis=0, keepdims=True))
            low = (e * (1.0 / jnp.sum(e, axis=0, keepdims=True))).astype(BF)
            s.p[rows_of((2 * i + sub) * s.micro + m, length), :] = low
            s.ot[hr, mr] = nn(s.vt[hr, mr], low).astype(BF)


def out_project(s, rb):
    def body(i):
        r = rows_of(i, rb)
        mid = s.x[r, :].astype(F32) + nn(s.ot[:, r].T, s.wo[...])
        s.mid[r, :] = mid
        s.y[r, :] = mid
        scale = lax.rsqrt(jnp.mean(mid * mid, axis=-1, keepdims=True) + EPSILON)
        n = (mid * scale * s.gain[1:2, :]).astype(BF)
        s.k[r, :] = n
        s.n2t[:, r] = n.T
        s.dn[r, :] = jnp.zeros_like(mid)
        s.ct[:, r] = s.c[r, :].T

    loop(s.tokens // rb, body)


def ffn_rows(s, tile, ft, rb):
    cols = rows_of(tile, ft)

    def forward(i):
        s.hook("feed", 5 * tile + i)
        r = rows_of(i, rb)
        n = s.k[r, :]
        gate = nn(n, s.wg[:, cols])
        up = nn(n, s.wu[:, cols])
        dh = nt(s.c[r, :], s.wd[cols, :])
        square = gate * gate
        t = jnp.tanh(gate * (GELU_0 + (GELU_0 * GELU_1) * square))
        half = 0.5 + 0.5 * t
        act = gate * half
        slope = half + (0.5 * gate) * (1.0 - t * t) * (GELU_0 + (3.0 * GELU_0 * GELU_1) * square)
        hid = (act * up).astype(BF)
        dg = (dh * up * slope).astype(BF)
        du = (dh * act).astype(BF)
        s.hid[r, :] = hid
        s.dg[r, :] = dg
        s.du[r, :] = du
        s.y[r, :] += nn(hid, s.wd[cols, :])
        s.dn[r, :] += nt(dg, s.wg[:, cols]) + nt(du, s.wu[:, cols])

    loop(s.tokens // rb, forward)


def ffn_grads(s, tile, ft, gb):
    cols = rows_of(tile, ft)

    def grads(i):
        r = rows_of(i, gb)
        s.wd[cols, r] = nn(s.ct[r, :], s.hid[...]).astype(BF).T
        s.wg[r, cols] = nn(s.n2t[r, :], s.dg[...]).astype(BF)
        s.wu[r, cols] = nn(s.n2t[r, :], s.du[...]).astype(BF)

    loop(s.width // gb, grads)


def ffn_close(s, rb):
    def body(i):
        r = rows_of(i, rb)
        mid = s.mid[r, :]
        dn = s.dn[r, :]
        scale = lax.rsqrt(jnp.mean(mid * mid, axis=-1, keepdims=True) + EPSILON)
        gdn = dn * s.gain[1:2, :]
        dot = jnp.mean(gdn * mid, axis=-1, keepdims=True)
        dmid = s.c[r, :].astype(F32) + scale * gdn - mid * (scale * scale * scale * dot)
        s.small[1:2, :] += jnp.sum(dn * mid * scale, axis=0, keepdims=True)
        s.dn[r, :] = dmid
        s.k[r, :] = dmid.astype(BF)
        s.c[r, :] = s.y[r, :].astype(BF)

    loop(s.tokens // rb, body)


def out_backward(s, rb):
    def body(i):
        s.hook("outback", i)
        r = rows_of(i, rb)
        d = nt(s.k[r, :], s.wo[...]).astype(BF)
        s.do[r, :] = d
        s.dot[:, r] = d.T

    loop(s.tokens // rb, body)


def out_grads(s, gb):
    def grads(i):
        r = rows_of(i, gb)
        s.wo[r, :] = nn(s.ot[r, :], s.k[...]).astype(BF)

    loop(s.width // gb, grads)


def attend_back(s, i):
    length = s.length
    blocks = length // 128
    pair = lax.div(i, 2) + (s.heads // 4) * lax.rem(i, 2)
    here, natural = rows_of(i, 128), rows_of(pair, 128)
    keep = half_masks(BF)
    left = lax.broadcasted_iota(jnp.int32, (1, 128), 1) < 64
    parts = {}
    for sub in range(2):
        s.hook("back", 2 * i + sub)
        head = 2 * pair + sub
        hr = rows_of(head, 64)
        for m in range(s.micro):
            mr = slice(m * length, (m + 1) * length)
            pr = rows_of((2 * i + sub) * s.micro + m, length)
            dp = nt(s.v[mr, here] * keep[sub], s.do[mr, natural])
            inner = jnp.sum(s.dot[hr, mr].astype(F32) * s.ot[hr, mr].astype(F32), axis=0, keepdims=True)
            ds = s.p[pr, :].astype(F32) * (dp - inner)
            if m == 0:
                s.toep[...] = jnp.zeros_like(s.toep)
            for j in range(blocks):
                at = 128 * (blocks - 1 - j)
                s.toep[:, at : at + length] += ds[128 * j : 128 * (j + 1), :]
            low = ds.astype(BF)
            s.ds[...] = low
            parts[sub, m, 2] = nn(s.kt[hr, mr], low)
            parts[sub, m, 0] = nn(s.ds[...], s.q[mr, here])
            parts[sub, m, 1] = nn(s.p[pr, :], s.do[mr, natural])
            if sub == 1:
                s.k[mr, here] = jnp.where(left, parts[0, m, 0], parts[1, m, 0]).astype(BF)
                s.v[mr, here] = jnp.where(left, parts[0, m, 1], parts[1, m, 1]).astype(BF)
                s.q[mr, here] = jnp.concatenate([parts[0, m, 2], parts[1, m, 2]], axis=0).astype(BF).T
        fold = s.toep[...]
        rows = 64
        while rows >= 8:
            fold = fold[:rows, :] + pltpu.roll(fold[rows:, :], 2 * length - rows, 1)
            rows //= 2
        for r in range(8):
            s.goff[r, pl.ds(head, 1), :] = fold[r : r + 1, :]


def slab(s, chunk, side):
    start = chunk * (4 * s.micro * s.length) + side * s.width
    return pl.ds(pl.multiple_of(start, 128), s.width)


def chunk_grads(s, chunk, gb):
    cols = rows_of(chunk, 256)

    def body(i):
        r = rows_of(i, gb)
        for w, grad in enumerate((s.q, s.k, s.v)):
            g = nn(s.n1t[r, :], grad[:, cols]).astype(BF)
            for side in range(2):
                start = chunk * (4 * s.micro * s.length) + side * s.width + i * gb
                s.p[pl.ds(pl.multiple_of(start, gb & -gb), gb), 128 * w : 128 * (w + 1)] = g[:, 128 * side : 128 * (side + 1)]

    loop(s.width // gb, body)


def table_grad(s):
    total = None
    for r in range(8):
        part = pltpu.roll(s.goff[r, :, :], 127 - r, 1)
        total = part if total is None else total + part
    return contract(total, bucket_classes(s), (1, 1), precision=PRECISE)


def qkv_back_input(s, rb):
    order = [spot(s, pair) for pair in range(s.heads // 2)]

    def body(i):
        s.hook("input", i + 1)
        r = rows_of(i, rb)
        dn = None
        for grad, weight in ((s.q, s.wq), (s.k, s.wk), (s.v, s.wv)):
            part = nt(jnp.concatenate([grad[r, 128 * at : 128 * (at + 1)] for at in order], axis=1), weight[...])
            dn = part if dn is None else dn + part
        x = s.x[r, :].astype(F32)
        scale = lax.rsqrt(jnp.mean(x * x, axis=-1, keepdims=True) + EPSILON)
        gdn = dn * s.gain[0:1, :]
        dot = jnp.mean(gdn * x, axis=-1, keepdims=True)
        s.small[0:1, :] += jnp.sum(dn * x * scale, axis=0, keepdims=True)
        s.x[r, :] = (s.dn[r, :] + scale * gdn - x * (scale * scale * scale * dot)).astype(BF)

    loop(s.tokens // rb, body)


OUT = 3


def ffn_unit(part, which):
    return 4 + 3 * part + which


def place(s):
    s.z, s.row, s.col = lax.axis_index("dp"), lax.axis_index("row"), lax.axis_index("col")
    s.core, s.xx = lax.rem(s.row, 2), lax.div(s.row, 2)
    s.row_p = 2 * s.xx + 1 - s.core
    s.row_x = 2 * (1 - s.xx) + s.core
    s.row_px = 2 * (1 - s.xx) + 1 - s.core
    s.col_y = 1 - s.col
    s.to_p, s.to_x = (s.z, s.row_p, s.col), (s.z, s.row_x, s.col)
    s.to_y, s.to_xy = (s.z, s.row, s.col_y), (s.z, s.row_x, s.col_y)
    s.me = 2 * s.row + s.col
    s.plane = [(s.z, lax.rem(s.row + (i // 2), 4), lax.rem(s.col + i % 2, 2)) for i in range(1, 8)]
    s.stack = [(lax.rem(s.z + i, 4), s.row, s.col) for i in range(1, 4)]
    s.plane_ids = [2 * row + col for _, row, col in s.plane]
    s.stack_ids = [z for z, _, _ in s.stack]
    s.inner = jnp.logical_and(s.z >= 1, s.z <= 2)
    s.outer = jnp.logical_not(s.inner)
    s.z_in, s.z_out = 1 + lax.div(s.z, 2), 3 * lax.div(s.z, 2)


def greet(s):
    barrier = pltpu.get_barrier_semaphore()
    for peer in s.plane + s.stack:
        pl.semaphore_signal(barrier, inc=1, device_id=peer, device_id_type=MESH)
    pl.semaphore_wait(barrier, len(s.plane) + len(s.stack))


def unit_shape(s, unit):
    rb, cb = s.width // 4, s.width // 2
    if unit <= OUT:
        return rb, cb
    part = s.hidden // CHUNKS
    return (part // 4, cb) if (unit - 4) % 3 == 2 else (rb, part // 2)


def span(start, size):
    return pl.ds(pl.multiple_of(start, size & -size), size)


def block(s, unit, row, col, half=None, grad=False):
    rb, cb = unit_shape(s, unit)
    size = rb if half is None else rb // 2
    down = row * rb + (0 if half is None else half * size)
    if unit < OUT and grad:
        return s.p.at[span(unit * (4 * s.micro * s.length) + col * s.width + down, size), 0:cb]
    if unit <= OUT:
        return (s.wq, s.wk, s.wv, s.wo)[unit].at[span(down, size), span(col * cb, cb)]
    part, which = divmod(unit - 4, 3)
    offset = part * (s.hidden // CHUNKS)
    if which == 2:
        return s.wd.at[span(offset + down, size), span(col * cb, cb)]
    return (s.wg, s.wu)[which].at[span(down, size), span(offset + col * cb, cb)]


def send(s, family, unit, kind, src, dst, peer):
    return pltpu.make_async_remote_copy(
        src_ref=src, dst_ref=dst, send_sem=getattr(s, family + "_send").at[unit, kind],
        recv_sem=getattr(s, family + "_recv").at[unit, kind], device_id=peer, device_id_type=MESH)


def own_source(s, unit, half=None):
    rb, cb = unit_shape(s, unit)
    if unit <= OUT:
        piece, start = s.pieces[unit], 0
    else:
        part, which = divmod(unit - 4, 3)
        if which < 2:
            return block(s, unit, s.row, s.col, half)
        piece, start = s.pieces[6], part * rb
    if half is None:
        return piece.at[start : start + rb, :]
    return piece.at[start + half * (rb // 2) : start + (half + 1) * (rb // 2), :]


def own_copies(s, unit):
    rb, cb = unit_shape(s, unit)
    own = block(s, unit, s.row, s.col)
    part, which = divmod(unit - 4, 3)
    if unit <= OUT or which == 2:
        return [pltpu.make_async_copy(own_source(s, unit), own, s.own_sems.at[unit, 0])]
    piece, half = s.pieces[4 + which], cb // 2
    size = s.hidden // 4
    offset = part * (s.hidden // CHUNKS)
    mine = (s.wg, s.wu)[which]
    return [
        pltpu.make_async_copy(
            piece.at[:, i * size + part * half : i * size + (part + 1) * half],
            mine.at[span(s.row * rb, rb), span(offset + s.col * cb + i * half, half)], s.own_sems.at[unit, i])
        for i in range(2)]


def ag_copy(s, unit, kind):
    b = functools.partial(block, s, unit)
    if kind < 3:
        return send(s, "ag", unit, kind, own_source(s, unit), b(s.row, s.col), (s.to_x, s.to_y, s.to_p)[kind])
    there, peer = [
        (b(s.row_x, s.col, 0), s.to_y), (b(s.row, s.col_y, 1), s.to_x), (b(s.row_x, s.col), s.to_p), (b(s.row, s.col_y), s.to_p),
        (b(s.row_x, s.col_y, 0), s.to_p), (b(s.row_x, s.col_y, 1), s.to_p)][kind - 3]
    return send(s, "ag", unit, kind, there, there, peer)


def ag_arrive(s, unit, kind):
    b = functools.partial(block, s, unit)
    where = [
        b(s.row_x, s.col), b(s.row, s.col_y), b(s.row_p, s.col), b(s.row_x, s.col_y, 0), b(s.row_x, s.col_y, 1),
        b(s.row_px, s.col), b(s.row_p, s.col_y), b(s.row_px, s.col_y, 0), b(s.row_px, s.col_y, 1)][kind]
    send(s, "ag", unit, kind, where, where, s.to_p).wait_recv()


def shuffled(unit):
    return unit > OUT and (unit - 4) % 3 < 2


def own_wait(s, unit):
    for copy in own_copies(s, unit):
        copy.wait()


def ag_open(s, unit):
    if shuffled(unit):
        own_wait(s, unit)
    for kind in range(3):
        ag_copy(s, unit, kind).start()


def ag_relay(s, unit):
    for kind in range(2):
        ag_arrive(s, unit, kind)
        ag_copy(s, unit, kind + 3).start()
        ag_copy(s, unit, kind + 5).start()


def ag_corner(s, unit):
    for kind in (3, 4):
        ag_arrive(s, unit, kind)
        ag_copy(s, unit, kind + 4).start()


def ag_near(s, unit):
    if not shuffled(unit):
        own_wait(s, unit)
    for kind in (2, 5):
        ag_arrive(s, unit, kind)


def ag_far(s, unit):
    for kind in (6, 7, 8):
        ag_arrive(s, unit, kind)


def ag_close(s, unit):
    ag_near(s, unit)
    ag_far(s, unit)


def ag_sent(s, unit):
    for kind in range(9):
        ag_copy(s, unit, kind).wait_send()


def swap_copy(s, family, i, peer, slot):
    slots = getattr(s, family + "_slots")
    return pltpu.make_async_remote_copy(
        src_ref=getattr(s, family + "_from"), dst_ref=slots.at[slot], send_sem=getattr(s, family + "_send").at[i],
        recv_sem=getattr(s, family + "_recv").at[slot], device_id=peer, device_id_type=MESH)


def swap_open(s, family, peers, me):
    getattr(s, family + "_slots")[me] = getattr(s, family + "_from")[...]
    for i, peer in enumerate(peers):
        swap_copy(s, family, i, peer, me).start()


def swap_wait(s, family, peers, ids):
    for i, (peer, slot) in enumerate(zip(peers, ids)):
        copy = swap_copy(s, family, i, peer, slot)
        copy.wait_recv()
        copy.wait_send()


def swap_close(s, family, peers, ids):
    swap_wait(s, family, peers, ids)
    slots = getattr(s, family + "_slots")
    total = slots[0]
    for i in range(1, len(ids) + 1):
        total = total + slots[i]
    return total


def small_rows(s):
    return 2 * (s.width // 128) + s.heads


def small_pack(s, table):
    wide = s.width // 128
    for i in range(2):
        for j in range(wide):
            s.near_from[i * wide + j : i * wide + j + 1, :] = s.small[i : i + 1, 128 * j : 128 * (j + 1)]
    s.near_from[2 * wide : 2 * wide + s.heads, 0 : s.buckets] = table


def small_turn(s, unit):
    s.far_from[...] = swap_close(s, "near", s.plane, s.plane_ids)
    swap_open(s, "far", s.stack, s.z)


DIRECT = 2


def quarter(s, unit, row, index):
    rb, cb = unit_shape(s, unit)
    return s.p.at[span(unit * (4 * s.micro * s.length) + s.col * s.width + row * rb + index * (rb // 4), rb // 4), 0:cb]


def rs_copy(s, unit, kind):
    b = functools.partial(block, s, unit, grad=True)
    n = lambda name: getattr(s, f"{name}{unit}")
    low = s.z - 1
    if unit == DIRECT and kind >= 10:
        peer, there = s.stack[(kind - 10) % 3], s.stack_ids[(kind - 10) % 3]
        if kind < 13:
            return send(s, "rs", unit, kind, quarter(s, unit, s.row, there), n("zq").at[kind - 10], peer)
        return send(s, "rs", unit, kind, quarter(s, unit, s.row, s.z), quarter(s, unit, s.row_p, s.z), peer)
    if kind < 4:
        x, col = divmod(kind, 2)
        return send(s, "rs", unit, kind, b(2 * x + 1 - s.core, col), n("pr").at[x, col], s.to_p)
    if kind < 6:
        return send(s, "rs", unit, kind, b(s.row_x, kind - 4, 0), n("xa").at[kind - 4], s.to_x)
    if kind < 8:
        return send(s, "rs", unit, kind, b(2 * (kind - 6) + s.core, s.col_y, 1), n("yb").at[kind - 6], s.to_y)
    up, side = (s.z_out, s.row, s.col), (3 - s.z, s.row, s.col)
    src, dst, peer = [
        lambda: (b(s.row, s.col_y, 0), n("ya"), s.to_y),
        lambda: (b(s.row_x, s.col, 1), n("xb"), s.to_x),
        lambda: (b(s.row, s.col), n("zi"), (s.z_in, s.row, s.col)),
        lambda: (b(s.row, s.col, 1 - low), n("zx"), side),
        lambda: (b(s.row, s.col, low), b(s.row_p, s.col, low), side),
        lambda: (b(s.row, s.col, low), b(s.row_p, s.col, low), up),
        lambda: (b(s.row_p, s.col, 1 - low), b(s.row_p, s.col, 1 - low), up)][kind - 8]()
    return send(s, "rs", unit, kind, src, dst, peer)


def rs_arrive(s, unit, kind):
    b = functools.partial(block, s, unit, grad=True)
    n = lambda name: getattr(s, f"{name}{unit}")
    if unit == DIRECT and kind >= 13:
        where = quarter(s, unit, s.row_p, lax.rem(s.z + 4 - (kind - 12), 4))
    elif unit == DIRECT and kind >= 10:
        where = n("zq").at[kind - 10]
    elif kind < 4:
        where = n("pr").at[kind // 2, kind % 2]
    elif kind < 6:
        where = n("xa").at[kind - 4]
    elif kind < 8:
        where = n("yb").at[kind - 6]
    elif kind < 12:
        where = n(("ya", "xb", "zi", "zx")[kind - 8])
    else:
        where = b(s.row_p, s.col, (2 - s.z, s.z_in - 1, 2 - s.z_in)[kind - 12])
    send(s, "rs", unit, kind, where, where, s.to_p).wait_recv()
    return where


def add_into(target, source):
    rows = target.shape[0]
    step = 32 if rows % 32 == 0 else 16

    def body(i):
        r = rows_of(i, step)
        target[r, :] = target[r, :] + source[r, :]

    loop(rows // step, body)


def rs_1(s, unit):
    for kind in range(4):
        rs_copy(s, unit, kind).start()


def rs_2(s, unit):
    b = functools.partial(block, s, unit, grad=True)
    for kind in range(4):
        x, col = divmod(kind, 2)
        add_into(b(2 * x + s.core, col), rs_arrive(s, unit, kind))
    for kind in range(4, 8):
        rs_copy(s, unit, kind).start()


def rs_3(s, unit):
    b = functools.partial(block, s, unit, grad=True)
    for col in range(2):
        add_into(b(s.row, col, 0), rs_arrive(s, unit, 4 + col))
    rs_copy(s, unit, 8).start()
    for x in range(2):
        add_into(b(2 * x + s.core, s.col, 1), rs_arrive(s, unit, 6 + x))
    rs_copy(s, unit, 9).start()


def rs_4(s, unit):
    b = functools.partial(block, s, unit, grad=True)
    for half in range(2):
        add_into(b(s.row, s.col, half), rs_arrive(s, unit, 8 + half))
    for kind in range(10):
        rs_copy(s, unit, kind).wait_send()
    if unit == DIRECT:
        for kind in (11, 10, 12):
            rs_copy(s, unit, kind).start()
        return

    @pl.when(s.outer)
    def _():
        rs_copy(s, unit, 10).start()


def rs_5(s, unit):
    if unit == DIRECT:
        mine = quarter(s, unit, s.row, s.z)
        for kind in (10, 12, 11):
            add_into(mine, rs_arrive(s, unit, kind))
        for kind in (14, 13, 15):
            rs_copy(s, unit, kind).start()
        quarter(s, unit, s.row_p, s.z)[...] = mine[...]
        return

    @pl.when(s.inner)
    def _():
        add_into(block(s, unit, s.row, s.col, grad=True), rs_arrive(s, unit, 10))
        rs_copy(s, unit, 11).start()


def rs_6(s, unit):
    if unit == DIRECT:
        for kind in (13, 15, 14):
            rs_arrive(s, unit, kind)
        for kind in range(10, 16):
            rs_copy(s, unit, kind).wait_send()
        rs_out(s, unit).start()
        return

    @pl.when(s.inner)
    def _():
        mine = block(s, unit, s.row, s.col, s.z - 1, grad=True)
        add_into(mine, rs_arrive(s, unit, 11))
        rs_copy(s, unit, 12).start()
        rs_copy(s, unit, 13).start()
        done = block(s, unit, s.row_p, s.col, s.z - 1, grad=True)
        done[...] = mine[...]


def rs_7(s, unit):
    @pl.when(s.inner)
    def _():
        rs_arrive(s, unit, 12)
        rs_copy(s, unit, 14).start()
        for kind in (11, 12, 13):
            rs_copy(s, unit, kind).wait_send()

    @pl.when(s.outer)
    def _():
        rs_arrive(s, unit, 13)
        rs_copy(s, unit, 10).wait_send()


def rs_8(s, unit):
    @pl.when(s.inner)
    def _():
        rs_copy(s, unit, 14).wait_send()

    @pl.when(s.outer)
    def _():
        rs_arrive(s, unit, 14)

    rs_out(s, unit).start()


def rs_out(s, unit):
    return pltpu.make_async_copy(block(s, unit, s.row_p, s.col, grad=True), s.unit_out[unit], s.out_sems.at[unit])


PLAN = {
    ("start", 0): (("o", 0), ("o", 1), ("o", 2)),
    ("project", 0): (("r", 0), ("n", 0), ("o", 3)),
    ("project", 1): (("r", 1), ("n", 1)),
    ("project", 2): (("r", 2), ("n", 2), ("o", 4)),
    ("attend", 0): (("c", 0),),
    ("attend", 1): (("o", 5),),
    ("attend", 2): (("r", 3),),
    ("attend", 3): (("c", 1),),
    ("attend", 4): (("o", 6),),
    ("attend", 5): (("c", 2),),
    ("project", 3): (("r", 4), ("o", 7), ("f", 0)),
    ("project", 4): (("f", 1),),
    ("project", 5): (("r", 5), ("f", 2)),
    ("attend", 6): (("o", 8),),
    ("attend", 7): (("c", 3),),
    ("attend", 8): (("r", 6),),
    ("attend", 9): (("c", 4), ("o", 9)),
    ("attend", 10): (("r", 7),),
    ("attend", 11): (("c", 5), ("o", 10)),
    ("feed_in", 0): (("x", 3),),
    ("feed", 0): (("c", 6), ("r", 8), ("o", 11), ("o", 12), ("r", 9), ("x", 4), ("x", 5), ("x", 6)),
    ("feed", 1): (("c", 7), ("r", 10), ("o", 13)),
    ("feed", 4): (("c", 8), ("r", 11)),
    ("feed", 5): (("c", 9), ("r", 12), ("o", 14), (1, 4), (1, 5), (1, 6), ("x", 7), ("x", 8), ("x", 9), ("c", 10), ("o", 15)),
    ("feed", 6): (("r", 13), (2, 4), (2, 5), (2, 6), ("c", 11)),
    ("feed", 9): (("c", 12), ("r", 14)),
    ("feed", 10): (("r", 15), (1, 7), (1, 8), (1, 9), ("x", 10), ("x", 11), ("x", 12), ("c", 13)),
    ("feed", 11): ((3, 4), (2, 7), (2, 8), (2, 9)),
    ("feed", 14): ((3, 5), (3, 6)),
    ("feed", 15): (("c", 14), ("c", 15), (4, 4), (1, 10), (1, 11), ("x", 13), ("x", 14), ("x", 15)),
    ("feed", 16): ((3, 7), (3, 8), (2, 10), (2, 11)),
    ("feed", 19): ((5, 4), (4, 5), (3, 9)),
    ("close", 0): ((4, 6), (4, 7), (4, 8)),
    ("outback", 0): ((6, 4), (1, 12), (1, 13), (1, 14), (1, 15), (5, 5), (3, 10)),
    ("outback", 1): ((2, 12),),
    ("outback", 2): ((3, 11), (2, 13), (2, 14), (5, 6)),
    ("outback", 3): ((7, 4), (4, 9), (2, 15)),
    ("outgrad", 0): ((6, 5), (5, 7), (4, 10)),
    ("outgrad", 1): ((1, 3),),
    ("back", 1): ((8, 4), (6, 6), (5, 8), (4, 11), (3, 12)),
    ("back", 2): ((7, 5), (6, 7), (5, 9), (3, 13), (2, 3)),
    ("back", 3): ((5, 10), (7, 6)),
    ("chunk", 0): ((1, 0), (8, 5), (7, 7), (6, 8), (5, 11), (3, 14), (3, 15), (6, 9), (4, 12)),
    ("back", 5): ((8, 6), (6, 10), (4, 13), (2, 0)),
    ("back", 6): ((8, 7), (7, 8)),
    ("back", 7): ((6, 11), (5, 12), (3, 3)),
    ("chunk", 1): ((1, 1), (8, 8), (7, 9), (7, 10), (5, 13), (4, 14), (4, 15)),
    ("back", 9): ((7, 11), (6, 12), (3, 0), (2, 1)),
    ("back", 10): ((4, 3),),
    ("back", 11): ((8, 9), (8, 10), (6, 13), (5, 14)),
    ("chunk", 2): ((1, 2), (8, 11), (7, 12), (5, 15), (4, 0)),
    ("input", 1): ((7, 13), (2, 2), (6, 14), (3, 1), (5, 3)),
    ("input", 3): ((8, 12), (8, 13), (6, 15)),
    ("input", 4): ((7, 14), (5, 0), (3, 2), (6, 3)),
    ("tail", 0): ((7, 15), (4, 1), (8, 14), (6, 0), (4, 2), ("w", 0), (7, 3), (8, 15), (5, 1), (7, 0), (8, 3), (5, 2), (8, 0), (6, 1), (6, 2), (7, 1), (8, 1)),
}


NAMES = ("wq", "wk", "wv", "wo", "wg", "wu", "wd")
UNITS = OUT + 1 + 3 * CHUNKS
EARLY = tuple(range(4, 12))
ACTS = {"o": ag_open, "r": ag_relay, "c": ag_corner, "x": ag_close, "n": ag_near, "f": ag_far, "w": small_turn, 1: rs_1, 2: rs_2, 3: rs_3, 4: rs_4, 5: rs_5, 6: rs_6, 7: rs_7, 8: rs_8}


def act_all(s, todo):
    for act, unit in todo if s.comm else ():
        ACTS[act](s, unit)


def hook(s, phase, index):
    entries = sorted((number, todo) for (name, number), todo in PLAN.items() if name == phase)
    if not s.comm:
        return
    if isinstance(index, int):
        for number, todo in entries:
            if number == index:
                act_all(s, todo)
        return

    def pick(some):
        if len(some) == 1:
            pl.when(index == some[0][0])(functools.partial(act_all, s, some[0][1]))
        elif some:
            middle = len(some) // 2
            pl.when(index < some[middle][0])(lambda: pick(some[:middle]))
            pl.when(index >= some[middle][0])(lambda: pick(some[middle:]))

    pick(entries)


def gains_in(s):
    for i, gain in enumerate((s.gain_one, s.gain_two)):
        if s.comm:
            s.gain_from[i : i + 1, 0 : gain.shape[1]] = gain[...].astype(F32)
        else:
            s.gain[i : i + 1, :] = gain[...].astype(F32)


def gains_spread(s):
    swap_wait(s, "gain", s.plane, s.plane_ids)
    count = s.gain_one.shape[1]
    wide = (128, s.width)
    lane, spot = lax.broadcasted_iota(jnp.int32, wide, 0), lax.broadcasted_iota(jnp.int32, wide, 1)
    total = None
    for i in range(8):
        part = nn(s.gain_slots[i].astype(BF), jnp.logical_and(spot == lane + count * i, lane < count).astype(BF))
        total = part if total is None else total + part
    s.gain[...] = total


def layer(cfg, *refs):
    s = types.SimpleNamespace(**cfg)
    for name, ref in zip(cfg["names"], refs):
        setattr(s, name, ref)
    s.pieces = [getattr(s, n + "_in") for n in NAMES]
    comm = s.comm
    s.hook = functools.partial(hook, s)
    load_x = pltpu.make_async_copy(s.x_in, s.x, s.io_sems.at[2])
    load_c = pltpu.make_async_copy(s.c_in, s.c, s.io_sems.at[1])
    tiny_loads = [
        pltpu.make_async_copy(getattr(s, name + "_in"), getattr(s, name), s.tiny_sems.at[i])
        for i, name in enumerate(("gain_one", "gain_two", "seg", "bucket", "table"))]
    for copy in tiny_loads + [load_x, load_c]:
        copy.start()
    Q, K, V, O = range(4)
    if comm:
        place(s)
        s.unit_out = [getattr(s, f"unit{u}_out") for u in range(UNITS)]
        greet(s)
        for copy in tiny_loads:
            copy.wait()
        s.gain_from[...] = jnp.zeros_like(s.gain_from)
        gains_in(s)
        swap_open(s, "gain", s.plane, s.me)
        s.hook("start", 0)
        for unit in range(UNITS):
            for copy in own_copies(s, unit):
                copy.start()
    else:
        weights = [pltpu.make_async_copy(piece, getattr(s, n), s.load_sems.at[i]) for i, (n, piece) in enumerate(zip(NAMES, s.pieces))]
        for copy in weights:
            copy.start()
        for copy in tiny_loads:
            copy.wait()
        gains_in(s)
    s.small[...] = jnp.zeros_like(s.small)
    s.near_from[...] = jnp.zeros_like(s.near_from)
    offset_rows(s)
    tw, wt = (s.tokens, s.width), (s.width, s.tokens)
    vm = pltpu.VMEM

    def attention(a, mask, toep):
        s.a, s.mask, s.toep = a, mask, toep
        masks(s)
        load_x.wait()
        if comm:
            gains_spread(s)
        else:
            for copy in weights:
                copy.wait()
        norm_in(s, 256)
        pairs = s.heads // 4
        for part in range(2):
            side = (s.col if part == 0 else s.col_y) if comm else part
            for w in (Q, K, V):
                s.hook("project", 3 * part + w)
                project(s, w, side, s.tokens)
            loop(pairs, functools.partial(attend_pair, s, side, 2 * pairs * part))

    skew = vm((128, 2 * s.length), F32)
    pl.run_scoped(attention, vm(tw, BF), vm((s.micro, s.length, s.length), F32), skew)
    s.n2t = s.vt

    def feed(act, mid, y, ct):
        s.mid, s.y, s.ct = mid, y, ct
        s.dg, s.du = (act.at[:, i * s.ft : (i + 1) * s.ft] for i in range(2))
        s.hid = s.x.at[:, 0 : s.ft]
        load_c.wait()
        s.hook("feed_in", 0)
        out_project(s, 512)

        def step(t):
            ffn_rows(s, t, s.ft, s.rb)
            s.hook("feed", 5 * t + 4)
            if comm:
                for part in range(CHUNKS):

                    @pl.when(t == part)
                    def _():
                        for which in range(3):
                            ag_sent(s, ffn_unit(part, which))

            ffn_grads(s, t, s.ft, s.gb)

        loop(s.hidden // s.ft, step)
        s.hook("close", 0)
        ffn_close(s, 256)

    pl.run_scoped(feed, vm((s.tokens, 2 * s.ft), BF), vm(tw, F32), vm(tw, F32), vm(wt, BF))
    put_y = pltpu.make_async_copy(s.c, s.y_out, s.io_sems.at[0])
    put_x = pltpu.make_async_copy(s.x, s.gi_out, s.io_sems.at[1])
    put_y.start()
    load_x.start()

    def back(toep, ds, goff, *bufs):
        s.toep, s.ds, s.goff = toep, ds, goff
        s.do, s.dot = s.c, s.vt
        for name, ref in zip(s.rs_names, bufs):
            setattr(s, name, ref)
        if comm:
            for peer in [s.to_p, s.to_x, s.to_y] + s.stack:
                pl.semaphore_signal(s.ready, inc=1, device_id=peer, device_id_type=MESH)
            pl.semaphore_wait(s.ready, 6)
        put_y.wait()
        out_backward(s, 256)
        s.hook("outgrad", 0)
        if comm:
            for unit in range(4):
                ag_sent(s, unit)
        out_grads(s, 768)
        s.hook("outgrad", 1)

        def step(i):
            attend_back(s, i)

            @pl.when(lax.rem(i, 2) == 1)
            def _():
                chunk_grads(s, lax.div(i, 2), 768)
                s.hook("chunk", lax.div(i, 2))

        loop(s.heads // 2, step)
        s.hook("input", 0)
        table = table_grad(s)
        load_x.wait()
        qkv_back_input(s, 256)
        put_x.start()
        small_pack(s, table)
        if comm:
            swap_open(s, "near", s.plane, s.me)
            s.hook("tail", 0)
            s.small_sum[...] = swap_close(s, "far", s.stack, s.stack_ids)
            for unit in range(UNITS):
                rs_out(s, unit).wait()
        else:
            s.small_sum[...] = s.near_from[...]
            outs = [pltpu.make_async_copy(getattr(s, n), getattr(s, n + "_out"), s.load_sems.at[i + 3]) for i, n in enumerate(NAMES[3:])]
            for copy in outs:
                copy.start()
            for copy in outs:
                copy.wait()
            half = s.heads // 4
            for w, n in enumerate(NAMES[:3]):
                for pair in range(s.heads // 2):
                    copy = pltpu.make_async_copy(
                        s.p.at[slab(s, pair % half, pair // half), 128 * w : 128 * (w + 1)],
                        getattr(s, n + "_out").at[:, 128 * pair : 128 * (pair + 1)], s.load_sems.at[w])
                    copy.start()
                    copy.wait()

    pl.run_scoped(
        back, skew, vm((s.length, s.length), BF), vm((8, s.heads, 2 * s.length), F32), *[vm(shape, BF) for shape in s.rs_shapes])
    put_small = pltpu.make_async_copy(s.small_sum, s.small_out, s.tiny_sems.at[5])
    put_small.start()
    put_x.wait()
    put_small.wait()


def call_layer(comm, x, c, weights, gains, seg, bucket, table, full):
    tokens, width = x.shape
    micro, length = seg.shape
    heads, buckets = table.shape
    hidden = full[4][1]
    ft, vm, sem = 512, pltpu.VMEM, pltpu.SemaphoreType.DMA
    tw, wt, tiny = (tokens, width), (width, tokens), (2 * (width // 128) + heads, 128)
    s = types.SimpleNamespace(
        comm=comm, tokens=tokens, width=width, micro=micro, length=length, hidden=hidden, heads=heads, buckets=buckets, ft=ft, gb=768, rb=512,
        rs_names=[], rs_shapes=[])
    scratch = dict(
        x=vm(tw, BF), c=vm(tw, BF), **{n: vm(shape, BF) for n, shape in zip(NAMES, full)},
        n1t=vm(wt, BF), q=vm(tw, BF), k=vm(tw, BF), v=vm(tw, BF), kt=vm(wt, BF), vt=vm(wt, BF), ot=vm(wt, BF),
        dn=vm(tw, F32), p=vm((heads * micro * length, length), BF),
        offs=vm((heads, 2 * length), F32), gain=vm((8, width), F32), small=vm((2, width), F32), near_from=vm(tiny, F32),
        turned=vm((1, 2 * length), jnp.int32), io_sems=sem((3,)), load_sems=sem((7,)), out_sems=sem((UNITS,)),
    )
    out_shape = [(tw, BF)] * 2
    if comm:
        scratch.update(
            gain_from=vm((8, 128), F32), far_from=vm(tiny, F32),
            gain_slots=vm((8, 8, 128), F32), near_slots=vm((8, *tiny), F32), far_slots=vm((4, *tiny), F32),
            ag_send=sem((UNITS, 9)), ag_recv=sem((UNITS, 9)), own_sems=sem((UNITS, 2)), rs_send=sem((UNITS, 16)), rs_recv=sem((UNITS, 16)),
            gain_send=sem((7,)), gain_recv=sem((8,)), near_send=sem((7,)), near_recv=sem((8,)), far_send=sem((3,)), far_recv=sem((4,)),
            ready=pltpu.SemaphoreType.REGULAR,
        )
        for unit in range(UNITS):
            rb, cb = unit_shape(s, unit)
            hb = rb // 2
            shapes = dict(pr=(2, 2, rb, cb), xa=(2, hb, cb), yb=(2, hb, cb), ya=(hb, cb), xb=(hb, cb), zi=(rb, cb), zx=(hb, cb))
            if unit == DIRECT:
                del shapes["zi"], shapes["zx"]
                shapes["zq"] = (3, rb // 4, cb)
            for name, shape in shapes.items():
                if unit in EARLY:
                    scratch[f"{name}{unit}"] = vm(shape, BF)
                else:
                    s.rs_names.append(f"{name}{unit}")
                    s.rs_shapes.append(shape)
            out_shape.append(((rb, cb), BF))
        grad_names = [f"unit{unit}_out" for unit in range(UNITS)]
    else:
        out_shape += [(shape, BF) for shape in full]
        grad_names = [n + "_out" for n in NAMES]
    tiny_ins = dict(gain_one=gains[0], gain_two=gains[1], seg=seg, bucket=bucket, table=table)
    for name, array in tiny_ins.items():
        scratch[name] = vm(array.shape, array.dtype)
    scratch.update(tiny_sems=sem((6,)), small_sum=vm(tiny, F32))
    ins = ["x_in", "c_in"] + [n + "_in" for n in NAMES] + [name + "_in" for name in tiny_ins]
    outs = ["y_out", "gi_out"] + grad_names + ["small_out"]
    out_shape.append((tiny, F32))
    names = ins + outs + list(scratch)
    far = pl.BlockSpec(memory_space=pl.ANY)
    params = dict(vmem_limit_bytes=67043328)
    if comm:
        params.update(collective_id=0, has_side_effects=True)

    def body(*refs):
        cfg = dict(vars(s), names=names)
        layer(cfg, *refs)

    return pl.pallas_call(
        body, out_shape=[jax.ShapeDtypeStruct(*o) for o in out_shape],
        in_specs=[far] * len(ins), out_specs=[far] * len(outs), scratch_shapes=list(scratch.values()),
        compiler_params=pltpu.CompilerParams(**params),
    )(x, c, *weights, *gains, seg, bucket, table)


def finish_kernel(cfg, *refs):
    s = types.SimpleNamespace(**cfg)
    srcs, outs = refs[: 3 + UNITS], refs[3 + UNITS : 3 + UNITS + 12]
    bufs = refs[15 + UNITS : 15 + 3 + 2 * UNITS]
    wide, tiny, (in_sems, out_sems) = refs[18 + 2 * UNITS : -5], refs[-5:-2], refs[-2:]
    loads = [pltpu.make_async_copy(src, buf, in_sems.at[i]) for i, (src, buf) in enumerate(zip(srcs, bufs))]
    for i in [len(loads) - 1] + list(range(2, len(loads) - 1)) + [0, 1]:
        loads[i].start()
    row, col = lax.axis_index("row"), lax.axis_index("col")
    y, gi, gain_one, gq, gk, gv, go, table, gain_two, gg, gu, gd = outs
    small, units = bufs[-1], bufs[2:-1]
    stores = []

    def leave(buf, out):
        stores.append(pltpu.make_async_copy(buf, out, out_sems.at[len(stores)]))
        stores[-1].start()

    loads[-1].wait()
    rows = s.width // 128
    at = lax.rem(s.width - s.gain_count * (2 * row + col), s.width)
    for i, out in enumerate((gain_one, gain_two)):
        full = jnp.concatenate([small[i * rows + j : i * rows + j + 1, :] for j in range(rows)], axis=1)
        tiny[i][...] = pltpu.roll(jnp.broadcast_to(full, (8, s.width)), at, 1)[0:1, 0 : s.gain_count]
        leave(tiny[i], out)
    tiny[2][...] = small[2 * rows : 2 * rows + s.heads, 0 : s.buckets]
    leave(tiny[2], table)
    wq, wk, wv, wo, wg, wu, wd = wide
    for unit in range(3):
        loads[2 + unit].wait()
        for w, buf in enumerate((wq, wk, wv)):
            buf[:, 128 * unit : 128 * (unit + 1)] = units[unit][:, 128 * w : 128 * (w + 1)].astype(F32)
    for buf, out in ((wq, gq), (wk, gk), (wv, gv)):
        leave(buf, out)
    loads[2 + OUT].wait()
    wo[...] = units[OUT][...].astype(F32)
    leave(wo, go)
    for which, buf, out in ((0, wg, gg), (1, wu, gu), (2, wd, gd)):
        for part in range(CHUNKS):
            unit = ffn_unit(part, which)
            loads[2 + unit].wait()
            rows, cols = units[unit].shape
            if which == 2:
                buf[part * rows : (part + 1) * rows, :] = units[unit][...].astype(F32)
            else:
                size = buf.shape[1] // 2
                for i in range(2):
                    at = i * size + part * (cols // 2)
                    buf[:, at : at + cols // 2] = units[unit][:, i * (cols // 2) : (i + 1) * (cols // 2)].astype(F32)
        leave(buf, out)
    for i, out in enumerate((y, gi)):
        loads[i].wait()
        leave(bufs[i], out)
    for copy in stores:
        copy.wait()


def finish(arrays, gain_count, heads, buckets, blocks):
    vm, sh = pltpu.VMEM, jax.ShapeDtypeStruct
    far = pl.BlockSpec(memory_space=pl.ANY)
    y, gi = arrays[:2]
    b = [sh(shape, F32) for shape in blocks]
    gain = sh((1, gain_count), F32)
    cfg = dict(width=y.shape[1], gain_count=gain_count, heads=heads, buckets=buckets)
    return pl.pallas_call(
        functools.partial(finish_kernel, cfg),
        out_shape=[sh(y.shape, BF), sh(gi.shape, BF), gain, *b[:4], sh((heads, buckets), F32), gain, *b[4:]],
        in_specs=[far] * len(arrays), out_specs=[far] * 12,
        scratch_shapes=[vm(a.shape, a.dtype) for a in arrays] + [vm(shape, F32) for shape in blocks]
        + [vm(gain.shape, F32)] * 2 + [vm((heads, buckets), F32)]
        + [pltpu.SemaphoreType.DMA((len(arrays),)), pltpu.SemaphoreType.DMA((12,))],
        compiler_params=pltpu.CompilerParams(vmem_limit_bytes=67043328),
    )(*arrays)


def open_block(gathered, row_count, column_count):
    _, rows, columns = gathered.shape
    grid = gathered.reshape(row_count, column_count, rows, columns).transpose(0, 2, 1, 3)
    return grid.reshape(row_count * rows, column_count * columns)


def close_block(full, row_count, column_count):
    rows, columns = full.shape[0] // row_count, full.shape[1] // column_count
    grid = full.reshape(row_count, rows, column_count, columns).transpose(0, 2, 1, 3)
    return grid.reshape(row_count * column_count, rows, columns)


def shards(block_input, segment_ids, bucket, gain_attn, w_query, w_key, w_value, w_out, bias_table, gain_ffn, w_gate, w_up, w_down, cotangent):
    row_count, column_count = lax.axis_size("row"), lax.axis_size("col")
    micro, length, width = block_input.shape
    tokens, gain_count = micro * length, gain_attn.shape[0]
    buckets, heads = bias_table.shape
    pieces = [w_query, w_key, w_value, w_out, w_gate, w_up, w_down]
    full = [(p.shape[0] * row_count, p.shape[1] * column_count) for p in pieces]
    fits = row_count == 4 and column_count == 2 and lax.axis_size("dp") == 4
    x, c = block_input.reshape(tokens, width), cotangent.reshape(tokens, width)
    gains = [gain_attn[None], gain_ffn[None]]
    plane = ("row", "col")
    if fits:
        out = call_layer(True, x, c, pieces, gains, segment_ids, bucket[None], bias_table.T, full)
        y, gi, one, gq, gk, gv, go, table, two, gg, gu, gd = finish(
            out, gain_count, heads, buckets, [p.shape for p in pieces])
        return y.reshape(block_input.shape), gi.reshape(block_input.shape), one[0], gq, gk, gv, go, table.T, two[0], gg, gu, gd
    gains = [lax.all_gather(g, plane, axis=1, tiled=True) for g in gains]
    weights = [open_block(lax.all_gather(p[None], plane, axis=0, tiled=True), row_count, column_count) for p in pieces]
    out = call_layer(False, x, c, weights, gains, segment_ids, bucket[None], bias_table.T, full)
    y, gi, grads, small = out[0], out[1], out[2:9], out[9]
    small = lax.psum(small, ("dp",) + plane)
    grads = [lax.psum_scatter(close_block(g, row_count, column_count), plane, scatter_dimension=0, tiled=True)[0] for g in grads]
    gq, gk, gv, go, gg, gu, gd = (lax.psum(g, "dp").astype(F32) for g in grads)
    mine = (lax.axis_index("row") * column_count + lax.axis_index("col")) * gain_count
    one, two = (lax.dynamic_slice(small[i * (width // 128) : (i + 1) * (width // 128)].reshape(-1), (mine,), (gain_count,)) for i in range(2))
    table = small[2 * (width // 128) :, :buckets].T
    return y.reshape(block_input.shape), gi.reshape(block_input.shape), one, gq, gk, gv, go, table, two, gg, gu, gd


def solution(mesh):
    whole = P(None, ("dp", "row", "col"), None)
    split, gain = P("row", "col"), P(("row", "col"))
    return jax.shard_map(
        shards, mesh=mesh,
        in_specs=(whole, P(None, ("dp", "row", "col")), P(), gain, split, split, split, split, P(), gain, split, split, split, whole),
        out_specs=(whole, whole, gain, split, split, split, split, P(), gain, split, split, split),
        check_vma=False)
```

```python
import functools
import types

import jax
import jax.numpy as jnp
from jax import lax
from jax.experimental import pallas as pl
from jax.experimental.pallas import tpu as pltpu
from jax.sharding import PartitionSpec as P

F32 = jnp.float32
BF = jnp.bfloat16
EPSILON = 1e-06
NEGATIVE = -1e30
PRECISE = lax.Precision.HIGHEST
MESH = pl.DeviceIdType.MESH
CHUNKS = 4
GELU_0 = 0.7978845608028654
GELU_1 = 0.044715


def contract(left, right, dims, **more):
    return lax.dot_general(left, right, ((dims[:1], dims[1:]), ((), ())), preferred_element_type=F32, **more)


def nn(left, right):
    return contract(left, right, (1, 0))


def nt(left, right):
    return contract(left, right, (1, 1))


def rows_of(index, size):
    return pl.ds(pl.multiple_of(index * size, size), size)


def loop(count, body):
    lax.fori_loop(0, count, lambda index, carry: (body(index), carry)[1], 0)


def bucket_classes(s):
    return (s.turned[...] == lax.broadcasted_iota(jnp.int32, (s.buckets, 2 * s.length), 0)).astype(F32)


def offset_rows(s):
    twice = 2 * s.length
    s.turned[...] = jnp.full((1, twice), -1, jnp.int32)
    s.turned[:, 0 : twice - 1] = s.bucket[...]
    flip = (lax.broadcasted_iota(jnp.int32, (128, 128), 0) + lax.broadcasted_iota(jnp.int32, (128, 128), 1) == 127).astype(BF)
    parts = [nn(s.turned[:, i : i + 128].astype(F32).astype(BF), flip) for i in range(0, twice, 128)]
    turned = jnp.concatenate(parts[::-1], axis=1)
    s.turned[...] = pltpu.roll(turned, twice - 1, 1).astype(jnp.int32)
    s.offs[...] = contract(s.table[...], bucket_classes(s), (1, 0), precision=PRECISE)


def masks(s):
    for m in range(s.micro):
        row = s.seg[m : m + 1, :].astype(F32)
        column = jnp.broadcast_to(row, (128, s.length)).T
        for i in range(0, s.length, 128):
            s.mask[m, :, i : i + 128] = jnp.where(column == row[:, i : i + 128], 0.0, NEGATIVE)


def norm_in(s, rb):
    def body(i):
        r = rows_of(i, rb)
        x = s.x[r, :].astype(F32)
        scale = lax.rsqrt(jnp.mean(x * x, axis=-1, keepdims=True) + EPSILON)
        n = (x * scale * s.gain[0:1, :]).astype(BF)
        s.a[r, :] = n
        s.n1t[:, r] = n.T

    loop(s.tokens // rb, body)


def spot(s, pair):
    half = s.heads // 4
    return 2 * (pair % half) + pair // half


def project(s, which, side, rb):
    weight, out, out_t = ((s.wq, s.q, None), (s.wk, s.k, s.kt), (s.wv, s.v, s.vt))[which]
    wide = s.width // 2
    cols = pl.ds(pl.multiple_of(side * wide, 128), wide)

    def body(i):
        r = rows_of(i, rb)
        p = nn(s.a[r, :], weight[:, cols]).astype(BF)
        for j in range(s.heads // 4):
            out[r, rows_of(2 * j + side, 128)] = p[:, 128 * j : 128 * (j + 1)]
        if out_t is not None:
            out_t[cols, r] = p.T

    loop(s.tokens // rb, body)


def half_masks(dtype):
    lane = lax.broadcasted_iota(jnp.int32, (1, 128), 1)
    return [(lane < 64).astype(dtype), (lane >= 64).astype(dtype)]


def attend_pair(s, side, late, j):
    length = s.length
    blocks = length // 128
    pair, i = (s.heads // 4) * side + j, 2 * j + side
    here = rows_of(i, 128)
    keep = half_masks(BF)
    for sub in range(2):
        s.hook("attend", late + 2 * j + sub)
        head = 2 * pair + sub
        hr = rows_of(head, 64)
        row = jnp.broadcast_to(s.offs[pl.ds(head, 1), :], (128, 2 * length))
        s.toep[...] = pltpu.roll(row, 2 * length - 127, 1, stride=1, stride_axis=0)
        for m in range(s.micro):
            mr = slice(m * length, (m + 1) * length)
            scores = nt(s.k[mr, here] * keep[sub], s.q[mr, here])
            bias = jnp.concatenate([s.toep[:, 128 * b : 128 * b + length] for b in reversed(range(blocks))], axis=0)
            scores = scores + bias + s.mask[m]
            e = jnp.exp(scores - jnp.max(scores, axis=0, keepdims=True))
            low = (e * (1.0 / jnp.sum(e, axis=0, keepdims=True))).astype(BF)
            s.p[rows_of((2 * i + sub) * s.micro + m, length), :] = low
            s.ot[hr, mr] = nn(s.vt[hr, mr], low).astype(BF)


def out_project(s, rb):
    def body(i):
        r = rows_of(i, rb)
        mid = s.x[r, :].astype(F32) + nn(s.ot[:, r].T, s.wo[...])
        s.mid[r, :] = mid
        s.y[r, :] = mid
        scale = lax.rsqrt(jnp.mean(mid * mid, axis=-1, keepdims=True) + EPSILON)
        n = (mid * scale * s.gain[1:2, :]).astype(BF)
        s.k[r, :] = n
        s.n2t[:, r] = n.T
        s.dn[r, :] = jnp.zeros_like(mid)
        s.ct[:, r] = s.c[r, :].T

    loop(s.tokens // rb, body)


def ffn_rows(s, tile, ft, rb):
    cols = rows_of(tile, ft)

    def forward(i):
        s.hook("feed", 5 * tile + i)
        r = rows_of(i, rb)
        n = s.k[r, :]
        gate = nn(n, s.wg[:, cols])
        up = nn(n, s.wu[:, cols])
        dh = nt(s.c[r, :], s.wd[cols, :])
        square = gate * gate
        t = jnp.tanh(gate * (GELU_0 + (GELU_0 * GELU_1) * square))
        half = 0.5 + 0.5 * t
        act = gate * half
        slope = half + (0.5 * gate) * (1.0 - t * t) * (GELU_0 + (3.0 * GELU_0 * GELU_1) * square)
        hid = (act * up).astype(BF)
        dg = (dh * up * slope).astype(BF)
        du = (dh * act).astype(BF)
        s.hid[r, :] = hid
        s.dg[r, :] = dg
        s.du[r, :] = du
        s.y[r, :] += nn(hid, s.wd[cols, :])
        s.dn[r, :] += nt(dg, s.wg[:, cols]) + nt(du, s.wu[:, cols])

    loop(s.tokens // rb, forward)


def ffn_grads(s, tile, ft, gb):
    cols = rows_of(tile, ft)

    def grads(i):
        r = rows_of(i, gb)
        s.wd[cols, r] = nn(s.ct[r, :], s.hid[...]).astype(BF).T
        s.wg[r, cols] = nn(s.n2t[r, :], s.dg[...]).astype(BF)
        s.wu[r, cols] = nn(s.n2t[r, :], s.du[...]).astype(BF)

    loop(s.width // gb, grads)


def ffn_close(s, rb):
    def body(i):
        r = rows_of(i, rb)
        mid = s.mid[r, :]
        dn = s.dn[r, :]
        scale = lax.rsqrt(jnp.mean(mid * mid, axis=-1, keepdims=True) + EPSILON)
        gdn = dn * s.gain[1:2, :]
        dot = jnp.mean(gdn * mid, axis=-1, keepdims=True)
        dmid = s.c[r, :].astype(F32) + scale * gdn - mid * (scale * scale * scale * dot)
        s.small[1:2, :] += jnp.sum(dn * mid * scale, axis=0, keepdims=True)
        s.dn[r, :] = dmid
        s.k[r, :] = dmid.astype(BF)
        s.c[r, :] = s.y[r, :].astype(BF)

    loop(s.tokens // rb, body)


def out_backward(s, rb):
    def body(i):
        s.hook("outback", i)
        r = rows_of(i, rb)
        d = nt(s.k[r, :], s.wo[...]).astype(BF)
        s.do[r, :] = d
        s.dot[:, r] = d.T

    loop(s.tokens // rb, body)


def out_grads(s, gb):
    def grads(i):
        r = rows_of(i, gb)
        s.wo[r, :] = nn(s.ot[r, :], s.k[...]).astype(BF)

    loop(s.width // gb, grads)


def attend_back(s, i):
    length = s.length
    blocks = length // 128
    pair = lax.div(i, 2) + (s.heads // 4) * lax.rem(i, 2)
    here, natural = rows_of(i, 128), rows_of(pair, 128)
    keep = half_masks(BF)
    left = lax.broadcasted_iota(jnp.int32, (1, 128), 1) < 64
    parts = {}
    for sub in range(2):
        s.hook("back", 2 * i + sub)
        head = 2 * pair + sub
        hr = rows_of(head, 64)
        for m in range(s.micro):
            mr = slice(m * length, (m + 1) * length)
            pr = rows_of((2 * i + sub) * s.micro + m, length)
            dp = nt(s.v[mr, here] * keep[sub], s.do[mr, natural])
            inner = jnp.sum(s.dot[hr, mr].astype(F32) * s.ot[hr, mr].astype(F32), axis=0, keepdims=True)
            ds = s.p[pr, :].astype(F32) * (dp - inner)
            if m == 0:
                s.toep[...] = jnp.zeros_like(s.toep)
            for j in range(blocks):
                at = 128 * (blocks - 1 - j)
                s.toep[:, at : at + length] += ds[128 * j : 128 * (j + 1), :]
            low = ds.astype(BF)
            s.ds[...] = low
            parts[sub, m, 2] = nn(s.kt[hr, mr], low)
            parts[sub, m, 0] = nn(s.ds[...], s.q[mr, here])
            parts[sub, m, 1] = nn(s.p[pr, :], s.do[mr, natural])
            if sub == 1:
                s.k[mr, here] = jnp.where(left, parts[0, m, 0], parts[1, m, 0]).astype(BF)
                s.v[mr, here] = jnp.where(left, parts[0, m, 1], parts[1, m, 1]).astype(BF)
                s.q[mr, here] = jnp.concatenate([parts[0, m, 2], parts[1, m, 2]], axis=0).astype(BF).T
        fold = s.toep[...]
        rows = 64
        while rows >= 8:
            fold = fold[:rows, :] + pltpu.roll(fold[rows:, :], 2 * length - rows, 1)
            rows //= 2
        for r in range(8):
            s.goff[r, pl.ds(head, 1), :] = fold[r : r + 1, :]


def slab(s, chunk, side):
    start = chunk * (4 * s.micro * s.length) + side * s.width
    return pl.ds(pl.multiple_of(start, 128), s.width)


def chunk_grads(s, chunk, gb):
    cols = rows_of(chunk, 256)

    def body(i):
        r = rows_of(i, gb)
        for w, grad in enumerate((s.q, s.k, s.v)):
            g = nn(s.n1t[r, :], grad[:, cols]).astype(BF)
            for side in range(2):
                start = chunk * (4 * s.micro * s.length) + side * s.width + i * gb
                s.p[pl.ds(pl.multiple_of(start, gb & -gb), gb), 128 * w : 128 * (w + 1)] = g[:, 128 * side : 128 * (side + 1)]

    loop(s.width // gb, body)


def table_grad(s):
    total = None
    for r in range(8):
        part = pltpu.roll(s.goff[r, :, :], 127 - r, 1)
        total = part if total is None else total + part
    return contract(total, bucket_classes(s), (1, 1), precision=PRECISE)


def qkv_back_input(s, rb):
    order = [spot(s, pair) for pair in range(s.heads // 2)]

    def body(i):
        s.hook("input", i + 1)
        r = rows_of(i, rb)
        dn = None
        for grad, weight in ((s.q, s.wq), (s.k, s.wk), (s.v, s.wv)):
            part = nt(jnp.concatenate([grad[r, 128 * at : 128 * (at + 1)] for at in order], axis=1), weight[...])
            dn = part if dn is None else dn + part
        x = s.x[r, :].astype(F32)
        scale = lax.rsqrt(jnp.mean(x * x, axis=-1, keepdims=True) + EPSILON)
        gdn = dn * s.gain[0:1, :]
        dot = jnp.mean(gdn * x, axis=-1, keepdims=True)
        s.small[0:1, :] += jnp.sum(dn * x * scale, axis=0, keepdims=True)
        s.x[r, :] = (s.dn[r, :] + scale * gdn - x * (scale * scale * scale * dot)).astype(BF)

    loop(s.tokens // rb, body)


OUT = 3


def ffn_unit(part, which):
    return 4 + 3 * part + which


def place(s):
    s.z, s.row, s.col = lax.axis_index("dp"), lax.axis_index("row"), lax.axis_index("col")
    s.core, s.xx = lax.rem(s.row, 2), lax.div(s.row, 2)
    s.row_p = 2 * s.xx + 1 - s.core
    s.row_x = 2 * (1 - s.xx) + s.core
    s.row_px = 2 * (1 - s.xx) + 1 - s.core
    s.col_y = 1 - s.col
    s.to_p, s.to_x = (s.z, s.row_p, s.col), (s.z, s.row_x, s.col)
    s.to_y, s.to_xy = (s.z, s.row, s.col_y), (s.z, s.row_x, s.col_y)
    s.me = 2 * s.row + s.col
    s.plane = [(s.z, lax.rem(s.row + (i // 2), 4), lax.rem(s.col + i % 2, 2)) for i in range(1, 8)]
    s.stack = [(lax.rem(s.z + i, 4), s.row, s.col) for i in range(1, 4)]
    s.plane_ids = [2 * row + col for _, row, col in s.plane]
    s.stack_ids = [z for z, _, _ in s.stack]
    s.inner = jnp.logical_and(s.z >= 1, s.z <= 2)
    s.outer = jnp.logical_not(s.inner)
    s.z_in, s.z_out = 1 + lax.div(s.z, 2), 3 * lax.div(s.z, 2)


def greet(s):
    barrier = pltpu.get_barrier_semaphore()
    for peer in s.plane + s.stack:
        pl.semaphore_signal(barrier, inc=1, device_id=peer, device_id_type=MESH)
    pl.semaphore_wait(barrier, len(s.plane) + len(s.stack))


def unit_shape(s, unit):
    rb, cb = s.width // 4, s.width // 2
    if unit <= OUT:
        return rb, cb
    part = s.hidden // CHUNKS
    return (part // 4, cb) if (unit - 4) % 3 == 2 else (rb, part // 2)


def span(start, size):
    return pl.ds(pl.multiple_of(start, size & -size), size)


def block(s, unit, row, col, half=None, grad=False):
    rb, cb = unit_shape(s, unit)
    size = rb if half is None else rb // 2
    down = row * rb + (0 if half is None else half * size)
    if unit < OUT and grad:
        return s.p.at[span(unit * (4 * s.micro * s.length) + col * s.width + down, size), 0:cb]
    if unit <= OUT:
        return (s.wq, s.wk, s.wv, s.wo)[unit].at[span(down, size), span(col * cb, cb)]
    part, which = divmod(unit - 4, 3)
    offset = part * (s.hidden // CHUNKS)
    if which == 2:
        return s.wd.at[span(offset + down, size), span(col * cb, cb)]
    return (s.wg, s.wu)[which].at[span(down, size), span(offset + col * cb, cb)]


def send(s, family, unit, kind, src, dst, peer):
    return pltpu.make_async_remote_copy(
        src_ref=src, dst_ref=dst, send_sem=getattr(s, family + "_send").at[unit, kind],
        recv_sem=getattr(s, family + "_recv").at[unit, kind], device_id=peer, device_id_type=MESH)


def own_source(s, unit, half=None):
    rb, cb = unit_shape(s, unit)
    if unit <= OUT:
        piece, start = s.pieces[unit], 0
    else:
        part, which = divmod(unit - 4, 3)
        if which < 2:
            return block(s, unit, s.row, s.col, half)
        piece, start = s.pieces[6], part * rb
    if half is None:
        return piece.at[start : start + rb, :]
    return piece.at[start + half * (rb // 2) : start + (half + 1) * (rb // 2), :]


def own_copies(s, unit):
    rb, cb = unit_shape(s, unit)
    own = block(s, unit, s.row, s.col)
    part, which = divmod(unit - 4, 3)
    if unit <= OUT or which == 2:
        return [pltpu.make_async_copy(own_source(s, unit), own, s.own_sems.at[unit, 0])]
    piece, half = s.pieces[4 + which], cb // 2
    size = s.hidden // 4
    offset = part * (s.hidden // CHUNKS)
    mine = (s.wg, s.wu)[which]
    return [
        pltpu.make_async_copy(
            piece.at[:, i * size + part * half : i * size + (part + 1) * half],
            mine.at[span(s.row * rb, rb), span(offset + s.col * cb + i * half, half)], s.own_sems.at[unit, i])
        for i in range(2)]


def ag_copy(s, unit, kind):
    b = functools.partial(block, s, unit)
    if kind < 3:
        return send(s, "ag", unit, kind, own_source(s, unit), b(s.row, s.col), (s.to_x, s.to_y, s.to_p)[kind])
    there, peer = [
        (b(s.row_x, s.col, 0), s.to_y), (b(s.row, s.col_y, 1), s.to_x), (b(s.row_x, s.col), s.to_p), (b(s.row, s.col_y), s.to_p),
        (b(s.row_x, s.col_y, 0), s.to_p), (b(s.row_x, s.col_y, 1), s.to_p)][kind - 3]
    return send(s, "ag", unit, kind, there, there, peer)


def ag_arrive(s, unit, kind):
    b = functools.partial(block, s, unit)
    where = [
        b(s.row_x, s.col), b(s.row, s.col_y), b(s.row_p, s.col), b(s.row_x, s.col_y, 0), b(s.row_x, s.col_y, 1),
        b(s.row_px, s.col), b(s.row_p, s.col_y), b(s.row_px, s.col_y, 0), b(s.row_px, s.col_y, 1)][kind]
    send(s, "ag", unit, kind, where, where, s.to_p).wait_recv()


def shuffled(unit):
    return unit > OUT and (unit - 4) % 3 < 2


def own_wait(s, unit):
    for copy in own_copies(s, unit):
        copy.wait()


def ag_open(s, unit):
    if shuffled(unit):
        own_wait(s, unit)
    for kind in range(3):
        ag_copy(s, unit, kind).start()


def ag_relay(s, unit):
    for kind in range(2):
        ag_arrive(s, unit, kind)
        ag_copy(s, unit, kind + 3).start()
        ag_copy(s, unit, kind + 5).start()


def ag_corner(s, unit):
    for kind in (3, 4):
        ag_arrive(s, unit, kind)
        ag_copy(s, unit, kind + 4).start()


def ag_near(s, unit):
    if not shuffled(unit):
        own_wait(s, unit)
    for kind in (2, 5):
        ag_arrive(s, unit, kind)


def ag_far(s, unit):
    for kind in (6, 7, 8):
        ag_arrive(s, unit, kind)


def ag_close(s, unit):
    ag_near(s, unit)
    ag_far(s, unit)


def ag_sent(s, unit):
    for kind in range(9):
        ag_copy(s, unit, kind).wait_send()


def swap_copy(s, family, i, peer, slot):
    slots = getattr(s, family + "_slots")
    return pltpu.make_async_remote_copy(
        src_ref=getattr(s, family + "_from"), dst_ref=slots.at[slot], send_sem=getattr(s, family + "_send").at[i],
        recv_sem=getattr(s, family + "_recv").at[slot], device_id=peer, device_id_type=MESH)


def swap_open(s, family, peers, me):
    getattr(s, family + "_slots")[me] = getattr(s, family + "_from")[...]
    for i, peer in enumerate(peers):
        swap_copy(s, family, i, peer, me).start()


def swap_wait(s, family, peers, ids):
    for i, (peer, slot) in enumerate(zip(peers, ids)):
        copy = swap_copy(s, family, i, peer, slot)
        copy.wait_recv()
        copy.wait_send()


def swap_close(s, family, peers, ids):
    swap_wait(s, family, peers, ids)
    slots = getattr(s, family + "_slots")
    total = slots[0]
    for i in range(1, len(ids) + 1):
        total = total + slots[i]
    return total


def small_rows(s):
    return 2 * (s.width // 128) + s.heads


def small_pack(s, table):
    wide = s.width // 128
    for i in range(2):
        for j in range(wide):
            s.near_from[i * wide + j : i * wide + j + 1, :] = s.small[i : i + 1, 128 * j : 128 * (j + 1)]
    s.near_from[2 * wide : 2 * wide + s.heads, 0 : s.buckets] = table


def small_turn(s, unit):
    s.far_from[...] = swap_close(s, "near", s.plane, s.plane_ids)
    swap_open(s, "far", s.stack, s.z)


DIRECT = 2


def quarter(s, unit, row, index):
    rb, cb = unit_shape(s, unit)
    return s.p.at[span(unit * (4 * s.micro * s.length) + s.col * s.width + row * rb + index * (rb // 4), rb // 4), 0:cb]


def rs_copy(s, unit, kind):
    b = functools.partial(block, s, unit, grad=True)
    n = lambda name: getattr(s, f"{name}{unit}")
    low = s.z - 1
    if unit == DIRECT and kind >= 10:
        peer, there = s.stack[(kind - 10) % 3], s.stack_ids[(kind - 10) % 3]
        if kind < 13:
            return send(s, "rs", unit, kind, quarter(s, unit, s.row, there), n("zq").at[kind - 10], peer)
        return send(s, "rs", unit, kind, quarter(s, unit, s.row, s.z), quarter(s, unit, s.row_p, s.z), peer)
    if kind < 4:
        x, col = divmod(kind, 2)
        return send(s, "rs", unit, kind, b(2 * x + 1 - s.core, col), n("pr").at[x, col], s.to_p)
    if kind < 6:
        return send(s, "rs", unit, kind, b(s.row_x, kind - 4, 0), n("xa").at[kind - 4], s.to_x)
    if kind < 8:
        return send(s, "rs", unit, kind, b(2 * (kind - 6) + s.core, s.col_y, 1), n("yb").at[kind - 6], s.to_y)
    up, side = (s.z_out, s.row, s.col), (3 - s.z, s.row, s.col)
    src, dst, peer = [
        lambda: (b(s.row, s.col_y, 0), n("ya"), s.to_y),
        lambda: (b(s.row_x, s.col, 1), n("xb"), s.to_x),
        lambda: (b(s.row, s.col), n("zi"), (s.z_in, s.row, s.col)),
        lambda: (b(s.row, s.col, 1 - low), n("zx"), side),
        lambda: (b(s.row, s.col, low), b(s.row_p, s.col, low), side),
        lambda: (b(s.row, s.col, low), b(s.row_p, s.col, low), up),
        lambda: (b(s.row_p, s.col, 1 - low), b(s.row_p, s.col, 1 - low), up)][kind - 8]()
    return send(s, "rs", unit, kind, src, dst, peer)


def rs_arrive(s, unit, kind):
    b = functools.partial(block, s, unit, grad=True)
    n = lambda name: getattr(s, f"{name}{unit}")
    if unit == DIRECT and kind >= 13:
        where = quarter(s, unit, s.row_p, lax.rem(s.z + 4 - (kind - 12), 4))
    elif unit == DIRECT and kind >= 10:
        where = n("zq").at[kind - 10]
    elif kind < 4:
        where = n("pr").at[kind // 2, kind % 2]
    elif kind < 6:
        where = n("xa").at[kind - 4]
    elif kind < 8:
        where = n("yb").at[kind - 6]
    elif kind < 12:
        where = n(("ya", "xb", "zi", "zx")[kind - 8])
    else:
        where = b(s.row_p, s.col, (2 - s.z, s.z_in - 1, 2 - s.z_in)[kind - 12])
    send(s, "rs", unit, kind, where, where, s.to_p).wait_recv()
    return where


def add_into(target, source):
    rows = target.shape[0]
    step = 32 if rows % 32 == 0 else 16

    def body(i):
        r = rows_of(i, step)
        target[r, :] = target[r, :] + source[r, :]

    loop(rows // step, body)


def rs_1(s, unit):
    for kind in range(4):
        rs_copy(s, unit, kind).start()


def rs_2(s, unit):
    b = functools.partial(block, s, unit, grad=True)
    for kind in range(4):
        x, col = divmod(kind, 2)
        add_into(b(2 * x + s.core, col), rs_arrive(s, unit, kind))
    for kind in range(4, 8):
        rs_copy(s, unit, kind).start()


def rs_3(s, unit):
    b = functools.partial(block, s, unit, grad=True)
    for col in range(2):
        add_into(b(s.row, col, 0), rs_arrive(s, unit, 4 + col))
    rs_copy(s, unit, 8).start()
    for x in range(2):
        add_into(b(2 * x + s.core, s.col, 1), rs_arrive(s, unit, 6 + x))
    rs_copy(s, unit, 9).start()


def rs_4(s, unit):
    b = functools.partial(block, s, unit, grad=True)
    for half in range(2):
        add_into(b(s.row, s.col, half), rs_arrive(s, unit, 8 + half))
    for kind in range(10):
        rs_copy(s, unit, kind).wait_send()
    if unit == DIRECT:
        for kind in (11, 10, 12):
            rs_copy(s, unit, kind).start()
        return

    @pl.when(s.outer)
    def _():
        rs_copy(s, unit, 10).start()


def rs_5(s, unit):
    if unit == DIRECT:
        mine = quarter(s, unit, s.row, s.z)
        for kind in (10, 12, 11):
            add_into(mine, rs_arrive(s, unit, kind))
        for kind in (14, 13, 15):
            rs_copy(s, unit, kind).start()
        quarter(s, unit, s.row_p, s.z)[...] = mine[...]
        return

    @pl.when(s.inner)
    def _():
        add_into(block(s, unit, s.row, s.col, grad=True), rs_arrive(s, unit, 10))
        rs_copy(s, unit, 11).start()


def rs_6(s, unit):
    if unit == DIRECT:
        for kind in (13, 15, 14):
            rs_arrive(s, unit, kind)
        for kind in range(10, 16):
            rs_copy(s, unit, kind).wait_send()
        rs_out(s, unit).start()
        return

    @pl.when(s.inner)
    def _():
        mine = block(s, unit, s.row, s.col, s.z - 1, grad=True)
        add_into(mine, rs_arrive(s, unit, 11))
        rs_copy(s, unit, 12).start()
        rs_copy(s, unit, 13).start()
        done = block(s, unit, s.row_p, s.col, s.z - 1, grad=True)
        done[...] = mine[...]


def rs_7(s, unit):
    @pl.when(s.inner)
    def _():
        rs_arrive(s, unit, 12)
        rs_copy(s, unit, 14).start()
        for kind in (11, 12, 13):
            rs_copy(s, unit, kind).wait_send()

    @pl.when(s.outer)
    def _():
        rs_arrive(s, unit, 13)
        rs_copy(s, unit, 10).wait_send()


def rs_8(s, unit):
    @pl.when(s.inner)
    def _():
        rs_copy(s, unit, 14).wait_send()

    @pl.when(s.outer)
    def _():
        rs_arrive(s, unit, 14)

    rs_out(s, unit).start()


def rs_out(s, unit):
    return pltpu.make_async_copy(block(s, unit, s.row_p, s.col, grad=True), s.unit_out[unit], s.out_sems.at[unit])


PLAN = {
    ("start", 0): (("o", 0), ("o", 1), ("o", 2)),
    ("project", 0): (("r", 0), ("n", 0), ("o", 3)),
    ("project", 1): (("r", 1), ("n", 1)),
    ("project", 2): (("r", 2), ("n", 2), ("c", 0), ("o", 4)),
    ("attend", 1): (("o", 5),),
    ("attend", 2): (("r", 3),),
    ("attend", 3): (("c", 1),),
    ("attend", 4): (("c", 2), ("o", 6)),
    ("attend", 5): (("o", 7),),
    ("project", 3): (("r", 4), ("f", 0)),
    ("project", 4): (("f", 1),),
    ("project", 5): (("r", 5), ("f", 2)),
    ("attend", 6): (("c", 3), ("o", 8)),
    ("attend", 8): (("r", 6),),
    ("attend", 9): (("o", 9), ("r", 7)),
    ("attend", 10): (("c", 4),),
    ("attend", 11): (("c", 5), ("o", 10)),
    ("feed_in", 0): (("o", 11), ("x", 3), ("r", 8)),
    ("feed", 0): (("c", 6), ("r", 9), ("x", 4), ("x", 5), ("x", 6), ("c", 7), ("o", 12)),
    ("feed", 1): (("r", 10), ("o", 13)),
    ("feed", 4): (("c", 8), ("c", 9), ("r", 11), ("o", 14)),
    ("feed", 5): (("r", 12), (1, 4), (1, 5), (1, 6), ("x", 7), ("x", 8), ("x", 9)),
    ("feed", 6): (("c", 10), ("r", 13), ("o", 15), (2, 4), (2, 5), (2, 6), ("c", 11)),
    ("feed", 9): (("r", 14),),
    ("feed", 10): (("c", 12), ("c", 13), (1, 7), (1, 8), (1, 9), ("x", 10), ("x", 11), ("x", 12), ("r", 15)),
    ("feed", 11): ((3, 4), (2, 7), (2, 8), (2, 9)),
    ("feed", 14): ((3, 5), (3, 6)),
    ("feed", 15): (("c", 14), ("c", 15), (1, 10), (1, 11), ("x", 13), ("x", 14), ("x", 15), (4, 4)),
    ("feed", 16): ((3, 7), (2, 10), (2, 11), (3, 8)),
    ("feed", 19): ((5, 4), (4, 5), (3, 9)),
    ("close", 0): ((4, 6), (4, 7)),
    ("outback", 0): ((6, 4), (3, 10), (1, 12), (1, 13), (1, 14), (1, 15), (5, 5)),
    ("outback", 1): ((3, 11), (2, 12), (2, 13)),
    ("outback", 2): ((5, 6), (4, 8), (2, 14), (2, 15), (7, 4), (4, 9)),
    ("outback", 3): ((6, 5),),
    ("outgrad", 0): ((5, 7), (4, 10)),
    ("outgrad", 1): ((1, 3), (6, 6), (4, 11)),
    ("back", 1): ((8, 4), (7, 5), (5, 8), (3, 12), (2, 3)),
    ("back", 2): ((6, 7), (5, 9), (3, 13), (7, 6)),
    ("back", 3): ((8, 5), (6, 8), (5, 10), (3, 14)),
    ("chunk", 0): ((1, 0), (8, 6), (7, 7), (6, 9), (5, 11), (4, 12), (3, 15)),
    ("back", 5): ((7, 8), (6, 10), (2, 0)),
    ("back", 6): ((3, 3), (8, 7), (7, 9)),
    ("back", 7): ((6, 11), (5, 12), (4, 13), (4, 14)),
    ("chunk", 1): ((1, 1), (8, 8), (8, 9), (7, 10), (4, 15)),
    ("back", 9): ((7, 11), (6, 12), (5, 13), (3, 0), (2, 1)),
    ("back", 10): ((4, 3), (8, 10), (5, 14)),
    ("back", 11): ((8, 11), (7, 12)),
    ("chunk", 2): ((1, 2), (6, 13), (6, 14), (5, 15), (4, 0)),
    ("input", 1): ((8, 12), (5, 3), (3, 1)),
    ("input", 2): ((2, 2),),
    ("input", 3): ((7, 13),),
    ("input", 4): ((7, 14), (6, 15), (5, 0), (4, 1)),
    ("tail", 0): ((6, 3), (8, 13), (3, 2), (8, 14), (7, 15), (6, 0), (5, 1), (7, 3), (4, 2), ("w", 0), (8, 15), (7, 0), (6, 1), (8, 3), (8, 0), (5, 2), (7, 1), (8, 1), (6, 2)),
}


NAMES = ("wq", "wk", "wv", "wo", "wg", "wu", "wd")
UNITS = OUT + 1 + 3 * CHUNKS
EARLY = tuple(range(4, 12))
ACTS = {"o": ag_open, "r": ag_relay, "c": ag_corner, "x": ag_close, "n": ag_near, "f": ag_far, "w": small_turn, 1: rs_1, 2: rs_2, 3: rs_3, 4: rs_4, 5: rs_5, 6: rs_6, 7: rs_7, 8: rs_8}


def act_all(s, todo):
    for act, unit in todo if s.comm else ():
        ACTS[act](s, unit)


def hook(s, phase, index):
    entries = sorted((number, todo) for (name, number), todo in PLAN.items() if name == phase)
    if not s.comm:
        return
    if isinstance(index, int):
        for number, todo in entries:
            if number == index:
                act_all(s, todo)
        return

    def pick(some):
        if len(some) == 1:
            pl.when(index == some[0][0])(functools.partial(act_all, s, some[0][1]))
        elif some:
            middle = len(some) // 2
            pl.when(index < some[middle][0])(lambda: pick(some[:middle]))
            pl.when(index >= some[middle][0])(lambda: pick(some[middle:]))

    pick(entries)


def gains_in(s):
    for i, gain in enumerate((s.gain_one, s.gain_two)):
        if s.comm:
            s.gain_from[i : i + 1, 0 : gain.shape[1]] = gain[...].astype(F32)
        else:
            s.gain[i : i + 1, :] = gain[...].astype(F32)


def gains_spread(s):
    swap_wait(s, "gain", s.plane, s.plane_ids)
    count = s.gain_one.shape[1]
    wide = (128, s.width)
    lane, spot = lax.broadcasted_iota(jnp.int32, wide, 0), lax.broadcasted_iota(jnp.int32, wide, 1)
    total = None
    for i in range(8):
        part = nn(s.gain_slots[i].astype(BF), jnp.logical_and(spot == lane + count * i, lane < count).astype(BF))
        total = part if total is None else total + part
    s.gain[...] = total


def layer(cfg, *refs):
    s = types.SimpleNamespace(**cfg)
    for name, ref in zip(cfg["names"], refs):
        setattr(s, name, ref)
    s.pieces = [getattr(s, n + "_in") for n in NAMES]
    comm = s.comm
    s.hook = functools.partial(hook, s)
    load_x = pltpu.make_async_copy(s.x_in, s.x, s.io_sems.at[2])
    load_c = pltpu.make_async_copy(s.c_in, s.c, s.io_sems.at[1])
    tiny_loads = [
        pltpu.make_async_copy(getattr(s, name + "_in"), getattr(s, name), s.tiny_sems.at[i])
        for i, name in enumerate(("gain_one", "gain_two", "seg", "bucket", "table"))]
    for copy in tiny_loads + [load_x, load_c]:
        copy.start()
    Q, K, V, O = range(4)
    if comm:
        place(s)
        s.unit_out = [getattr(s, f"unit{u}_out") for u in range(UNITS)]
        greet(s)
        for copy in tiny_loads:
            copy.wait()
        s.gain_from[...] = jnp.zeros_like(s.gain_from)
        gains_in(s)
        swap_open(s, "gain", s.plane, s.me)
        s.hook("start", 0)
        for unit in range(UNITS):
            for copy in own_copies(s, unit):
                copy.start()
    else:
        weights = [pltpu.make_async_copy(piece, getattr(s, n), s.load_sems.at[i]) for i, (n, piece) in enumerate(zip(NAMES, s.pieces))]
        for copy in weights:
            copy.start()
        for copy in tiny_loads:
            copy.wait()
        gains_in(s)
    s.small[...] = jnp.zeros_like(s.small)
    s.near_from[...] = jnp.zeros_like(s.near_from)
    offset_rows(s)
    tw, wt = (s.tokens, s.width), (s.width, s.tokens)
    vm = pltpu.VMEM

    def attention(a, mask, toep):
        s.a, s.mask, s.toep = a, mask, toep
        masks(s)
        load_x.wait()
        if comm:
            gains_spread(s)
        else:
            for copy in weights:
                copy.wait()
        norm_in(s, 256)
        pairs = s.heads // 4
        for part in range(2):
            side = (s.col if part == 0 else s.col_y) if comm else part
            for w in (Q, K, V):
                s.hook("project", 3 * part + w)
                project(s, w, side, s.tokens)
            loop(pairs, functools.partial(attend_pair, s, side, 2 * pairs * part))

    skew = vm((128, 2 * s.length), F32)
    pl.run_scoped(attention, vm(tw, BF), vm((s.micro, s.length, s.length), F32), skew)
    s.n2t = s.vt

    def feed(act, mid, y, ct):
        s.mid, s.y, s.ct = mid, y, ct
        s.dg, s.du = (act.at[:, i * s.ft : (i + 1) * s.ft] for i in range(2))
        s.hid = s.x.at[:, 0 : s.ft]
        load_c.wait()
        s.hook("feed_in", 0)
        out_project(s, 512)

        def step(t):
            ffn_rows(s, t, s.ft, s.rb)
            s.hook("feed", 5 * t + 4)
            if comm:
                for part in range(CHUNKS):

                    @pl.when(t == part)
                    def _():
                        for which in range(3):
                            ag_sent(s, ffn_unit(part, which))

            ffn_grads(s, t, s.ft, s.gb)

        loop(s.hidden // s.ft, step)
        s.hook("close", 0)
        ffn_close(s, 256)

    pl.run_scoped(feed, vm((s.tokens, 2 * s.ft), BF), vm(tw, F32), vm(tw, F32), vm(wt, BF))
    put_y = pltpu.make_async_copy(s.c, s.y_out, s.io_sems.at[0])
    put_x = pltpu.make_async_copy(s.x, s.gi_out, s.io_sems.at[1])
    put_y.start()
    load_x.start()

    def back(toep, ds, goff, *bufs):
        s.toep, s.ds, s.goff = toep, ds, goff
        s.do, s.dot = s.c, s.vt
        for name, ref in zip(s.rs_names, bufs):
            setattr(s, name, ref)
        if comm:
            for peer in [s.to_p, s.to_x, s.to_y] + s.stack:
                pl.semaphore_signal(s.ready, inc=1, device_id=peer, device_id_type=MESH)
            pl.semaphore_wait(s.ready, 6)
        put_y.wait()
        out_backward(s, 256)
        s.hook("outgrad", 0)
        if comm:
            for unit in range(4):
                ag_sent(s, unit)
        out_grads(s, 768)
        s.hook("outgrad", 1)

        def step(i):
            attend_back(s, i)

            @pl.when(lax.rem(i, 2) == 1)
            def _():
                chunk_grads(s, lax.div(i, 2), 768)
                s.hook("chunk", lax.div(i, 2))

        loop(s.heads // 2, step)
        s.hook("input", 0)
        table = table_grad(s)
        load_x.wait()
        qkv_back_input(s, 256)
        put_x.start()
        small_pack(s, table)
        if comm:
            swap_open(s, "near", s.plane, s.me)
            s.hook("tail", 0)
            s.small_sum[...] = swap_close(s, "far", s.stack, s.stack_ids)
            for unit in range(UNITS):
                rs_out(s, unit).wait()
        else:
            s.small_sum[...] = s.near_from[...]
            outs = [pltpu.make_async_copy(getattr(s, n), getattr(s, n + "_out"), s.load_sems.at[i + 3]) for i, n in enumerate(NAMES[3:])]
            for copy in outs:
                copy.start()
            for copy in outs:
                copy.wait()
            half = s.heads // 4
            for w, n in enumerate(NAMES[:3]):
                for pair in range(s.heads // 2):
                    copy = pltpu.make_async_copy(
                        s.p.at[slab(s, pair % half, pair // half), 128 * w : 128 * (w + 1)],
                        getattr(s, n + "_out").at[:, 128 * pair : 128 * (pair + 1)], s.load_sems.at[w])
                    copy.start()
                    copy.wait()

    pl.run_scoped(
        back, skew, vm((s.length, s.length), BF), vm((8, s.heads, 2 * s.length), F32), *[vm(shape, BF) for shape in s.rs_shapes])
    put_small = pltpu.make_async_copy(s.small_sum, s.small_out, s.tiny_sems.at[5])
    put_small.start()
    put_x.wait()
    put_small.wait()


def call_layer(comm, x, c, weights, gains, seg, bucket, table, full):
    tokens, width = x.shape
    micro, length = seg.shape
    heads, buckets = table.shape
    hidden = full[4][1]
    ft, vm, sem = 512, pltpu.VMEM, pltpu.SemaphoreType.DMA
    tw, wt, tiny = (tokens, width), (width, tokens), (2 * (width // 128) + heads, 128)
    s = types.SimpleNamespace(
        comm=comm, tokens=tokens, width=width, micro=micro, length=length, hidden=hidden, heads=heads, buckets=buckets, ft=ft, gb=768, rb=512,
        rs_names=[], rs_shapes=[])
    scratch = dict(
        x=vm(tw, BF), c=vm(tw, BF), **{n: vm(shape, BF) for n, shape in zip(NAMES, full)},
        n1t=vm(wt, BF), q=vm(tw, BF), k=vm(tw, BF), v=vm(tw, BF), kt=vm(wt, BF), vt=vm(wt, BF), ot=vm(wt, BF),
        dn=vm(tw, F32), p=vm((heads * micro * length, length), BF),
        offs=vm((heads, 2 * length), F32), gain=vm((8, width), F32), small=vm((2, width), F32), near_from=vm(tiny, F32),
        turned=vm((1, 2 * length), jnp.int32), io_sems=sem((3,)), load_sems=sem((7,)), out_sems=sem((UNITS,)),
    )
    out_shape = [(tw, BF)] * 2
    if comm:
        scratch.update(
            gain_from=vm((8, 128), F32), far_from=vm(tiny, F32),
            gain_slots=vm((8, 8, 128), F32), near_slots=vm((8, *tiny), F32), far_slots=vm((4, *tiny), F32),
            ag_send=sem((UNITS, 9)), ag_recv=sem((UNITS, 9)), own_sems=sem((UNITS, 2)), rs_send=sem((UNITS, 16)), rs_recv=sem((UNITS, 16)),
            gain_send=sem((7,)), gain_recv=sem((8,)), near_send=sem((7,)), near_recv=sem((8,)), far_send=sem((3,)), far_recv=sem((4,)),
            ready=pltpu.SemaphoreType.REGULAR,
        )
        for unit in range(UNITS):
            rb, cb = unit_shape(s, unit)
            hb = rb // 2
            shapes = dict(pr=(2, 2, rb, cb), xa=(2, hb, cb), yb=(2, hb, cb), ya=(hb, cb), xb=(hb, cb), zi=(rb, cb), zx=(hb, cb))
            if unit == DIRECT:
                del shapes["zi"], shapes["zx"]
                shapes["zq"] = (3, rb // 4, cb)
            for name, shape in shapes.items():
                if unit in EARLY:
                    scratch[f"{name}{unit}"] = vm(shape, BF)
                else:
                    s.rs_names.append(f"{name}{unit}")
                    s.rs_shapes.append(shape)
            out_shape.append(((rb, cb), BF))
        grad_names = [f"unit{unit}_out" for unit in range(UNITS)]
    else:
        out_shape += [(shape, BF) for shape in full]
        grad_names = [n + "_out" for n in NAMES]
    tiny_ins = dict(gain_one=gains[0], gain_two=gains[1], seg=seg, bucket=bucket, table=table)
    for name, array in tiny_ins.items():
        scratch[name] = vm(array.shape, array.dtype)
    scratch.update(tiny_sems=sem((6,)), small_sum=vm(tiny, F32))
    ins = ["x_in", "c_in"] + [n + "_in" for n in NAMES] + [name + "_in" for name in tiny_ins]
    outs = ["y_out", "gi_out"] + grad_names + ["small_out"]
    out_shape.append((tiny, F32))
    names = ins + outs + list(scratch)
    far = pl.BlockSpec(memory_space=pl.ANY)
    params = dict(vmem_limit_bytes=67043328)
    if comm:
        params.update(collective_id=0, has_side_effects=True)

    def body(*refs):
        cfg = dict(vars(s), names=names)
        layer(cfg, *refs)

    return pl.pallas_call(
        body, out_shape=[jax.ShapeDtypeStruct(*o) for o in out_shape],
        in_specs=[far] * len(ins), out_specs=[far] * len(outs), scratch_shapes=list(scratch.values()),
        compiler_params=pltpu.CompilerParams(**params),
    )(x, c, *weights, *gains, seg, bucket, table)


def finish_kernel(cfg, *refs):
    s = types.SimpleNamespace(**cfg)
    srcs, outs = refs[: 3 + UNITS], refs[3 + UNITS : 3 + UNITS + 12]
    bufs = refs[15 + UNITS : 15 + 3 + 2 * UNITS]
    wide, tiny, (in_sems, out_sems) = refs[18 + 2 * UNITS : -5], refs[-5:-2], refs[-2:]
    loads = [pltpu.make_async_copy(src, buf, in_sems.at[i]) for i, (src, buf) in enumerate(zip(srcs, bufs))]
    for i in [len(loads) - 1] + list(range(2, len(loads) - 1)) + [0, 1]:
        loads[i].start()
    row, col = lax.axis_index("row"), lax.axis_index("col")
    y, gi, gain_one, gq, gk, gv, go, table, gain_two, gg, gu, gd = outs
    small, units = bufs[-1], bufs[2:-1]
    stores = []

    def leave(buf, out):
        stores.append(pltpu.make_async_copy(buf, out, out_sems.at[len(stores)]))
        stores[-1].start()

    loads[-1].wait()
    rows = s.width // 128
    at = lax.rem(s.width - s.gain_count * (2 * row + col), s.width)
    for i, out in enumerate((gain_one, gain_two)):
        full = jnp.concatenate([small[i * rows + j : i * rows + j + 1, :] for j in range(rows)], axis=1)
        tiny[i][...] = pltpu.roll(jnp.broadcast_to(full, (8, s.width)), at, 1)[0:1, 0 : s.gain_count]
        leave(tiny[i], out)
    tiny[2][...] = small[2 * rows : 2 * rows + s.heads, 0 : s.buckets]
    leave(tiny[2], table)
    wq, wk, wv, wo, wg, wu, wd = wide
    for unit in range(3):
        loads[2 + unit].wait()
        for w, buf in enumerate((wq, wk, wv)):
            buf[:, 128 * unit : 128 * (unit + 1)] = units[unit][:, 128 * w : 128 * (w + 1)].astype(F32)
    for buf, out in ((wq, gq), (wk, gk), (wv, gv)):
        leave(buf, out)
    loads[2 + OUT].wait()
    wo[...] = units[OUT][...].astype(F32)
    leave(wo, go)
    for which, buf, out in ((0, wg, gg), (1, wu, gu), (2, wd, gd)):
        for part in range(CHUNKS):
            unit = ffn_unit(part, which)
            loads[2 + unit].wait()
            rows, cols = units[unit].shape
            if which == 2:
                buf[part * rows : (part + 1) * rows, :] = units[unit][...].astype(F32)
            else:
                size = buf.shape[1] // 2
                for i in range(2):
                    at = i * size + part * (cols // 2)
                    buf[:, at : at + cols // 2] = units[unit][:, i * (cols // 2) : (i + 1) * (cols // 2)].astype(F32)
        leave(buf, out)
    for i, out in enumerate((y, gi)):
        loads[i].wait()
        leave(bufs[i], out)
    for copy in stores:
        copy.wait()


def finish(arrays, gain_count, heads, buckets, blocks):
    vm, sh = pltpu.VMEM, jax.ShapeDtypeStruct
    far = pl.BlockSpec(memory_space=pl.ANY)
    y, gi = arrays[:2]
    b = [sh(shape, F32) for shape in blocks]
    gain = sh((1, gain_count), F32)
    cfg = dict(width=y.shape[1], gain_count=gain_count, heads=heads, buckets=buckets)
    return pl.pallas_call(
        functools.partial(finish_kernel, cfg),
        out_shape=[sh(y.shape, BF), sh(gi.shape, BF), gain, *b[:4], sh((heads, buckets), F32), gain, *b[4:]],
        in_specs=[far] * len(arrays), out_specs=[far] * 12,
        scratch_shapes=[vm(a.shape, a.dtype) for a in arrays] + [vm(shape, F32) for shape in blocks]
        + [vm(gain.shape, F32)] * 2 + [vm((heads, buckets), F32)]
        + [pltpu.SemaphoreType.DMA((len(arrays),)), pltpu.SemaphoreType.DMA((12,))],
        compiler_params=pltpu.CompilerParams(vmem_limit_bytes=67043328),
    )(*arrays)


def open_block(gathered, row_count, column_count):
    _, rows, columns = gathered.shape
    grid = gathered.reshape(row_count, column_count, rows, columns).transpose(0, 2, 1, 3)
    return grid.reshape(row_count * rows, column_count * columns)


def close_block(full, row_count, column_count):
    rows, columns = full.shape[0] // row_count, full.shape[1] // column_count
    grid = full.reshape(row_count, rows, column_count, columns).transpose(0, 2, 1, 3)
    return grid.reshape(row_count * column_count, rows, columns)


def shards(block_input, segment_ids, bucket, gain_attn, w_query, w_key, w_value, w_out, bias_table, gain_ffn, w_gate, w_up, w_down, cotangent):
    row_count, column_count = lax.axis_size("row"), lax.axis_size("col")
    micro, length, width = block_input.shape
    tokens, gain_count = micro * length, gain_attn.shape[0]
    buckets, heads = bias_table.shape
    pieces = [w_query, w_key, w_value, w_out, w_gate, w_up, w_down]
    full = [(p.shape[0] * row_count, p.shape[1] * column_count) for p in pieces]
    fits = row_count == 4 and column_count == 2 and lax.axis_size("dp") == 4
    x, c = block_input.reshape(tokens, width), cotangent.reshape(tokens, width)
    gains = [gain_attn[None], gain_ffn[None]]
    plane = ("row", "col")
    if fits:
        out = call_layer(True, x, c, pieces, gains, segment_ids, bucket[None], bias_table.T, full)
        y, gi, one, gq, gk, gv, go, table, two, gg, gu, gd = finish(
            out, gain_count, heads, buckets, [p.shape for p in pieces])
        return y.reshape(block_input.shape), gi.reshape(block_input.shape), one[0], gq, gk, gv, go, table.T, two[0], gg, gu, gd
    gains = [lax.all_gather(g, plane, axis=1, tiled=True) for g in gains]
    weights = [open_block(lax.all_gather(p[None], plane, axis=0, tiled=True), row_count, column_count) for p in pieces]
    out = call_layer(False, x, c, weights, gains, segment_ids, bucket[None], bias_table.T, full)
    y, gi, grads, small = out[0], out[1], out[2:9], out[9]
    small = lax.psum(small, ("dp",) + plane)
    grads = [lax.psum_scatter(close_block(g, row_count, column_count), plane, scatter_dimension=0, tiled=True)[0] for g in grads]
    gq, gk, gv, go, gg, gu, gd = (lax.psum(g, "dp").astype(F32) for g in grads)
    mine = (lax.axis_index("row") * column_count + lax.axis_index("col")) * gain_count
    one, two = (lax.dynamic_slice(small[i * (width // 128) : (i + 1) * (width // 128)].reshape(-1), (mine,), (gain_count,)) for i in range(2))
    table = small[2 * (width // 128) :, :buckets].T
    return y.reshape(block_input.shape), gi.reshape(block_input.shape), one, gq, gk, gv, go, table, two, gg, gu, gd


def solution(mesh):
    whole = P(None, ("dp", "row", "col"), None)
    split, gain = P("row", "col"), P(("row", "col"))
    return jax.shard_map(
        shards, mesh=mesh,
        in_specs=(whole, P(None, ("dp", "row", "col")), P(), gain, split, split, split, split, P(), gain, split, split, split, whole),
        out_specs=(whole, whole, gain, split, split, split, split, P(), gain, split, split, split),
        check_vma=False)
```
